32 devices in a mesh: ctx: 8 (over y, x, core), head: 4 (over z).
Axes of the slice: x: 2, y: 2, z: 4, core: 2. Of those that a mesh axis runs over, the one named last changes fastest.
Arguments:
- hidden: bfloat16 [16384, 1024], P(('ctx', 'head')), may hold values from -6 to 6
- cotangent: bfloat16 [16384, 1024], P(('ctx', 'head')), may hold values from -6 to 6
- segment_ids: int32 [16384], replicated, may hold values from 0 to 15, as said below
- adapter_ids: int32 [4], replicated, may hold values from 0 to 7
- attn_gain: float32 [1024], replicated, may hold values from 0.1 to 1.9
- query_gain: float32 [64], replicated, may hold values from 0.1 to 1.9
- key_gain: float32 [64], replicated, may hold values from 0.1 to 1.9
- ffn_gain: float32 [1024], replicated, may hold values from 0.1 to 1.9
- qkv_weight: bfloat16 [1024, 2048], P(('ctx', 'head')), may hold values from -0.1875 to 0.1875
- out_weight: bfloat16 [1024, 1024], P(('ctx', 'head')), may hold values from -1.5 to 1.5
- gate_up_weight: bfloat16 [1024, 9216], P(('ctx', 'head')), may hold values from -0.1875 to 0.1875
- down_weight: bfloat16 [4608, 1024], P(('ctx', 'head')), may hold values from -0.1875 to 0.1875
- qkv_down: bfloat16 [8, 48, 1024], P(None, None, ('ctx', 'head')), may hold values from -0.1875 to 0.1875
- qkv_up: bfloat16 [8, 16, 2048], P(None, None, ('ctx', 'head')), may hold values from -0.4375 to 0.4375
- out_down: bfloat16 [8, 16, 1024], P(None, None, ('ctx', 'head')), may hold values from -1.5 to 1.5
- out_up: bfloat16 [8, 16, 1024], P(None, None, ('ctx', 'head')), may hold values from -0.75 to 0.75
- mlp_down: bfloat16 [8, 32, 1024], P(None, None, ('ctx', 'head')), may hold values from -0.1875 to 0.1875
- mlp_up: bfloat16 [8, 16, 9216], P(None, None, ('ctx', 'head')), may hold values from -0.4375 to 0.4375
- ffd_down: bfloat16 [8, 16, 4608], P(None, None, ('ctx', 'head')), may hold values from -0.09375 to 0.09375
- ffd_up: bfloat16 [8, 16, 1024], P(None, None, ('ctx', 'head')), may hold values from -0.75 to 0.75
Outputs:
- output: bfloat16 [16384, 1024], P(('ctx', 'head'))
- input_grad: float32 [16384, 1024], P(('ctx', 'head'))
- qkv_down_grad: float32 [8, 48, 1024], P(None, None, ('ctx', 'head'))
- qkv_up_grad: float32 [8, 16, 2048], P(None, None, ('ctx', 'head'))
- out_down_grad: float32 [8, 16, 1024], P(None, None, ('ctx', 'head'))
- out_up_grad: float32 [8, 16, 1024], P(None, None, ('ctx', 'head'))
- mlp_down_grad: float32 [8, 32, 1024], P(None, None, ('ctx', 'head'))
- mlp_up_grad: float32 [8, 16, 9216], P(None, None, ('ctx', 'head'))
- ffd_down_grad: float32 [8, 16, 4608], P(None, None, ('ctx', 'head'))
- ffd_up_grad: float32 [8, 16, 1024], P(None, None, ('ctx', 'head'))
The draws below stay inside these ranges and needn't reach their ends.
Inputs may be any that keep to these rules, and one draw needn't show every extreme that they name: `segment_ids`: never falling along the tokens and taking every value from 0 to the most; every document holds at most 2048 tokens and one holds exactly 2048.
All inputs are finite; a program needn't handle non-finite values.
Results may differ from the reference program's by a relative error of at most 0.018.
Values may be sent and summed in bfloat16 or wider, within the bound.
No kernel may reach another device: no remote copies, remote signals or barrier semaphores. Data moves between devices by JAX's collectives and lax.ppermute only.
A program may use at most 256 MiB of HBM per device.

```python
import math
import jax
import jax.numpy as jnp
from jax import lax

D = 1024
HEADS = 16
KV_HEADS = 8
HEAD_DIM = 64
FF = 4608
RANK = 16
ADAPTERS = 8
NSEQ = 4
SEGMAX = 2048
QBLOCK = 512
QW = 1024
KW = 512
TOKENS = 16384
SEQLEN = 4096


def draw_segment_ids(key, part):
    half = SEGMAX // 2
    count = TOKENS // half
    jitter = jax.random.randint(jax.random.fold_in(key, 11), (count,), 1, half // 2)
    merged = jax.random.randint(jax.random.fold_in(key, 12), (), 0, count - 2)
    index = jnp.arange(count, dtype=jnp.int32)
    offsets = jnp.where(index == merged + 2, jitter[merged], jitter)
    starts = index * half + offsets
    valid = (index != merged + 1).astype(jnp.int32)
    marks = jnp.zeros((TOKENS,), jnp.int32).at[starts].add(valid)
    return jnp.cumsum(marks).astype(jnp.int32)


def place_ends(array, rng, low, largest):
    longest = array.shape.index(max(array.shape))
    spots = []
    for shift in (0, 1):
        where = [jax.random.randint(jax.random.fold_in(rng, axis), (), 0, length) for axis, length in enumerate(array.shape)]
        where[longest] = (where[longest] + shift) % array.shape[longest]
        spots.append(tuple(where))
    return array.at[spots[0]].set(low).at[spots[1]].set(largest)


def shard_levels(rng, dims, cuts, least, high):
    gain, own = 1.0, jax.random.fold_in(rng, 6)
    for position, blocks in cuts:
        heights = jnp.exp(jax.random.uniform(jax.random.fold_in(own, position), (blocks,), jnp.float32, least / len(cuts), high / len(cuts)))
        gain = gain * jnp.repeat(heights, dims[position] // blocks).reshape([-1 if axis == position else 1 for axis in range(len(dims))])
    return gain


def centred(rng, dims, spread, limit, split=(), kind=jnp.bfloat16):
    entries = jax.random.normal(rng, dims, jnp.float32) * spread
    if len(split) > 0:
        entries = shard_levels(rng, dims, split, -0.22, 0.18) * entries
    return jnp.clip(entries, min=-limit, max=limit).astype(kind)


def setup_inputs(seed: int = 0) -> dict:
    streams_of = jax.random.split(jax.random.key(seed), 21)
    return {
        "hidden": centred(streams_of[0], (TOKENS, D), 1.0, 6.0, ((0, 32),)),
        "cotangent": centred(streams_of[1], (TOKENS, D), 1.0, 6.0, ((0, 32),)),
        "segment_ids": draw_segment_ids(jax.random.fold_in(streams_of[20], 71), 0),
        "adapter_ids": place_ends(jax.random.randint(streams_of[3], (NSEQ,), 0, ADAPTERS), jax.random.fold_in(streams_of[3], 1), 0, ADAPTERS - 1).astype(jnp.int32),
        "attn_gain": jnp.clip(1.0 + 0.18 * jax.random.normal(streams_of[4], (D,), jnp.float32), 0.1, 1.9),
        "query_gain": jnp.clip(1.0 + 0.18 * jax.random.normal(streams_of[5], (HEAD_DIM,), jnp.float32), 0.1, 1.9),
        "key_gain": jnp.clip(1.0 + 0.18 * jax.random.normal(streams_of[6], (HEAD_DIM,), jnp.float32), 0.1, 1.9),
        "ffn_gain": jnp.clip(1.0 + 0.18 * jax.random.normal(streams_of[7], (D,), jnp.float32), 0.1, 1.9),
        "qkv_weight": centred(streams_of[8], (D, QW + 2 * KW), D ** -0.5, 0.1875, ((0, 32),)),
        "out_weight": centred(streams_of[9], (QW, D), (QW // 64) ** -0.5, 1.5, ((0, 32),)),
        "gate_up_weight": centred(streams_of[10], (D, 2 * FF), D ** -0.5, 0.1875, ((0, 32),)),
        "down_weight": centred(streams_of[11], (FF, D), (FF // 4) ** -0.5, 0.1875, ((0, 32),)),
        "qkv_down": centred(streams_of[12], (ADAPTERS, 3 * RANK, D), D ** -0.5, 0.1875, ((2, 32),)),
        "qkv_up": centred(streams_of[13], (ADAPTERS, RANK, QW + 2 * KW), (RANK * 12) ** -0.5, 0.4375, ((2, 32),)),
        "out_down": centred(streams_of[14], (ADAPTERS, RANK, QW), (QW // 64) ** -0.5, 1.5, ((2, 32),)),
        "out_up": centred(streams_of[15], (ADAPTERS, RANK, D), (RANK * 4) ** -0.5, 0.75, ((2, 32),)),
        "mlp_down": centred(streams_of[16], (ADAPTERS, 2 * RANK, D), D ** -0.5, 0.1875, ((2, 32),)),
        "mlp_up": centred(streams_of[17], (ADAPTERS, RANK, 2 * FF), (RANK * 12) ** -0.5, 0.4375, ((2, 32),)),
        "ffd_down": centred(streams_of[18], (ADAPTERS, RANK, FF), FF ** -0.5, 0.09375, ((2, 32),)),
        "ffd_up": centred(streams_of[19], (ADAPTERS, RANK, D), (RANK * 4) ** -0.5, 0.75, ((2, 32),)),
    }


precise = lax.Precision.HIGHEST
epsilon = 1e-05
rope_base = 1000000.0

@jax.custom_vjp
def low(v):
    return lax.optimization_barrier(v.astype(jnp.bfloat16)).astype(jnp.float32)

@jax.custom_vjp
def low_back(v):
    return v

def low_keep(v):
    return (low(v), None)

def low_pass(kept, grad):
    return (grad,)

def back_keep(v):
    return (v, None)

def back_low(kept, grad):
    return (low(grad),)
low.defvjp(low_keep, low_pass)
low_back.defvjp(back_keep, back_low)

def product(left_side, right_side):
    return jnp.dot(left_side, right_side, precision=precise, preferred_element_type=jnp.float32)

def rms_norm(values, gain_row):
    return values * lax.rsqrt(lax.optimization_barrier(jnp.mean(values * values, axis=-1, keepdims=True)) + epsilon) * gain_row

def rope_tables(positions):
    middle = HEAD_DIM // 2
    frequency = jnp.power(rope_base, -(2.0 / HEAD_DIM) * jnp.arange(middle, dtype=jnp.float32))
    angles = positions.astype(jnp.float32)[:, None] * frequency[None, :]
    return (jnp.cos(angles)[:, None, :], jnp.sin(angles)[:, None, :])

def rotate(values, cosine, sine_part):
    middle = values.shape[-1] // 2
    leading = values[..., :middle]
    trailing = values[..., middle:]
    return jnp.concatenate([leading * cosine - trailing * sine_part, trailing * cosine + leading * sine_part], axis=-1)

def prepare_heads(projected, positions, query_gain, key_gain):
    length = projected.shape[0]
    cosine, sine_part = rope_tables(positions)
    query_rows = projected[:, :QW].reshape(length, HEADS, HEAD_DIM)
    key_rows = projected[:, QW:QW + KW].reshape(length, KV_HEADS, HEAD_DIM)
    value_rows = projected[:, QW + KW:].reshape(length, KV_HEADS, HEAD_DIM)
    query_rows = rotate(rms_norm(query_rows, query_gain), cosine, sine_part)
    key_rows = rotate(rms_norm(key_rows, key_gain), cosine, sine_part)
    grouped = query_rows.reshape(length, KV_HEADS, HEADS // KV_HEADS * HEAD_DIM)
    return (grouped, jnp.concatenate([key_rows, value_rows], axis=-1))

def lowrank(inputs, down_rows, up_rows, bounds):
    reduced = low_back(low(product(inputs, down_rows.T)))
    pieces = [product(reduced[:, RANK * member:RANK * (member + 1)], up_rows[:, bounds[member]:bounds[member + 1]]) for member in range(len(bounds) - 1)]
    return jnp.concatenate(pieces, axis=1)

def attend_sequence(grouped, keyvals, segments):
    length = grouped.shape[0]
    padded_kv = jnp.concatenate([jnp.zeros((SEGMAX,) + keyvals.shape[1:], jnp.float32), keyvals], axis=0)
    padded_seg = jnp.concatenate([jnp.full((SEGMAX,), -1, jnp.int32), segments.astype(jnp.int32)])
    window_rows = SEGMAX + QBLOCK
    score_scale = HEAD_DIM ** (-0.5)

    def one_block(offset):
        query_block = lax.dynamic_slice_in_dim(grouped, offset, QBLOCK, 0).reshape(QBLOCK, KV_HEADS, HEADS // KV_HEADS, HEAD_DIM)
        window = lax.dynamic_slice_in_dim(padded_kv, offset, window_rows, 0)
        key_rows = window[..., :HEAD_DIM]
        value_rows = window[..., HEAD_DIM:]
        seg_keys = lax.dynamic_slice_in_dim(padded_seg, offset, window_rows, 0)
        seg_query = lax.dynamic_slice_in_dim(padded_seg, offset + SEGMAX, QBLOCK, 0)
        query_pos = offset + jnp.arange(QBLOCK, dtype=jnp.int32)
        key_pos = offset - SEGMAX + jnp.arange(window_rows, dtype=jnp.int32)
        allowed = (key_pos[None, :] <= query_pos[:, None]) & (seg_keys[None, :] == seg_query[:, None])
        scores = low_back(jnp.einsum('qcgd,scd->cgqs', query_block, key_rows, precision=precise) * score_scale)
        scores = jnp.where(allowed[None, None], scores, -1e+30)
        attention = low(jax.nn.softmax(scores, axis=-1))
        mixture = jnp.einsum('cgqs,scd->qcgd', attention, value_rows, precision=precise)
        return mixture.reshape(QBLOCK, KV_HEADS, HEADS // KV_HEADS * HEAD_DIM)
    starts = jnp.arange(length // QBLOCK, dtype=jnp.int32) * QBLOCK
    blocks = lax.map(jax.checkpoint(one_block), starts)
    return blocks.reshape(length, KV_HEADS, HEADS // KV_HEADS * HEAD_DIM)

def block_forward(hidden_rows, segments, adapter_pick, gains, frozen, *adapters):
    attn_gain, query_gain, key_gain, ffn_gain = gains
    qkv_full, out_full, gate_up_full, down_full = frozen
    chosen = [lax.dynamic_index_in_dim(member, adapter_pick, 0, keepdims=False) for member in adapters]
    positions = jnp.arange(SEQLEN, dtype=jnp.int32)
    normed = low(rms_norm(hidden_rows, attn_gain))
    projected = low_back(product(normed, qkv_full) + lowrank(normed, chosen[0], chosen[1], (0, QW, QW + KW, QW + 2 * KW)))
    grouped, keyvals = prepare_heads(projected, positions, query_gain, key_gain)
    grouped = low_back(low(grouped))
    keyvals = low_back(low(keyvals))
    mixture = low_back(low(attend_sequence(grouped, keyvals, segments))).reshape(SEQLEN, QW)
    branch = low_back(product(mixture, out_full) + lowrank(mixture, chosen[2], chosen[3], (0, D)))
    middle = hidden_rows + branch

    def feed_rows(row_block):
        normed_two = low(rms_norm(row_block, ffn_gain))
        gate_up = low_back(product(normed_two, gate_up_full) + lowrank(normed_two, chosen[4], chosen[5], (0, FF, 2 * FF)))
        hidden_units = low(jax.nn.silu(gate_up[:, :FF]) * gate_up[:, FF:])
        branch_two = low_back(product(hidden_units, down_full) + lowrank(hidden_units, chosen[6], chosen[7], (0, D)))
        return row_block + branch_two
    piece_rows = math.gcd(SEQLEN, 4096)
    result = lax.map(jax.checkpoint(feed_rows), middle.reshape(SEQLEN // piece_rows, piece_rows, D))
    return result.reshape(SEQLEN, D)

def reference(hidden, cotangent, segment_ids, adapter_ids, attn_gain, query_gain, key_gain, ffn_gain, qkv_weight, out_weight, gate_up_weight, down_weight, qkv_down, qkv_up, out_down, out_up, mlp_down, mlp_up, ffd_down, ffd_up):
    gains = (attn_gain.astype(jnp.float32), query_gain.astype(jnp.float32), key_gain.astype(jnp.float32), ffn_gain.astype(jnp.float32))
    frozen = tuple((member.astype(jnp.float32) for member in (qkv_weight, out_weight, gate_up_weight, down_weight)))
    adapters = tuple((member.astype(jnp.float32) for member in (qkv_down, qkv_up, out_down, out_up, mlp_down, mlp_up, ffd_down, ffd_up)))
    hidden_seq = hidden.astype(jnp.float32).reshape(NSEQ, SEQLEN, D)
    cot_seq = cotangent.astype(jnp.float32).reshape(NSEQ, SEQLEN, D)
    seg_seq = segment_ids.astype(jnp.int32).reshape(NSEQ, SEQLEN)

    def one_sequence(totals, scanned):
        row_block, cot_rows, segments, adapter_pick = scanned

        def forward(operand, *adapt):
            return block_forward(operand, segments, adapter_pick, gains, frozen, *adapt)
        result, pullback = jax.vjp(forward, row_block, *adapters)
        gradients = pullback(cot_rows)
        totals = tuple((before + after for before, after in zip(totals, gradients[1:])))
        return (totals, (result.astype(jnp.bfloat16), gradients[0]))
    starting = tuple((jnp.zeros(member.shape, jnp.float32) for member in adapters))
    totals, (outputs, input_grads) = lax.scan(one_sequence, starting, (hidden_seq, cot_seq, seg_seq, adapter_ids.astype(jnp.int32)))
    return (outputs.reshape(TOKENS, D), input_grads.reshape(TOKENS, D), totals[0], totals[1], totals[2], totals[3], totals[4], totals[5], totals[6], totals[7])
```

```python
import functools
import math

import jax
import jax.numpy as jnp
from jax import lax
from jax.experimental import pallas as pl
from jax.experimental.pallas import tpu as pltpu
from jax.sharding import PartitionSpec as P

D = 1024
HEADS = 16
KV_HEADS = 8
HEAD_DIM = 64
FF = 4608
RANK = 16
ADAPTERS = 8
NSEQ = 4
SEGMAX = 2048
QW = 1024
KW = 512
PAIR = 2 * HEAD_DIM
BLOCK = 256
AXES = ("ctx", "head")

epsilon = 1e-05
rope_base = 1000000.0
LOG2E = math.log2(math.e)
QSCALE = HEAD_DIM**-0.5 * LOG2E
F32 = jnp.float32
BF16 = jnp.bfloat16


def matmul(left_side, right_side):
    return jnp.dot(left_side, right_side, preferred_element_type=F32)


def contract_rows(left_side, right_side):
    return lax.dot_general(left_side, right_side, (((0,), (0,)), ((), ())), preferred_element_type=F32)


def contract_cols(left_side, right_side):
    return lax.dot_general(left_side, right_side, (((1,), (1,)), ((), ())), preferred_element_type=F32)


def rms_norm(values, gain_row):
    return values * lax.rsqrt(jnp.mean(values * values, axis=-1, keepdims=True) + epsilon) * gain_row


def rope_tables(positions):
    middle = HEAD_DIM // 2
    frequency = jnp.power(rope_base, -(2.0 / HEAD_DIM) * jnp.arange(middle, dtype=F32))
    angles = positions.astype(F32)[:, None] * frequency[None, :]
    return (jnp.cos(angles)[:, None, :], jnp.sin(angles)[:, None, :])


def rotate(values, cosine, sine_part):
    middle = values.shape[-1] // 2
    leading = values[..., :middle]
    trailing = values[..., middle:]
    return jnp.concatenate(
        [leading * cosine - trailing * sine_part, trailing * cosine + leading * sine_part], axis=-1
    )


def prepare_heads(projected, positions, query_gain, key_gain):
    length = projected.shape[0]
    cosine, sine_part = rope_tables(positions)
    query_rows = projected[:, :QW].reshape(length, HEADS, HEAD_DIM)
    key_rows = projected[:, QW : QW + KW].reshape(length, KV_HEADS, HEAD_DIM)
    value_rows = projected[:, QW + KW :].reshape(length, KV_HEADS, HEAD_DIM)
    query_rows = rotate(rms_norm(query_rows, query_gain), cosine, sine_part)
    key_rows = rotate(rms_norm(key_rows, key_gain), cosine, sine_part)
    grouped = query_rows.reshape(length, KV_HEADS, PAIR)
    return (grouped, jnp.concatenate([key_rows, value_rows], axis=-1))


def rank_apply(reduced, up_rows, bounds):
    return jnp.concatenate(
        [
            matmul(
                reduced[:, RANK * member : RANK * (member + 1)],
                up_rows[:, bounds[member] : bounds[member + 1]],
            )
            for member in range(len(bounds) - 1)
        ],
        axis=1,
    )


def rank_back(grad_low, reduced, up_rows, bounds):
    up_grad = jnp.concatenate(
        [
            contract_rows(
                reduced[:, RANK * member : RANK * (member + 1)],
                grad_low[:, bounds[member] : bounds[member + 1]],
            )
            for member in range(len(bounds) - 1)
        ],
        axis=1,
    )
    reduced_grad = jnp.concatenate(
        [
            contract_cols(
                grad_low[:, bounds[member] : bounds[member + 1]],
                up_rows[:, bounds[member] : bounds[member + 1]],
            )
            for member in range(len(bounds) - 1)
        ],
        axis=1,
    )
    return (up_grad, reduced_grad)


VMEM_SPEC = pl.BlockSpec(memory_space=pltpu.VMEM)
SMEM_SPEC = pl.BlockSpec(memory_space=pltpu.SMEM)


def lane_pad(width):
    return -(-width // 128) * 128


def layout_of(shapes):
    places = []
    offset = 0
    for index, (rows, width) in enumerate(shapes):
        for part in range(rows // RANK):
            places.append((index, part, offset, width))
            offset += width
    return places, lane_pad(offset)


def pack_adapters(adapter_ids, members, devices):
    places, width = layout_of([member.shape[1:] for member in members])
    per_seq = devices // NSEQ

    def kernel(ids, *refs):
        sources, out, slab = refs[: len(members)], refs[len(members)], refs[len(members) + 1]
        slab[...] = jnp.zeros_like(slab)
        for index, part, offset, size in places:
            slab[:, offset : offset + size] = sources[index][
                ids[pl.program_id(0)], RANK * part : RANK * (part + 1), :
            ]
        for step in range(per_seq):
            out[step] = slab[...]

    return pl.pallas_call(
        kernel,
        grid=(NSEQ,),
        in_specs=[SMEM_SPEC] + [pl.BlockSpec(member.shape, lambda s: (0, 0, 0)) for member in members],
        out_specs=pl.BlockSpec((per_seq, RANK, width), lambda s: (s, 0, 0)),
        out_shape=jax.ShapeDtypeStruct((devices, RANK, width), BF16),
        scratch_shapes=[pltpu.VMEM((RANK, width), BF16)],
        name="pack_adapters",
    )(adapter_ids, *members)


def unpack_adapters(slabs, shapes):
    devices = slabs.shape[0]
    places, _ = layout_of(shapes)

    def kernel(source, *outs):
        for index, part, offset, size in places:
            for device in range(devices):
                outs[index][RANK * part : RANK * (part + 1), device * size : (device + 1) * size] = source[
                    device, :, offset : offset + size
                ]

    return pl.pallas_call(
        kernel,
        in_specs=[VMEM_SPEC],
        out_specs=[VMEM_SPEC] * len(shapes),
        out_shape=[jax.ShapeDtypeStruct((rows, width * devices), BF16) for rows, width in shapes],
        name="unpack_adapters",
    )(slabs)


def pack_grads(grads, devices):
    places, width = layout_of([(grad.shape[0], grad.shape[1] // devices) for grad in grads])

    def kernel(*refs):
        sources, out = refs[: len(grads)], refs[len(grads)]
        for device in range(devices):
            for index, part, offset, size in places:
                out[device, :, offset : offset + size] = sources[index][
                    RANK * part : RANK * (part + 1), device * size : (device + 1) * size
                ].astype(BF16)

    return pl.pallas_call(
        kernel,
        in_specs=[VMEM_SPEC] * len(grads),
        out_specs=VMEM_SPEC,
        out_shape=jax.ShapeDtypeStruct((devices, RANK, width), BF16),
        name="pack_grads",
    )(*grads)


def reduce_grads(adapter_ids, slabs, shapes):
    devices, _, width = slabs.shape
    places, _ = layout_of(shapes)
    per_seq = devices // NSEQ

    def kernel(ids, source, *refs):
        outs, total = refs[: len(shapes)], refs[len(shapes)]
        total[...] = jnp.zeros_like(total)
        for seq in range(NSEQ):
            part_sum = jnp.sum(source[seq * per_seq : (seq + 1) * per_seq].astype(F32), axis=0)
            total[ids[seq]] += part_sum
        for index, part, offset, size in places:
            outs[index][:, RANK * part : RANK * (part + 1), :] = total[:, :, offset : offset + size]

    return pl.pallas_call(
        kernel,
        in_specs=[SMEM_SPEC, VMEM_SPEC],
        out_specs=[VMEM_SPEC] * len(shapes),
        out_shape=[jax.ShapeDtypeStruct((ADAPTERS, rows, size), F32) for rows, size in shapes],
        scratch_shapes=[pltpu.VMEM((ADAPTERS, RANK, width), F32)],
        name="reduce_grads",
    )(adapter_ids, slabs)


def split_three(value):
    first = value.astype(BF16)
    rest = value - first.astype(F32)
    second = rest.astype(BF16)
    third = (rest - second.astype(F32)).astype(BF16)
    return first, second, third


def with_columns(block, columns, lanes):
    out = jnp.where(lanes < HEAD_DIM, block, jnp.zeros_like(block))
    for step, column in enumerate(columns):
        out = jnp.where(lanes == HEAD_DIM + step, column, out)
    return out


def stacked_heads(pair, lanes):
    return jnp.concatenate([pair, pltpu.roll(pair, HEAD_DIM, 1)], axis=0)


def allowed(start_row, key_base, query_base, diagonal):
    keys = key_base + lax.broadcasted_iota(jnp.int32, (BLOCK, BLOCK), 0)
    inside = keys >= start_row
    if diagonal:
        queries = query_base + lax.broadcasted_iota(jnp.int32, (BLOCK, BLOCK), 1)
        inside = inside & (keys <= queries)
    return jnp.concatenate([inside, inside], axis=1)


def forward_attention(bounds, starts, queries, keyvals):
    rows = queries.shape[0]
    length = keyvals.shape[0]
    halo = length - rows
    steps = rows // BLOCK

    def kernel(bound_ref, start_ref, query_ref, keyval_ref, out_ref, log_ref, key_scr, value_scr):
        step = pl.program_id(0)

        @pl.when(step == 0)
        def _():
            lanes = lax.broadcasted_iota(jnp.int32, (length, 128), 1)
            both = keyval_ref[...].astype(F32)
            key_scr[...] = jnp.where(lanes < HEAD_DIM, both, 0.0).astype(BF16)
            values = jnp.where(lanes < HEAD_DIM, pltpu.roll(both, HEAD_DIM, 1), 1.0)
            value_scr[...] = values.T.astype(BF16)

        lanes = lax.broadcasted_iota(jnp.int32, (BLOCK, 128), 1)
        pair = query_ref[...].astype(F32)
        query = stacked_heads(pair, lanes).astype(BF16)
        start_row = start_ref[...]
        diagonal = halo // BLOCK + step
        first = bound_ref[0, step]
        clear = jnp.minimum(bound_ref[1, step], diagonal)

        def block(index, total, masked, is_diagonal):
            base = pl.multiple_of(index * BLOCK, BLOCK)
            scores = contract_cols(key_scr[pl.ds(base, BLOCK), :], query)
            weights = jnp.exp2(scores)
            if masked:
                keep = allowed(start_row, base, diagonal * BLOCK, is_diagonal)
                weights = jnp.where(keep, weights, 0.0)
            return total + matmul(value_scr[:, pl.ds(base, BLOCK)], weights.astype(BF16))

        total = jnp.zeros((128, 2 * BLOCK), F32)
        total = lax.fori_loop(first, clear, lambda i, t: block(i, t, True, False), total)
        total = lax.fori_loop(clear, diagonal, lambda i, t: block(i, t, False, False), total)
        total = block(diagonal, total, True, True)
        norm = total[HEAD_DIM : HEAD_DIM + 1, :]
        mixed = total[:HEAD_DIM, :] / norm
        out_ref[...] = jnp.concatenate([mixed[:, :BLOCK], mixed[:, BLOCK:]], axis=0).T.astype(BF16)
        log_ref[0] = jnp.broadcast_to(jnp.log2(norm), (8, 2 * BLOCK))

    return pl.pallas_call(
        kernel,
        grid_spec=pltpu.PrefetchScalarGridSpec(
            num_scalar_prefetch=1,
            grid=(steps,),
            in_specs=[
                pl.BlockSpec((1, BLOCK), lambda i, b: (0, i)),
                pl.BlockSpec((BLOCK, 128), lambda i, b: (i, 0)),
                pl.BlockSpec((length, 128), lambda i, b: (0, 0)),
            ],
            out_specs=[
                pl.BlockSpec((BLOCK, 128), lambda i, b: (i, 0)),
                pl.BlockSpec((1, 8, 2 * BLOCK), lambda i, b: (i, 0, 0)),
            ],
            scratch_shapes=[pltpu.VMEM((length, 128), BF16), pltpu.VMEM((128, length), BF16)],
        ),
        out_shape=[
            jax.ShapeDtypeStruct((rows, 128), BF16),
            jax.ShapeDtypeStruct((steps, 8, 2 * BLOCK), F32),
        ],
        compiler_params=pltpu.CompilerParams(vmem_limit_bytes=40 << 20),
        cost_estimate=pl.CostEstimate(
            flops=4 * rows * 1024 * 256 * 2, bytes_accessed=4 * rows * 256, transcendentals=rows * 2048
        ),
        name="forward_attention",
    )(bounds, starts, queries, keyvals)


def backward_attention(bounds, starts, queries, keyvals, mixed, logs, grads):
    rows = queries.shape[0]
    length = keyvals.shape[0]
    halo = length - rows
    steps = rows // BLOCK

    def kernel(
        bound_ref, start_ref, query_ref, keyval_ref, mixed_ref, log_ref, grad_ref,
        query_out, keyval_out, key_scr, value_scr, turned_scr, key_sum, value_sum,
    ):
        step = pl.program_id(0)

        @pl.when(step == 0)
        def _():
            lanes = lax.broadcasted_iota(jnp.int32, (length, 128), 1)
            both = keyval_ref[...].astype(F32)
            ones = jnp.where(lanes < HEAD_DIM + 3, 1.0, 0.0)
            keys = jnp.where(lanes < HEAD_DIM, both, ones)
            key_scr[...] = keys.astype(BF16)
            value_scr[...] = jnp.where(lanes < HEAD_DIM, pltpu.roll(both, HEAD_DIM, 1), ones).astype(BF16)
            turned_scr[...] = keys.T.astype(BF16)
            key_sum[...] = jnp.zeros_like(key_sum)
            value_sum[...] = jnp.zeros_like(value_sum)

        lanes = lax.broadcasted_iota(jnp.int32, (2 * BLOCK, 128), 1)
        query = stacked_heads(query_ref[...].astype(F32), lanes)
        grad = stacked_heads(grad_ref[...].astype(F32), lanes)
        weighed = stacked_heads(mixed_ref[...].astype(F32), lanes)
        inner = jnp.sum(jnp.where(lanes < HEAD_DIM, grad * weighed, 0.0), axis=1, keepdims=True)
        log_column = log_ref[0].T[:, :1]
        query_low = with_columns(query, [part.astype(F32) for part in split_three(-log_column)], lanes).astype(BF16)
        grad_low = with_columns(grad, [part.astype(F32) for part in split_three(-inner)], lanes).astype(BF16)
        start_row = start_ref[...]
        diagonal = halo // BLOCK + step
        first = bound_ref[0, step]
        clear = jnp.minimum(bound_ref[1, step], diagonal)

        def block(index, total, masked, is_diagonal):
            base = pl.multiple_of(index * BLOCK, BLOCK)
            where = pl.ds(base, BLOCK)
            weights = jnp.exp2(contract_cols(key_scr[where, :], query_low))
            if masked:
                keep = allowed(start_row, base, diagonal * BLOCK, is_diagonal)
                weights = jnp.where(keep, weights, 0.0)
            slopes = (weights * contract_cols(value_scr[where, :], grad_low)).astype(BF16)
            value_sum[where, :] += matmul(weights.astype(BF16), grad_low)
            key_sum[where, :] += matmul(slopes, query_low)
            return total + matmul(turned_scr[:, where], slopes)

        total = jnp.zeros((128, 2 * BLOCK), F32)
        total = lax.fori_loop(first, clear, lambda i, t: block(i, t, True, False), total)
        total = lax.fori_loop(clear, diagonal, lambda i, t: block(i, t, False, False), total)
        total = block(diagonal, total, True, True)
        total = total[:HEAD_DIM] * HEAD_DIM**-0.5
        query_out[...] = jnp.concatenate([total[:, :BLOCK], total[:, BLOCK:]], axis=0).T.astype(BF16)

        @pl.when(step == steps - 1)
        def _():
            whole = lax.broadcasted_iota(jnp.int32, (length, 128), 1)
            keyval_out[...] = jnp.where(
                whole < HEAD_DIM, key_sum[...] * (1.0 / LOG2E), pltpu.roll(value_sum[...], HEAD_DIM, 1)
            ).astype(keyval_out.dtype)

    return pl.pallas_call(
        kernel,
        grid_spec=pltpu.PrefetchScalarGridSpec(
            num_scalar_prefetch=1,
            grid=(steps,),
            in_specs=[
                pl.BlockSpec((1, BLOCK), lambda i, b: (0, i)),
                pl.BlockSpec((BLOCK, 128), lambda i, b: (i, 0)),
                pl.BlockSpec((length, 128), lambda i, b: (0, 0)),
                pl.BlockSpec((BLOCK, 128), lambda i, b: (i, 0)),
                pl.BlockSpec((1, 8, 2 * BLOCK), lambda i, b: (i, 0, 0)),
                pl.BlockSpec((BLOCK, 128), lambda i, b: (i, 0)),
            ],
            out_specs=[
                pl.BlockSpec((BLOCK, 128), lambda i, b: (i, 0)),
                pl.BlockSpec((length, 128), lambda i, b: (0, 0)),
            ],
            scratch_shapes=[
                pltpu.VMEM((length, 128), BF16),
                pltpu.VMEM((length, 128), BF16),
                pltpu.VMEM((128, length), BF16),
                pltpu.VMEM((length, 128), F32),
                pltpu.VMEM((length, 128), F32),
            ],
        ),
        out_shape=[
            jax.ShapeDtypeStruct((rows, 128), BF16),
            jax.ShapeDtypeStruct((length, 128), F32 if halo else BF16),
        ],
        compiler_params=pltpu.CompilerParams(vmem_limit_bytes=48 << 20),
        cost_estimate=pl.CostEstimate(
            flops=10 * rows * 1024 * 256 * 2, bytes_accessed=8 * rows * 256, transcendentals=rows * 2048
        ),
        name="backward_attention",
    )(bounds, starts, queries, keyvals, mixed, logs, grads)


def document_bounds(segment_ids, origin, halo, span, seq_start):
    tokens = segment_ids.shape[0]
    names = jnp.arange(tokens // (SEGMAX // 2), dtype=jnp.int32)
    begin = jnp.sum((segment_ids[None, :] < names[:, None]).astype(jnp.int32), axis=1)
    own = lax.dynamic_slice_in_dim(segment_ids, origin, span, 0)
    start = jnp.sum(jnp.where(own[None, :] == names[:, None], begin[:, None], 0), axis=0)
    start = jnp.maximum(start, seq_start) - (origin - halo)
    first = start[::BLOCK] // BLOCK
    clear = -(-start[BLOCK - 1 :: BLOCK] // BLOCK)
    bounds = jnp.stack([first, jnp.maximum(clear, first)])
    return bounds, start[None, :]


def local(
    hidden, cotangent, segment_ids, adapter_ids, attn_gain, query_gain, key_gain, ffn_gain,
    qkv_weight, out_weight, gate_up_weight, down_weight, *adapters,
):
    rows = hidden.shape[0]
    devices = lax.axis_size("ctx") * lax.axis_size("head")
    members = KV_HEADS
    groups = [[members * g + i for i in range(members)] for g in range(devices // members)]
    span = rows * members
    seq_length = rows * devices // NSEQ
    halo = 0 if span == seq_length else SEGMAX
    here = lax.axis_index("ctx") * lax.axis_size("head") + lax.axis_index("head")
    origin = here // members * span
    seq_start = origin // seq_length * seq_length
    positions = here * rows - seq_start + jnp.arange(rows, dtype=jnp.int32)
    bounds, starts = document_bounds(segment_ids, origin, halo, span, seq_start)

    def swap(value):
        return lax.all_to_all(value, AXES, 0, 0, axis_index_groups=groups, tiled=True)

    def shifted(value, by):
        pairs = [(i, i + by) for i in range(devices) if 0 <= i + by < devices]
        return lax.ppermute(value, AXES, pairs)

    def gather(value):
        return lax.all_gather(value, AXES, axis=0, tiled=True)

    shapes = [member.shape[1:] for member in adapters]
    slabs = lax.all_to_all(pack_adapters(adapter_ids, adapters, devices), AXES, 0, 0, tiled=True)
    chosen = unpack_adapters(slabs, shapes)

    qkv_full = gather(qkv_weight)
    out_full = gather(out_weight)
    gate_up_full = gather(gate_up_weight)
    down_full = gather(down_weight)

    qkv_bounds = (0, QW, QW + KW, QW + 2 * KW)
    inputs = hidden.astype(F32)
    normed, norm_pull = jax.vjp(lambda operand: rms_norm(operand, attn_gain), inputs)
    normed_low = normed.astype(BF16)
    reduced_qkv = contract_cols(normed_low, chosen[0]).astype(BF16)
    projected = matmul(normed_low, qkv_full) + rank_apply(reduced_qkv, chosen[1], qkv_bounds)
    (grouped, keyvals), head_pull = jax.vjp(
        lambda operand: prepare_heads(operand, positions, query_gain, key_gain), projected
    )
    sent = jnp.concatenate([grouped * QSCALE, keyvals], axis=-1).astype(BF16).transpose(1, 0, 2)
    arrived = swap(sent).reshape(span, 2 * PAIR)
    queries = arrived[:, :PAIR]
    keyval_rows = arrived[:, PAIR:]
    if halo:
        keyval_rows = jnp.concatenate([shifted(keyval_rows[span - halo :], members), keyval_rows], axis=0)
    mixed, logs = forward_attention(bounds, starts, queries, keyval_rows)
    mixture_tok = swap(mixed.reshape(members, rows, PAIR)).transpose(1, 0, 2).reshape(rows, QW)

    reduced_out = contract_cols(mixture_tok, chosen[2]).astype(BF16)
    branch = matmul(mixture_tok, out_full) + rank_apply(reduced_out, chosen[3], (0, D))
    middle = inputs + branch
    normed_two, norm_two_pull = jax.vjp(lambda operand: rms_norm(operand, ffn_gain), middle)
    normed_two_low = normed_two.astype(BF16)
    reduced_mlp = contract_cols(normed_two_low, chosen[4]).astype(BF16)
    gate_up = matmul(normed_two_low, gate_up_full) + rank_apply(reduced_mlp, chosen[5], (0, FF, 2 * FF))
    hidden_units, unit_pull = jax.vjp(
        lambda operand: jax.nn.silu(operand[:, :FF]) * operand[:, FF:], gate_up
    )
    units_low = hidden_units.astype(BF16)
    reduced_down = contract_cols(units_low, chosen[6]).astype(BF16)
    branch_two = matmul(units_low, down_full) + rank_apply(reduced_down, chosen[7], (0, D))
    output = (middle + branch_two).astype(BF16)

    ffd_up_grad, reduced_down_grad = rank_back(cotangent, reduced_down, chosen[7], (0, D))
    reduced_down_low = reduced_down_grad.astype(BF16)
    ffd_down_grad = contract_rows(reduced_down_low, units_low)
    units_grad = contract_cols(cotangent, down_full) + matmul(reduced_down_low, chosen[6])
    gate_up_grad = unit_pull(units_grad)[0].astype(BF16)
    mlp_up_grad, reduced_mlp_grad = rank_back(gate_up_grad, reduced_mlp, chosen[5], (0, FF, 2 * FF))
    reduced_mlp_low = reduced_mlp_grad.astype(BF16)
    mlp_down_grad = contract_rows(reduced_mlp_low, normed_two_low)
    normed_two_grad = contract_cols(gate_up_grad, gate_up_full) + matmul(reduced_mlp_low, chosen[4])
    middle_grad = cotangent.astype(F32) + norm_two_pull(normed_two_grad)[0]
    branch_grad = middle_grad.astype(BF16)
    out_up_grad, reduced_out_grad = rank_back(branch_grad, reduced_out, chosen[3], (0, D))
    reduced_out_low = reduced_out_grad.astype(BF16)
    out_down_grad = contract_rows(reduced_out_low, mixture_tok)
    mixture_grad = (contract_cols(branch_grad, out_full) + matmul(reduced_out_low, chosen[2])).astype(BF16)
    grad_rows = swap(mixture_grad.reshape(rows, members, PAIR).transpose(1, 0, 2)).reshape(span, PAIR)

    early = [out_down_grad, out_up_grad, mlp_down_grad, mlp_up_grad, ffd_down_grad, ffd_up_grad]
    early_slabs = lax.all_to_all(pack_grads(early, devices), AXES, 0, 0, tiled=True)
    early_owned = reduce_grads(adapter_ids, early_slabs, shapes[2:])

    query_grads, keyval_grads = backward_attention(
        bounds, starts, queries, keyval_rows, mixed, logs, grad_rows
    )
    if halo:
        returned = shifted(keyval_grads[:halo].astype(BF16), -members).astype(F32)
        keyval_grads = jnp.concatenate(
            [keyval_grads[halo : halo + span - halo], keyval_grads[span:] + returned], axis=0
        ).astype(BF16)
    back = jnp.concatenate([query_grads, keyval_grads], axis=1).reshape(members, rows, 2 * PAIR)
    back = swap(back).transpose(1, 0, 2).astype(F32)
    projected_grad = head_pull((back[..., :PAIR], back[..., PAIR:]))[0].astype(BF16)
    qkv_up_grad, reduced_qkv_grad = rank_back(projected_grad, reduced_qkv, chosen[1], qkv_bounds)
    reduced_qkv_low = reduced_qkv_grad.astype(BF16)
    qkv_down_grad = contract_rows(reduced_qkv_low, normed_low)
    late_slabs = lax.all_to_all(pack_grads([qkv_down_grad, qkv_up_grad], devices), AXES, 0, 0, tiled=True)
    late_owned = reduce_grads(adapter_ids, late_slabs, shapes[:2])
    normed_grad = contract_cols(projected_grad, qkv_full) + matmul(reduced_qkv_low, chosen[0])
    input_grad = middle_grad + norm_pull(normed_grad)[0]
    return (output, input_grad, *late_owned, *early_owned)


def solution(mesh):
    by_rows = P(AXES, None)
    by_cols = P(None, None, AXES)
    placed = (by_rows, by_rows) + (P(),) * 6 + (by_rows,) * 4 + (by_cols,) * 8
    return jax.shard_map(
        local,
        mesh=mesh,
        in_specs=placed,
        out_specs=(by_rows, by_rows) + (by_cols,) * 8,
        check_vma=False,
    )
```

```python
import functools
import math

import jax
import jax.numpy as jnp
from jax import lax
from jax.experimental import pallas as pl
from jax.experimental.pallas import tpu as pltpu
from jax.sharding import PartitionSpec as P

D = 1024
HEADS = 16
KV_HEADS = 8
HEAD_DIM = 64
FF = 4608
RANK = 16
ADAPTERS = 8
NSEQ = 4
SEGMAX = 2048
QW = 1024
KW = 512
PAIR = 2 * HEAD_DIM
BLOCK = 256
AXES = ("ctx", "head")

epsilon = 1e-05
rope_base = 1000000.0
LOG2E = math.log2(math.e)
QSCALE = HEAD_DIM**-0.5 * LOG2E
F32 = jnp.float32
BF16 = jnp.bfloat16


def matmul(left_side, right_side):
    return jnp.dot(left_side, right_side, preferred_element_type=F32)


def contract_rows(left_side, right_side):
    return lax.dot_general(left_side, right_side, (((0,), (0,)), ((), ())), preferred_element_type=F32)


def contract_cols(left_side, right_side):
    return lax.dot_general(left_side, right_side, (((1,), (1,)), ((), ())), preferred_element_type=F32)


def rope_tables(positions):
    middle = HEAD_DIM // 2
    frequency = jnp.power(rope_base, -(2.0 / HEAD_DIM) * jnp.arange(middle, dtype=F32))
    angles = positions.astype(F32)[:, None] * frequency[None, :]
    cosine, sine = jnp.cos(angles), jnp.sin(angles)
    return jnp.concatenate([cosine] * 4, axis=1), jnp.concatenate([-sine, sine] * 2, axis=1)


ANY_SPEC = pl.BlockSpec(memory_space=pl.ANY)


class Pieces:
    def __init__(self, blocks, rows):
        self.keys = [key for key, _ in blocks]
        self.blocks = [block for _, block in blocks]
        self.rows = rows

    def offsets(self):
        if self.keys[0] is None:
            return [(0, 0, self.rows)]
        depth = lax.axis_size("head")
        ctx, head = lax.axis_index("ctx"), lax.axis_index("head")
        found = []
        for flip, steps in self.keys:
            flips = [flip] if len(steps) == 1 else [flip ^ other for other in (0, 2, 4, 6)]
            size = self.blocks[0].shape[0] // (len(steps) * len(flips))
            for place, (flip, step) in enumerate([(flip, step) for flip in flips for step in steps]):
                device = jnp.bitwise_xor(ctx, flip) * depth + lax.rem(head - step + depth, depth)
                found.append((place * size, pl.multiple_of(device * size, 8), size))
        return found

    def copies(self, refs):
        found, offsets = [], self.offsets()
        share = len(offsets) // len(refs)
        for place, (source, target, size) in enumerate(offsets):
            found.append((refs[place // share], source, target, size))
        return found


def by_axes():
    return lax.axis_size("ctx") == 8 and lax.axis_size("head") == 4


def hop(value, flip, step):
    depth = lax.axis_size("head")
    pairs = [
        (ctx * depth + head, (ctx ^ flip) * depth + (head + step) % depth)
        for ctx in range(lax.axis_size("ctx"))
        for head in range(depth)
    ]
    return lax.ppermute(value, AXES, pairs)


def stack_shard(gate_up_weight, out_weight, down_weight):
    part, down_part = out_weight.shape[0], down_weight.shape[0]
    slices = 2 * FF // D

    def kernel(wide_ref, out_ref, down_ref, stacked_ref):
        for piece in range(slices):
            stacked_ref[piece * part : (piece + 1) * part, :] = wide_ref[:, piece * D : (piece + 1) * D]
        stacked_ref[slices * part : (slices + 1) * part, :] = out_ref[...]
        stacked_ref[(slices + 1) * part :, :] = down_ref[...]

    return pl.pallas_call(
        kernel,
        in_specs=[VMEM_SPEC] * 3,
        out_specs=VMEM_SPEC,
        out_shape=jax.ShapeDtypeStruct(((slices + 1) * part + down_part, D), BF16),
        name="stack_shard",
    )(gate_up_weight, out_weight, down_weight)


def whole_gather(value):
    full = lax.all_gather(value, AXES, axis=0, tiled=True)
    return Pieces([(None, full)], full.shape[0])


def start_loads(pieces, refs, target, sem):
    for ref, source, where, size in pieces.copies(refs):
        pltpu.make_async_copy(ref.at[pl.ds(source, size), :], target.at[pl.ds(where, size), :], sem).start()


def finish_loads(target, sem, columns=None):
    region = target if columns is None else target.at[:, columns]
    pltpu.make_async_copy(region, region, sem).wait()


def head_means(values, ones):
    first = values.astype(BF16)
    second = (values - first.astype(F32)).astype(BF16)
    return (matmul(first, ones) + matmul(second, ones)) * (1.0 / HEAD_DIM)


def head_ones():
    row = lax.broadcasted_iota(jnp.int32, (PAIR, PAIR), 0) // HEAD_DIM
    col = lax.broadcasted_iota(jnp.int32, (PAIR, PAIR), 1) // HEAD_DIM
    return jnp.where(row == col, 1.0, 0.0).astype(BF16)


def swapped_halves(values):
    lanes = lax.broadcasted_iota(jnp.int32, values.shape, 1)
    half = HEAD_DIM // 2
    return jnp.where(lanes % HEAD_DIM < half, pltpu.roll(values, PAIR - half, 1), pltpu.roll(values, half, 1))


def row_scale(values):
    return lax.rsqrt(jnp.mean(values * values, axis=1, keepdims=True) + epsilon)


def project_heads(hidden, gain, head_gain, tables, pieces, down, up):
    rows = hidden.shape[0]
    count = len(pieces.blocks)
    width = QW + 2 * KW

    def kernel(*refs):
        hidden_ref, gain_ref, head_gain_ref, cos_ref, sin_ref, down_ref, up_ref = refs[:7]
        blocks = refs[7 : 7 + count]
        sent_ref, low_ref, kept_ref, weight, sem = refs[7 + count :]
        start_loads(pieces, blocks, weight, sem)
        inputs = hidden_ref[...].astype(F32)
        normed = (inputs * row_scale(inputs) * gain_ref[...]).astype(BF16)
        low = contract_cols(normed, down_ref[...]).astype(BF16)
        low_ref[...] = low
        ones = head_ones()
        cos, sin = cos_ref[...], sin_ref[...]
        lanes = lax.broadcasted_iota(jnp.int32, (rows, PAIR), 1)
        finish_loads(weight, sem)

        def columns(start, size, group):
            return matmul(normed, weight[:, start : start + size]) + matmul(
                low[:, RANK * group : RANK * (group + 1)], up_ref[:, start : start + size]
            )

        def turned(values, gains):
            unit = values * lax.rsqrt(head_means(values * values, ones) + epsilon) * gains
            return unit * cos + swapped_halves(unit) * sin

        step = 2 * PAIR
        for start in range(0, QW, step):
            both = columns(start, step, 0)
            kept_ref[:, start : start + step] = both.astype(BF16)
            for side in range(2):
                query = turned(both[:, side * PAIR : (side + 1) * PAIR], head_gain_ref[0:1, :]) * QSCALE
                sent_ref[start // PAIR + side, :, :PAIR] = query.astype(BF16)
        for start in range(0, KW, step):
            both = columns(QW + start, step, 1)
            values = columns(QW + KW + start, step, 2)
            kept_ref[:, QW + start : QW + start + step] = both.astype(BF16)
            for side in range(2):
                where = slice(side * PAIR, (side + 1) * PAIR)
                key = turned(both[:, where], head_gain_ref[1:2, :])
                value = values[:, where]
                group = (start + side * PAIR) // HEAD_DIM
                sent_ref[group, :, PAIR:] = jnp.where(
                    lanes < HEAD_DIM, key, pltpu.roll(value, HEAD_DIM, 1)
                ).astype(BF16)
                sent_ref[group + 1, :, PAIR:] = jnp.where(
                    lanes < HEAD_DIM, pltpu.roll(key, HEAD_DIM, 1), value
                ).astype(BF16)

    return pl.pallas_call(
        kernel,
        in_specs=[VMEM_SPEC] * 7 + [ANY_SPEC] * count,
        out_specs=[VMEM_SPEC] * 3,
        out_shape=[
            jax.ShapeDtypeStruct((KV_HEADS, rows, 2 * PAIR), BF16),
            jax.ShapeDtypeStruct((rows, 3 * RANK), BF16),
            jax.ShapeDtypeStruct((rows, QW + KW), BF16),
        ],
        scratch_shapes=[pltpu.VMEM((D, width), BF16), pltpu.SemaphoreType.DMA],
        compiler_params=pltpu.CompilerParams(vmem_limit_bytes=40 << 20),
        cost_estimate=pl.CostEstimate(flops=2 * rows * D * width, bytes_accessed=10 << 20, transcendentals=0),
        name="project_heads",
    )(hidden, gain[None, :], head_gain, *tables, down, up, *pieces.blocks)


def project_back(back, kept, head_gain, tables, hidden, gain, low, up):
    rows = hidden.shape[0]
    width = QW + 2 * KW

    def kernel(
        back_ref, kept_ref, head_gain_ref, cos_ref, sin_ref, hidden_ref, gain_ref, low_ref, up_ref,
        grad_ref, low_grad_ref, up_grad_ref, down_grad_ref,
    ):
        ones = head_ones()
        cos, sin = cos_ref[...], sin_ref[...]
        lanes = lax.broadcasted_iota(jnp.int32, (rows, PAIR), 1)

        def through(grads, values, gains):
            slope = (grads * cos - swapped_halves(grads) * sin) * gains
            scale = lax.rsqrt(head_means(values * values, ones) + epsilon)
            unit = values * scale
            return scale * (slope - unit * head_means(slope * unit, ones))

        for group in range(KV_HEADS):
            where = slice(group * PAIR, (group + 1) * PAIR)
            grads = back_ref[group, :, :PAIR].astype(F32)
            grad_ref[:, where] = through(grads, kept_ref[:, where].astype(F32), head_gain_ref[0:1, :]).astype(BF16)
        for group in range(0, KV_HEADS, 2):
            even = back_ref[group, :, PAIR:].astype(F32)
            odd = back_ref[group + 1, :, PAIR:].astype(F32)
            keys = jnp.where(lanes < HEAD_DIM, even, pltpu.roll(odd, HEAD_DIM, 1))
            values = jnp.where(lanes < HEAD_DIM, pltpu.roll(even, HEAD_DIM, 1), odd)
            start = QW + group * HEAD_DIM
            where = slice(start, start + PAIR)
            grad_ref[:, where] = through(keys, kept_ref[:, where].astype(F32), head_gain_ref[1:2, :]).astype(BF16)
            grad_ref[:, start + KW : start + KW + PAIR] = values.astype(BF16)
        low = low_ref[...]
        turned = low.astype(F32).T.astype(BF16)
        edges = (0, QW, QW + KW, width)
        parts = []
        for group in range(3):
            where = slice(edges[group], edges[group + 1])
            grads = grad_ref[:, where]
            up_grad_ref[:, where] = matmul(turned[RANK * group : RANK * (group + 1), :], grads)
            parts.append(contract_cols(grads, up_ref[:, where]))
        low_grad = jnp.concatenate(parts, axis=1)
        low_grad_ref[...] = low_grad.astype(BF16)
        inputs = hidden_ref[...].astype(F32)
        normed = (inputs * row_scale(inputs) * gain_ref[...]).astype(BF16)
        down_grad_ref[...] = matmul(low_grad.T.astype(BF16), normed)

    return pl.pallas_call(
        kernel,
        in_specs=[VMEM_SPEC] * 9,
        out_specs=[VMEM_SPEC] * 4,
        out_shape=[
            jax.ShapeDtypeStruct((rows, width), BF16),
            jax.ShapeDtypeStruct((rows, 3 * RANK), BF16),
            jax.ShapeDtypeStruct((RANK, width), F32),
            jax.ShapeDtypeStruct((3 * RANK, D), F32),
        ],
        compiler_params=pltpu.CompilerParams(vmem_limit_bytes=40 << 20),
        name="project_back",
    )(back, kept, head_gain, *tables, hidden, gain[None, :], low, up)


def input_back(grad, low_grad, pieces, down, hidden, gain, middle_grad):
    rows = hidden.shape[0]
    count = len(pieces.blocks)

    def kernel(*refs):
        grad_ref, low_ref, down_ref, hidden_ref, gain_ref, middle_ref = refs[:6]
        blocks = refs[6 : 6 + count]
        out_ref, weight, sem = refs[6 + count :]
        start_loads(pieces, blocks, weight, sem)
        inputs = hidden_ref[...].astype(F32)
        scale = row_scale(inputs)
        slope = matmul(low_ref[...], down_ref[...])
        finish_loads(weight, sem)
        slope = (slope + contract_cols(grad_ref[...], weight[...])) * gain_ref[...]
        unit = inputs * scale
        inner = jnp.mean(slope * unit, axis=1, keepdims=True)
        out_ref[...] = middle_ref[...] + scale * (slope - unit * inner)

    return pl.pallas_call(
        kernel,
        in_specs=[VMEM_SPEC] * 6 + [ANY_SPEC] * count,
        out_specs=VMEM_SPEC,
        out_shape=jax.ShapeDtypeStruct((rows, D), F32),
        scratch_shapes=[pltpu.VMEM((D, QW + 2 * KW), BF16), pltpu.SemaphoreType.DMA],
        compiler_params=pltpu.CompilerParams(vmem_limit_bytes=40 << 20),
        cost_estimate=pl.CostEstimate(flops=2 * rows * D * 2048, bytes_accessed=10 << 20, transcendentals=0),
        name="input_back",
    )(grad, low_grad, down, hidden, gain[None, :], middle_grad, *pieces.blocks)


VMEM_SPEC = pl.BlockSpec(memory_space=pltpu.VMEM)
SMEM_SPEC = pl.BlockSpec(memory_space=pltpu.SMEM)


def lane_pad(width):
    return -(-width // 128) * 128


def layout_of(shapes):
    places = []
    offset = 0
    for index, (rows, width) in enumerate(shapes):
        for part in range(rows // RANK):
            places.append((index, part, offset, width))
            offset += width
    return places, lane_pad(offset)


def pack_adapters(adapter_ids, members, devices):
    places, width = layout_of([member.shape[1:] for member in members])
    per_seq = devices // NSEQ

    def kernel(ids, *refs):
        sources, out, slab = refs[: len(members)], refs[len(members)], refs[len(members) + 1]
        slab[...] = jnp.zeros_like(slab)
        for index, part, offset, size in places:
            slab[:, offset : offset + size] = sources[index][
                ids[pl.program_id(0)], RANK * part : RANK * (part + 1), :
            ]
        for step in range(per_seq):
            out[step] = slab[...]

    return pl.pallas_call(
        kernel,
        grid=(NSEQ,),
        in_specs=[SMEM_SPEC] + [pl.BlockSpec(member.shape, lambda s: (0, 0, 0)) for member in members],
        out_specs=pl.BlockSpec((per_seq, RANK, width), lambda s: (s, 0, 0)),
        out_shape=jax.ShapeDtypeStruct((devices, RANK, width), BF16),
        scratch_shapes=[pltpu.VMEM((RANK, width), BF16)],
        name="pack_adapters",
    )(adapter_ids, *members)


def unpack_adapters(slabs, shapes):
    devices = slabs.shape[0]
    places, _ = layout_of(shapes)

    def kernel(source, *outs):
        for index, part, offset, size in places:
            for device in range(devices):
                outs[index][RANK * part : RANK * (part + 1), device * size : (device + 1) * size] = source[
                    device, :, offset : offset + size
                ]

    return pl.pallas_call(
        kernel,
        in_specs=[VMEM_SPEC],
        out_specs=[VMEM_SPEC] * len(shapes),
        out_shape=[jax.ShapeDtypeStruct((rows, width * devices), BF16) for rows, width in shapes],
        name="unpack_adapters",
    )(slabs)


def pack_grads(grads, devices):
    places, width = layout_of([(grad.shape[0], grad.shape[1] // devices) for grad in grads])

    def kernel(*refs):
        sources, out = refs[: len(grads)], refs[len(grads)]
        for device in range(devices):
            for index, part, offset, size in places:
                out[device, :, offset : offset + size] = sources[index][
                    RANK * part : RANK * (part + 1), device * size : (device + 1) * size
                ].astype(BF16)

    return pl.pallas_call(
        kernel,
        in_specs=[VMEM_SPEC] * len(grads),
        out_specs=VMEM_SPEC,
        out_shape=jax.ShapeDtypeStruct((devices, RANK, width), BF16),
        name="pack_grads",
    )(*grads)


def reduce_grads(adapter_ids, slabs, shapes):
    devices, _, width = slabs.shape
    places, _ = layout_of(shapes)
    per_seq = devices // NSEQ

    def kernel(ids, source, *refs):
        outs, total = refs[: len(shapes)], refs[len(shapes)]
        total[...] = jnp.zeros_like(total)
        for seq in range(NSEQ):
            part_sum = jnp.sum(source[seq * per_seq : (seq + 1) * per_seq].astype(F32), axis=0)
            total[ids[seq]] += part_sum
        for index, part, offset, size in places:
            outs[index][:, RANK * part : RANK * (part + 1), :] = total[:, :, offset : offset + size]

    return pl.pallas_call(
        kernel,
        in_specs=[SMEM_SPEC, VMEM_SPEC],
        out_specs=[VMEM_SPEC] * len(shapes),
        out_shape=[jax.ShapeDtypeStruct((ADAPTERS, rows, size), F32) for rows, size in shapes],
        scratch_shapes=[pltpu.VMEM((ADAPTERS, RANK, width), F32)],
        name="reduce_grads",
    )(adapter_ids, slabs)


def split_three(value):
    first = value.astype(BF16)
    rest = value - first.astype(F32)
    second = rest.astype(BF16)
    third = (rest - second.astype(F32)).astype(BF16)
    return first, second, third


def with_columns(block, columns, lanes):
    out = jnp.where(lanes < HEAD_DIM, block, jnp.zeros_like(block))
    for step, column in enumerate(columns):
        out = jnp.where(lanes == HEAD_DIM + step, column, out)
    return out


def stacked_heads(pair, lanes):
    return jnp.concatenate([pair, pltpu.roll(pair, HEAD_DIM, 1)], axis=0)


def allowed(start_row, key_base, query_base, diagonal):
    keys = key_base + lax.broadcasted_iota(jnp.int32, (BLOCK, BLOCK), 0)
    inside = keys >= start_row
    if diagonal:
        queries = query_base + lax.broadcasted_iota(jnp.int32, (BLOCK, BLOCK), 1)
        inside = inside & (keys <= queries)
    return jnp.concatenate([inside, inside], axis=1)


def forward_attention(bounds, starts, queries, keyvals):
    rows = queries.shape[0]
    length = keyvals.shape[0]
    halo = length - rows
    steps = rows // BLOCK

    def kernel(bound_ref, start_ref, query_ref, keyval_ref, out_ref, log_ref, key_scr, value_scr):
        step = pl.program_id(0)

        @pl.when(step == 0)
        def _():
            lanes = lax.broadcasted_iota(jnp.int32, (length, 128), 1)
            both = keyval_ref[...].astype(F32)
            key_scr[...] = jnp.where(lanes < HEAD_DIM, both, 0.0).astype(BF16)
            values = jnp.where(lanes < HEAD_DIM, pltpu.roll(both, HEAD_DIM, 1), 1.0)
            value_scr[...] = values.T.astype(BF16)

        lanes = lax.broadcasted_iota(jnp.int32, (BLOCK, 128), 1)
        pair = query_ref[...].astype(F32)
        query = stacked_heads(pair, lanes).astype(BF16)
        start_row = start_ref[...]
        diagonal = halo // BLOCK + step
        first = bound_ref[0, step]
        clear = jnp.minimum(bound_ref[1, step], diagonal)

        def block(index, total, masked, is_diagonal):
            base = pl.multiple_of(index * BLOCK, BLOCK)
            scores = contract_cols(key_scr[pl.ds(base, BLOCK), :], query)
            weights = jnp.exp2(scores)
            if masked:
                keep = allowed(start_row, base, diagonal * BLOCK, is_diagonal)
                weights = jnp.where(keep, weights, 0.0)
            return total + matmul(value_scr[:, pl.ds(base, BLOCK)], weights.astype(BF16))

        total = jnp.zeros((128, 2 * BLOCK), F32)
        total = lax.fori_loop(first, clear, lambda i, t: block(i, t, True, False), total)
        total = lax.fori_loop(clear, diagonal, lambda i, t: block(i, t, False, False), total)
        total = block(diagonal, total, True, True)
        norm = total[HEAD_DIM : HEAD_DIM + 1, :]
        mixed = total[:HEAD_DIM, :] / norm
        out_ref[...] = jnp.concatenate([mixed[:, :BLOCK], mixed[:, BLOCK:]], axis=0).T.astype(BF16)
        log_ref[0] = jnp.broadcast_to(jnp.log2(norm), (8, 2 * BLOCK))

    return pl.pallas_call(
        kernel,
        grid_spec=pltpu.PrefetchScalarGridSpec(
            num_scalar_prefetch=1,
            grid=(steps,),
            in_specs=[
                pl.BlockSpec((1, BLOCK), lambda i, b: (0, i)),
                pl.BlockSpec((BLOCK, 128), lambda i, b: (i, 0)),
                pl.BlockSpec((length, 128), lambda i, b: (0, 0)),
            ],
            out_specs=[
                pl.BlockSpec((BLOCK, 128), lambda i, b: (i, 0)),
                pl.BlockSpec((1, 8, 2 * BLOCK), lambda i, b: (i, 0, 0)),
            ],
            scratch_shapes=[pltpu.VMEM((length, 128), BF16), pltpu.VMEM((128, length), BF16)],
        ),
        out_shape=[
            jax.ShapeDtypeStruct((rows, 128), BF16),
            jax.ShapeDtypeStruct((steps, 8, 2 * BLOCK), F32),
        ],
        compiler_params=pltpu.CompilerParams(vmem_limit_bytes=40 << 20),
        cost_estimate=pl.CostEstimate(
            flops=4 * rows * 1024 * 256 * 2, bytes_accessed=4 * rows * 256, transcendentals=rows * 2048
        ),
        name="forward_attention",
    )(bounds, starts, queries, keyvals)


def backward_attention(bounds, starts, queries, keyvals, mixed, logs, grads):
    rows = queries.shape[0]
    length = keyvals.shape[0]
    halo = length - rows
    steps = rows // BLOCK

    def kernel(
        bound_ref, start_ref, query_ref, keyval_ref, mixed_ref, log_ref, grad_ref,
        query_out, keyval_out, key_scr, value_scr, turned_scr, key_sum, value_sum,
    ):
        step = pl.program_id(0)

        @pl.when(step == 0)
        def _():
            lanes = lax.broadcasted_iota(jnp.int32, (length, 128), 1)
            both = keyval_ref[...].astype(F32)
            ones = jnp.where(lanes < HEAD_DIM + 3, 1.0, 0.0)
            keys = jnp.where(lanes < HEAD_DIM, both, ones)
            key_scr[...] = keys.astype(BF16)
            value_scr[...] = jnp.where(lanes < HEAD_DIM, pltpu.roll(both, HEAD_DIM, 1), ones).astype(BF16)
            turned_scr[...] = keys.T.astype(BF16)
            key_sum[...] = jnp.zeros_like(key_sum)
            value_sum[...] = jnp.zeros_like(value_sum)

        lanes = lax.broadcasted_iota(jnp.int32, (2 * BLOCK, 128), 1)
        query = stacked_heads(query_ref[...].astype(F32), lanes)
        grad = stacked_heads(grad_ref[...].astype(F32), lanes)
        weighed = stacked_heads(mixed_ref[...].astype(F32), lanes)
        inner = jnp.sum(jnp.where(lanes < HEAD_DIM, grad * weighed, 0.0), axis=1, keepdims=True)
        log_column = log_ref[0].T[:, :1]
        query_low = with_columns(query, [part.astype(F32) for part in split_three(-log_column)], lanes).astype(BF16)
        grad_low = with_columns(grad, [part.astype(F32) for part in split_three(-inner)], lanes).astype(BF16)
        start_row = start_ref[...]
        diagonal = halo // BLOCK + step
        first = bound_ref[0, step]
        clear = jnp.minimum(bound_ref[1, step], diagonal)

        def block(index, total, masked, is_diagonal):
            base = pl.multiple_of(index * BLOCK, BLOCK)
            where = pl.ds(base, BLOCK)
            weights = jnp.exp2(contract_cols(key_scr[where, :], query_low))
            if masked:
                keep = allowed(start_row, base, diagonal * BLOCK, is_diagonal)
                weights = jnp.where(keep, weights, 0.0)
            slopes = (weights * contract_cols(value_scr[where, :], grad_low)).astype(BF16)
            value_sum[where, :] += matmul(weights.astype(BF16), grad_low)
            key_sum[where, :] += matmul(slopes, query_low)
            return total + matmul(turned_scr[:, where], slopes)

        total = jnp.zeros((128, 2 * BLOCK), F32)
        total = lax.fori_loop(first, clear, lambda i, t: block(i, t, True, False), total)
        total = lax.fori_loop(clear, diagonal, lambda i, t: block(i, t, False, False), total)
        total = block(diagonal, total, True, True)
        total = total[:HEAD_DIM] * HEAD_DIM**-0.5
        query_out[...] = jnp.concatenate([total[:, :BLOCK], total[:, BLOCK:]], axis=0).T.astype(BF16)

        @pl.when(step == steps - 1)
        def _():
            whole = lax.broadcasted_iota(jnp.int32, (length, 128), 1)
            keyval_out[...] = jnp.where(
                whole < HEAD_DIM, key_sum[...] * (1.0 / LOG2E), pltpu.roll(value_sum[...], HEAD_DIM, 1)
            ).astype(keyval_out.dtype)

    return pl.pallas_call(
        kernel,
        grid_spec=pltpu.PrefetchScalarGridSpec(
            num_scalar_prefetch=1,
            grid=(steps,),
            in_specs=[
                pl.BlockSpec((1, BLOCK), lambda i, b: (0, i)),
                pl.BlockSpec((BLOCK, 128), lambda i, b: (i, 0)),
                pl.BlockSpec((length, 128), lambda i, b: (0, 0)),
                pl.BlockSpec((BLOCK, 128), lambda i, b: (i, 0)),
                pl.BlockSpec((1, 8, 2 * BLOCK), lambda i, b: (i, 0, 0)),
                pl.BlockSpec((BLOCK, 128), lambda i, b: (i, 0)),
            ],
            out_specs=[
                pl.BlockSpec((BLOCK, 128), lambda i, b: (i, 0)),
                pl.BlockSpec((length, 128), lambda i, b: (0, 0)),
            ],
            scratch_shapes=[
                pltpu.VMEM((length, 128), BF16),
                pltpu.VMEM((length, 128), BF16),
                pltpu.VMEM((128, length), BF16),
                pltpu.VMEM((length, 128), F32),
                pltpu.VMEM((length, 128), F32),
            ],
        ),
        out_shape=[
            jax.ShapeDtypeStruct((rows, 128), BF16),
            jax.ShapeDtypeStruct((length, 128), F32 if halo else BF16),
        ],
        compiler_params=pltpu.CompilerParams(vmem_limit_bytes=48 << 20),
        cost_estimate=pl.CostEstimate(
            flops=10 * rows * 1024 * 256 * 2, bytes_accessed=8 * rows * 256, transcendentals=rows * 2048
        ),
        name="backward_attention",
    )(bounds, starts, queries, keyvals, mixed, logs, grads)


def document_bounds(segment_ids, origin, halo, span, seq_start):
    tokens = segment_ids.shape[0]
    names = jnp.arange(tokens // (SEGMAX // 2), dtype=jnp.int32)
    begin = jnp.sum((segment_ids[None, :] < names[:, None]).astype(jnp.int32), axis=1)
    own = lax.dynamic_slice_in_dim(segment_ids, origin, span, 0)
    start = jnp.sum(jnp.where(own[None, :] == names[:, None], begin[:, None], 0), axis=0)
    start = jnp.maximum(start, seq_start) - (origin - halo)
    first = start[::BLOCK] // BLOCK
    clear = -(-start[BLOCK - 1 :: BLOCK] // BLOCK)
    bounds = jnp.stack([first, jnp.maximum(clear, first)])
    return bounds, start[None, :]


TILE = 512


def silu_parts(gate):
    share = 1.0 / (1.0 + jnp.exp(-gate))
    return share, gate * share


def feed_forward(mixed, hidden, cotangent, gain, weights, chosen):
    members, rows, _ = mixed.shape
    tiles = FF // TILE
    packed = isinstance(weights, Pieces)
    arrays = weights.blocks if packed else weights
    count = len(arrays)
    slices = 2 * FF // D

    def kernel(*refs):
        (
            mixed_ref, hidden_ref, cot_ref, gain_ref,
            out_down_ref, out_up_ref, mlp_down_ref, mlp_up_ref, ffd_down_ref, ffd_up_ref,
        ) = refs[:10]
        weight_refs = refs[10 : 10 + count]
        (
            output_ref, middle_grad_ref, mixed_grad_ref,
            out_down_grad, out_up_grad, mlp_down_grad, mlp_up_grad, ffd_down_grad, ffd_up_grad,
            wide_scr, down_scr, mix_scr, middle_scr, normed_scr, branch_scr, slope_scr,
            low_scr, low_turned, back_scr, back_turned, out_low_scr, down_sum, gate_sum, up_sum, sems,
        ) = refs[10 + count :]
        out_columns = slice(2 * FF, 2 * FF + D)

        def column_piece(piece):
            return slice(piece * D, (piece + 1) * D)

        if packed:
            blocks = weights.copies(weight_refs)
            devices = len(blocks)
            part, down_part = D // devices, FF // devices

            def start_piece(piece):
                for ref, source, where, size in blocks:
                    row = pl.multiple_of(where // size * part, 8)
                    pltpu.make_async_copy(
                        ref.at[pl.ds(source + piece * part, part), :],
                        wide_scr.at[pl.ds(row, part), column_piece(piece)],
                        sems.at[piece],
                    ).start()

            def start_down():
                for ref, source, where, size in blocks:
                    row = pl.multiple_of(where // size * down_part, 8)
                    pltpu.make_async_copy(
                        ref.at[pl.ds(source + (slices + 1) * part, down_part), :],
                        down_scr.at[pl.ds(row, down_part), :],
                        sems.at[slices + 1],
                    ).start()
        else:

            def start_piece(piece):
                columns = column_piece(piece)
                pltpu.make_async_copy(
                    weight_refs[0].at[:, columns], wide_scr.at[:, columns], sems.at[piece]
                ).start()

            def start_down():
                pltpu.make_async_copy(weight_refs[1], down_scr, sems.at[slices + 1]).start()

        def finish_piece(piece):
            region = wide_scr.at[:, column_piece(piece)]
            pltpu.make_async_copy(region, region, sems.at[piece]).wait()

        per_piece = D // TILE
        first_use = {}
        for piece in range(slices):
            uses = [c // TILE % tiles for c in range(piece * D, (piece + 1) * D, TILE)]
            first_use.setdefault(min(uses), []).append(piece)
        start_piece(slices)
        for piece in first_use[0]:
            start_piece(piece)
        start_down()

        cot = cot_ref[...]
        for member in range(members):
            mix_scr[:, member * PAIR : (member + 1) * PAIR] = mixed_ref[member]
        out_low = contract_cols(mix_scr[...], out_down_ref[...]).astype(BF16)
        out_low_scr[...] = out_low
        back = contract_cols(cot, ffd_up_ref[...])
        back_scr[...] = back.astype(BF16)
        back_turned[...] = back.T.astype(BF16)
        branch_scr[...] = jnp.zeros_like(branch_scr)
        slope_scr[...] = jnp.zeros_like(slope_scr)
        down_sum[...] = jnp.zeros_like(down_sum)
        gate_sum[...] = jnp.zeros_like(gate_sum)
        up_sum[...] = jnp.zeros_like(up_sum)
        finish_piece(slices)
        middle = (
            hidden_ref[...].astype(F32)
            + matmul(mix_scr[...], wide_scr[:, out_columns])
            + matmul(out_low, out_up_ref[...])
        )
        middle_scr[...] = middle
        normed = (middle * row_scale(middle) * gain_ref[...]).astype(BF16)
        normed_scr[...] = normed
        low = contract_cols(normed, mlp_down_ref[...])
        low_scr[...] = low.astype(BF16)
        low_turned[...] = low.T.astype(BF16)
        pltpu.make_async_copy(down_scr, down_scr, sems.at[slices + 1]).wait()

        def tile(index, carry):
            base = pl.multiple_of(index * TILE, TILE)
            gate_at, up_at = pl.ds(base, TILE), pl.ds(base + FF, TILE)
            for use, group in sorted(first_use.items()):

                @pl.when(index == use)
                def _(group=group):
                    for piece in group:
                        finish_piece(piece)

                if use > 0:

                    @pl.when(index == max(use - per_piece, 0))
                    def _(group=group):
                        for piece in group:
                            start_piece(piece)

            normed = normed_scr[...]
            low = low_scr[...]
            gate = matmul(normed, wide_scr[:, gate_at]) + matmul(low[:, :RANK], mlp_up_ref[:, gate_at])
            up = matmul(normed, wide_scr[:, up_at]) + matmul(low[:, RANK:], mlp_up_ref[:, up_at])
            share, active = silu_parts(gate)
            units = (active * up).astype(BF16)
            down = down_scr[gate_at, :]
            branch_scr[...] += matmul(units, down)
            down_sum[...] += contract_cols(units, ffd_down_ref[:, gate_at])
            ffd_down_grad[:, gate_at] = matmul(back_turned[...], units)
            units_grad = contract_cols(cot_ref[...], down) + matmul(back_scr[...], ffd_down_ref[:, gate_at])
            gate_grad = (units_grad * up * (share * (1.0 + gate * (1.0 - share)))).astype(BF16)
            up_grad = (units_grad * active).astype(BF16)
            slope_scr[...] += contract_cols(gate_grad, wide_scr[:, gate_at]) + contract_cols(
                up_grad, wide_scr[:, up_at]
            )
            gate_sum[...] += contract_cols(gate_grad, mlp_up_ref[:, gate_at])
            up_sum[...] += contract_cols(up_grad, mlp_up_ref[:, up_at])
            mlp_up_grad[:, gate_at] = matmul(low_turned[:RANK, :], gate_grad)
            mlp_up_grad[:, up_at] = matmul(low_turned[RANK:, :], up_grad)
            return carry

        lax.fori_loop(0, tiles, tile, 0)

        middle = middle_scr[...]
        cot = cot_ref[...]
        down_low = down_sum[...].astype(BF16)
        output_ref[...] = (middle + branch_scr[...] + matmul(down_low, ffd_up_ref[...])).astype(BF16)
        ffd_up_grad[...] = contract_rows(down_low, cot)
        low_grad = jnp.concatenate([gate_sum[...], up_sum[...]], axis=1).astype(BF16)
        mlp_down_grad[...] = contract_rows(low_grad, normed_scr[...])
        slope = gain_ref[...] * (slope_scr[...] + matmul(low_grad, mlp_down_ref[...]))
        scale = row_scale(middle)
        inner = jnp.mean(slope * middle, axis=1, keepdims=True)
        middle_grad = cot.astype(F32) + scale * slope - middle * (scale * scale * scale * inner)
        middle_grad_ref[...] = middle_grad
        branch_grad = middle_grad.astype(BF16)
        out_up_grad[...] = contract_rows(out_low_scr[...], branch_grad)
        out_low_grad = contract_cols(branch_grad, out_up_ref[...]).astype(BF16)
        out_down_grad[...] = contract_rows(out_low_grad, mix_scr[...])
        mixed_grad = contract_cols(branch_grad, wide_scr[:, out_columns]) + matmul(out_low_grad, out_down_ref[...])
        for member in range(members):
            mixed_grad_ref[member] = mixed_grad[:, member * PAIR : (member + 1) * PAIR].astype(BF16)

    results = pl.pallas_call(
        kernel,
        in_specs=[VMEM_SPEC] * 10 + [ANY_SPEC] * count,
        out_specs=[VMEM_SPEC] * 9,
        out_shape=[
            jax.ShapeDtypeStruct((rows, D), BF16),
            jax.ShapeDtypeStruct((rows, D), F32),
            jax.ShapeDtypeStruct((members, rows, PAIR), BF16),
            jax.ShapeDtypeStruct((RANK, QW), F32),
            jax.ShapeDtypeStruct((RANK, D), F32),
            jax.ShapeDtypeStruct((2 * RANK, D), F32),
            jax.ShapeDtypeStruct((RANK, 2 * FF), F32),
            jax.ShapeDtypeStruct((RANK, FF), F32),
            jax.ShapeDtypeStruct((RANK, D), F32),
        ],
        scratch_shapes=[
            pltpu.VMEM((D, 2 * FF + D), BF16), pltpu.VMEM((FF, D), BF16),
            pltpu.VMEM((rows, QW), BF16), pltpu.VMEM((rows, D), F32), pltpu.VMEM((rows, D), BF16),
            pltpu.VMEM((rows, D), F32), pltpu.VMEM((rows, D), F32),
            pltpu.VMEM((rows, 2 * RANK), BF16), pltpu.VMEM((2 * RANK, rows), BF16),
            pltpu.VMEM((rows, RANK), BF16), pltpu.VMEM((RANK, rows), BF16), pltpu.VMEM((rows, RANK), BF16),
            pltpu.VMEM((rows, RANK), F32), pltpu.VMEM((rows, RANK), F32), pltpu.VMEM((rows, RANK), F32),
            pltpu.SemaphoreType.DMA((2 + slices,)),
        ],
        compiler_params=pltpu.CompilerParams(vmem_limit_bytes=60 << 20),
        cost_estimate=pl.CostEstimate(
            flops=rows * (12 * D * FF + 4 * D * QW), bytes_accessed=6 * D * FF + 16 * rows * D,
            transcendentals=rows * FF,
        ),
        name="feed_forward",
    )(mixed, hidden, cotangent, gain[None, :], *chosen, *arrays)
    return results[0], results[1], results[2], list(results[3:])


def local(
    hidden, cotangent, segment_ids, adapter_ids, attn_gain, query_gain, key_gain, ffn_gain,
    qkv_weight, out_weight, gate_up_weight, down_weight, *adapters,
):
    rows = hidden.shape[0]
    devices = lax.axis_size("ctx") * lax.axis_size("head")
    members = KV_HEADS
    groups = [[members * g + i for i in range(members)] for g in range(devices // members)]
    span = rows * members
    seq_length = rows * devices // NSEQ
    halo = 0 if span == seq_length else SEGMAX
    here = lax.axis_index("ctx") * lax.axis_size("head") + lax.axis_index("head")
    origin = here // members * span
    seq_start = origin // seq_length * seq_length
    positions = here * rows - seq_start + jnp.arange(rows, dtype=jnp.int32)
    bounds, starts = document_bounds(segment_ids, origin, halo, span, seq_start)

    def swap(value):
        return lax.all_to_all(value, AXES, 0, 0, axis_index_groups=groups, tiled=True)

    def shifted(value, by):
        pairs = [(i, i + by) for i in range(devices) if 0 <= i + by < devices]
        return lax.ppermute(value, AXES, pairs)

    def gather(value):
        return lax.all_gather(value, AXES, axis=0, tiled=True)

    shapes = [member.shape[1:] for member in adapters]
    def exchange_adapters(members):
        return lax.all_to_all(pack_adapters(adapter_ids, members, devices), AXES, 0, 0, tiled=True)

    spread = by_axes()
    if spread:
        found = {(0, 0): stack_shard(gate_up_weight, out_weight, down_weight)}
        pending = []

        def move(*keys, extra=()):
            hops = [(found[key[0] ^ key[2], key[1] - key[3]], key[2], key[3]) for key in keys]
            hops += extra
            held = lax.optimization_barrier((*[value for value, _, _ in hops], *pending))
            results = [hop(value, flip, step) for value, (_, flip, step) in zip(held, hops)]
            found.update(zip([key[:2] for key in keys], results))
            pending[:] = results
            return results[len(keys) :]

        def cores(*keys):
            return [(flip, step, 1, 0) for flip, step in keys]

        def then(value):
            return lax.optimization_barrier((value, *pending))[0]

        line = move(extra=[(qkv_weight, 0, step) for step in range(1, 4)])
        slabs = exchange_adapters(adapters[:2])
        line = jnp.concatenate([qkv_weight] + line, axis=0)
        plane = move((0, 1, 0, 1), extra=[(line, flip, 0) for flip in (2, 4, 6)])
        pending.append(slabs)
        plane = jnp.concatenate([line] + plane, axis=0)
        (across,) = move((0, 2, 0, 1), (2, 0, 2, 0), (4, 0, 4, 0), extra=[(plane, 1, 0)])
        qkv = Pieces([((0, (0, 1, 2, 3)), plane), ((1, (0, 1, 2, 3)), across)], D)
        hidden_then = hidden
    else:
        qkv = whole_gather(qkv_weight)
        weights = [gather(jnp.concatenate([gate_up_weight, out_weight], axis=1)), gather(down_weight)]
        hidden_then = hidden
        slabs = exchange_adapters(adapters[:2])
    chosen = list(unpack_adapters(slabs, shapes[:2]))

    head_gain = jnp.stack([jnp.tile(query_gain, 2), jnp.tile(key_gain, 2)])
    tables = rope_tables(positions)
    sent, low_qkv, kept = project_heads(hidden_then, attn_gain, head_gain, tables, qkv, chosen[0], chosen[1])
    arrived = swap(sent).reshape(span, 2 * PAIR)
    queries = arrived[:, :PAIR]
    keyval_rows = arrived[:, PAIR:]
    if halo:
        keyval_rows = jnp.concatenate([shifted(keyval_rows[span - halo :], members), keyval_rows], axis=0)
    if spread:
        move((2, 1, 2, 0), (6, 0, 4, 0), *cores((1, 0)))
        first = pending[:]
        move((0, 3, 0, 1))
        pending[:] = first
        move((2, 2, 2, 0), (4, 1, 4, 0), *cores((1, 1), (3, 0)))
        move((6, 1, 2, 0), (4, 2, 4, 0), *cores((5, 0), (7, 0)))
        queries = then(queries)
        move((2, 3, 2, 0), (4, 3, 4, 0), *cores((1, 2), (3, 1), (5, 1)))
        slabs = exchange_adapters(lax.optimization_barrier((*adapters[2:], arrived))[:-1])
    else:
        slabs = exchange_adapters(adapters[2:])
    mixed, logs = forward_attention(bounds, starts, queries, keyval_rows)
    chosen += list(unpack_adapters(slabs, shapes[2:]))
    if spread:
        pending.append(logs)
        move((6, 3, 2, 0), (6, 2, 4, 0), *cores((3, 2), (5, 2), (1, 3), (7, 1)))
        move(*cores((3, 3), (5, 3), (7, 3), (7, 2)))
        weights = Pieces([((flip, (step,)), block) for (flip, step), block in found.items()], D)
    mixture_tok = swap(mixed.reshape(members, rows, PAIR))
    output, middle_grad, mixture_grad, early = feed_forward(
        mixture_tok, hidden, cotangent, ffn_gain, weights, chosen[2:]
    )
    grad_rows = swap(mixture_grad).reshape(span, PAIR)
    early_slabs = lax.all_to_all(pack_grads(early, devices), AXES, 0, 0, tiled=True)
    early_owned = reduce_grads(adapter_ids, early_slabs, shapes[2:])

    query_grads, keyval_grads = backward_attention(
        bounds, starts, queries, keyval_rows, mixed, logs, grad_rows
    )
    if halo:
        returned = shifted(keyval_grads[:halo].astype(BF16), -members).astype(F32)
        keyval_grads = jnp.concatenate(
            [keyval_grads[halo : halo + span - halo], keyval_grads[span:] + returned], axis=0
        ).astype(BF16)
    back = jnp.concatenate([query_grads, keyval_grads], axis=1).reshape(members, rows, 2 * PAIR)
    projected_grad, low_grad, qkv_up_grad, qkv_down_grad = project_back(
        swap(back), kept, head_gain, tables, hidden, attn_gain, low_qkv, chosen[1]
    )
    late_slabs = lax.all_to_all(pack_grads([qkv_down_grad, qkv_up_grad], devices), AXES, 0, 0, tiled=True)
    late_owned = reduce_grads(adapter_ids, late_slabs, shapes[:2])
    input_grad = input_back(projected_grad, low_grad, qkv, chosen[0], hidden, attn_gain, middle_grad)
    return (output, input_grad, *late_owned, *early_owned)


def solution(mesh):
    by_rows = P(AXES, None)
    by_cols = P(None, None, AXES)
    placed = (by_rows, by_rows) + (P(),) * 6 + (by_rows,) * 4 + (by_cols,) * 8
    return jax.shard_map(
        local,
        mesh=mesh,
        in_specs=placed,
        out_specs=(by_rows, by_rows) + (by_cols,) * 8,
        check_vma=False,
    )
```

```python
import functools
import math

import jax
import jax.numpy as jnp
from jax import lax
from jax.experimental import pallas as pl
from jax.experimental.pallas import tpu as pltpu
from jax.sharding import PartitionSpec as P

D = 1024
HEADS = 16
KV_HEADS = 8
HEAD_DIM = 64
FF = 4608
RANK = 16
ADAPTERS = 8
NSEQ = 4
SEGMAX = 2048
QW = 1024
KW = 512
PAIR = 2 * HEAD_DIM
BLOCK = 256
AXES = ("ctx", "head")

epsilon = 1e-05
rope_base = 1000000.0
LOG2E = math.log2(math.e)
QSCALE = HEAD_DIM**-0.5 * LOG2E
F32 = jnp.float32
BF16 = jnp.bfloat16


def matmul(left_side, right_side):
    return jnp.dot(left_side, right_side, preferred_element_type=F32)


def contract_rows(left_side, right_side):
    return lax.dot_general(left_side, right_side, (((0,), (0,)), ((), ())), preferred_element_type=F32)


def contract_cols(left_side, right_side):
    return lax.dot_general(left_side, right_side, (((1,), (1,)), ((), ())), preferred_element_type=F32)


def rope_tables(positions):
    middle = HEAD_DIM // 2
    frequency = jnp.power(rope_base, -(2.0 / HEAD_DIM) * jnp.arange(middle, dtype=F32))
    angles = positions.astype(F32)[:, None] * frequency[None, :]
    cosine, sine = jnp.cos(angles), jnp.sin(angles)
    return jnp.concatenate([cosine] * 4, axis=1), jnp.concatenate([-sine, sine] * 2, axis=1)


ANY_SPEC = pl.BlockSpec(memory_space=pl.ANY)


class Pieces:
    def __init__(self, blocks, rows):
        self.keys = [key for key, _ in blocks]
        self.blocks = [block for _, block in blocks]
        self.rows = rows

    def offsets(self):
        if self.keys[0] is None:
            return [(0, 0, self.rows)]
        depth = lax.axis_size("head")
        ctx, head = lax.axis_index("ctx"), lax.axis_index("head")
        found = []
        for flip, steps in self.keys:
            flips = [flip] if len(steps) == 1 else [flip ^ other for other in (0, 2, 4, 6)]
            size = self.blocks[0].shape[0] // (len(steps) * len(flips))
            for place, (flip, step) in enumerate([(flip, step) for flip in flips for step in steps]):
                device = jnp.bitwise_xor(ctx, flip) * depth + lax.rem(head - step + depth, depth)
                found.append((place * size, pl.multiple_of(device * size, 8), size))
        return found

    def copies(self, refs):
        found, offsets = [], self.offsets()
        share = len(offsets) // len(refs)
        for place, (source, target, size) in enumerate(offsets):
            found.append((refs[place // share], source, target, size))
        return found


def by_axes():
    return lax.axis_size("ctx") == 8 and lax.axis_size("head") == 4


def hop(value, flip, step):
    depth = lax.axis_size("head")
    pairs = [
        (ctx * depth + head, (ctx ^ flip) * depth + (head + step) % depth)
        for ctx in range(lax.axis_size("ctx"))
        for head in range(depth)
    ]
    return lax.ppermute(value, AXES, pairs)


def stack_shard(gate_up_weight, out_weight, down_weight):
    part, down_part = out_weight.shape[0], down_weight.shape[0]
    slices = 2 * FF // D

    def kernel(wide_ref, out_ref, down_ref, stacked_ref):
        for piece in range(slices):
            stacked_ref[piece * part : (piece + 1) * part, :] = wide_ref[:, piece * D : (piece + 1) * D]
        stacked_ref[slices * part : (slices + 1) * part, :] = out_ref[...]
        stacked_ref[(slices + 1) * part :, :] = down_ref[...]

    return pl.pallas_call(
        kernel,
        in_specs=[VMEM_SPEC] * 3,
        out_specs=VMEM_SPEC,
        out_shape=jax.ShapeDtypeStruct(((slices + 1) * part + down_part, D), BF16),
        name="stack_shard",
    )(gate_up_weight, out_weight, down_weight)


def whole_gather(value):
    full = lax.all_gather(value, AXES, axis=0, tiled=True)
    return Pieces([(None, full)], full.shape[0])


def start_loads(pieces, refs, target, sem):
    for ref, source, where, size in pieces.copies(refs):
        pltpu.make_async_copy(ref.at[pl.ds(source, size), :], target.at[pl.ds(where, size), :], sem).start()


def finish_loads(target, sem, columns=None):
    region = target if columns is None else target.at[:, columns]
    pltpu.make_async_copy(region, region, sem).wait()


def head_means(values, ones):
    first = values.astype(BF16)
    second = (values - first.astype(F32)).astype(BF16)
    return (matmul(first, ones) + matmul(second, ones)) * (1.0 / HEAD_DIM)


def head_ones():
    row = lax.broadcasted_iota(jnp.int32, (PAIR, PAIR), 0) // HEAD_DIM
    col = lax.broadcasted_iota(jnp.int32, (PAIR, PAIR), 1) // HEAD_DIM
    return jnp.where(row == col, 1.0, 0.0).astype(BF16)


def swapped_halves(values):
    lanes = lax.broadcasted_iota(jnp.int32, values.shape, 1)
    half = HEAD_DIM // 2
    return jnp.where(lanes % HEAD_DIM < half, pltpu.roll(values, PAIR - half, 1), pltpu.roll(values, half, 1))


def row_scale(values):
    return lax.rsqrt(jnp.mean(values * values, axis=1, keepdims=True) + epsilon)


ROWS = 256


def in_hbm(value):
    return pltpu.with_memory_space_constraint(value, pltpu.HBM)


def row_block(width):
    return pl.BlockSpec((ROWS, width), lambda i: (i, 0))


def fixed(shape):
    return pl.BlockSpec(shape, lambda i: (0,) * len(shape))


def project_heads(hidden, gain, head_gain, tables, pieces, down, up):
    rows = hidden.shape[0]
    count = len(pieces.blocks)
    width = QW + 2 * KW

    def kernel(*refs):
        hidden_ref, gain_ref, head_gain_ref, cos_ref, sin_ref, down_ref, up_ref = refs[:7]
        blocks = refs[7 : 7 + count]
        sent_ref, low_ref, kept_ref, weight, sem = refs[7 + count :]

        @pl.when(pl.program_id(0) == 0)
        def _():
            start_loads(pieces, blocks, weight, sem)
            finish_loads(weight, sem)

        inputs = hidden_ref[...].astype(F32)
        normed = (inputs * row_scale(inputs) * gain_ref[...]).astype(BF16)
        low = contract_cols(normed, down_ref[...]).astype(BF16)
        low_ref[...] = low
        ones = head_ones()
        cos, sin = cos_ref[...], sin_ref[...]
        lanes = lax.broadcasted_iota(jnp.int32, (ROWS, PAIR), 1)

        def columns(start, size, group):
            return matmul(normed, weight[:, start : start + size]) + matmul(
                low[:, RANK * group : RANK * (group + 1)], up_ref[:, start : start + size]
            )

        def turned(values, gains):
            unit = values * lax.rsqrt(head_means(values * values, ones) + epsilon) * gains
            return unit * cos + swapped_halves(unit) * sin

        step = 4 * PAIR
        for start in range(0, QW, step):
            some = columns(start, step, 0)
            kept_ref[:, start : start + step] = some.astype(BF16)
            for side in range(step // PAIR):
                query = turned(some[:, side * PAIR : (side + 1) * PAIR], head_gain_ref[0:1, :]) * QSCALE
                sent_ref[start // PAIR + side, :, :PAIR] = query.astype(BF16)
        for start in range(0, KW, step):
            some = columns(QW + start, step, 1)
            values = columns(QW + KW + start, step, 2)
            kept_ref[:, QW + start : QW + start + step] = some.astype(BF16)
            for side in range(step // PAIR):
                where = slice(side * PAIR, (side + 1) * PAIR)
                key = turned(some[:, where], head_gain_ref[1:2, :])
                value = values[:, where]
                group = (start + side * PAIR) // HEAD_DIM
                sent_ref[group, :, PAIR:] = jnp.where(
                    lanes < HEAD_DIM, key, pltpu.roll(value, HEAD_DIM, 1)
                ).astype(BF16)
                sent_ref[group + 1, :, PAIR:] = jnp.where(
                    lanes < HEAD_DIM, pltpu.roll(key, HEAD_DIM, 1), value
                ).astype(BF16)

    return pl.pallas_call(
        kernel,
        grid=(rows // ROWS,),
        in_specs=[
            row_block(D), fixed((1, D)), fixed((2, PAIR)), row_block(PAIR), row_block(PAIR),
            fixed((3 * RANK, D)), fixed((RANK, width)),
        ]
        + [ANY_SPEC] * count,
        out_specs=[
            pl.BlockSpec((KV_HEADS, ROWS, 2 * PAIR), lambda i: (0, i, 0)), row_block(3 * RANK), row_block(QW + KW),
        ],
        out_shape=[
            jax.ShapeDtypeStruct((KV_HEADS, rows, 2 * PAIR), BF16),
            jax.ShapeDtypeStruct((rows, 3 * RANK), BF16),
            jax.ShapeDtypeStruct((rows, QW + KW), BF16),
        ],
        scratch_shapes=[pltpu.VMEM((D, width), BF16), pltpu.SemaphoreType.DMA],
        compiler_params=pltpu.CompilerParams(vmem_limit_bytes=40 << 20),
        cost_estimate=pl.CostEstimate(flops=2 * rows * D * width, bytes_accessed=10 << 20, transcendentals=0),
        name="project_heads",
    )(hidden, gain[None, :], head_gain, *tables, down, up, *pieces.blocks)


def project_back(back, kept, head_gain, tables, hidden, gain, low, up, devices):
    rows = hidden.shape[0]
    width = QW + 2 * KW
    places, slab = layout_of([(3 * RANK, D // devices), (RANK, width // devices)])

    def kernel(
        back_ref, kept_ref, head_gain_ref, cos_ref, sin_ref, hidden_ref, gain_ref, low_ref, up_ref,
        grad_ref, low_grad_ref, packed_ref, down_sum, up_sum,
    ):
        ones = head_ones()
        cos, sin = cos_ref[...], sin_ref[...]
        lanes = lax.broadcasted_iota(jnp.int32, (ROWS, PAIR), 1)

        @pl.when(pl.program_id(0) == 0)
        def _():
            down_sum[...] = jnp.zeros_like(down_sum)
            up_sum[...] = jnp.zeros_like(up_sum)

        def through(grads, values, gains):
            slope = (grads * cos - swapped_halves(grads) * sin) * gains
            scale = lax.rsqrt(head_means(values * values, ones) + epsilon)
            unit = values * scale
            return scale * (slope - unit * head_means(slope * unit, ones))

        for group in range(KV_HEADS):
            where = slice(group * PAIR, (group + 1) * PAIR)
            grads = back_ref[group, :, :PAIR].astype(F32)
            grad_ref[:, where] = through(grads, kept_ref[:, where].astype(F32), head_gain_ref[0:1, :]).astype(BF16)
        for group in range(0, KV_HEADS, 2):
            even = back_ref[group, :, PAIR:].astype(F32)
            odd = back_ref[group + 1, :, PAIR:].astype(F32)
            keys = jnp.where(lanes < HEAD_DIM, even, pltpu.roll(odd, HEAD_DIM, 1))
            values = jnp.where(lanes < HEAD_DIM, pltpu.roll(even, HEAD_DIM, 1), odd)
            start = QW + group * HEAD_DIM
            where = slice(start, start + PAIR)
            grad_ref[:, where] = through(keys, kept_ref[:, where].astype(F32), head_gain_ref[1:2, :]).astype(BF16)
            grad_ref[:, start + KW : start + KW + PAIR] = values.astype(BF16)
        turned = low_ref[...].astype(F32).T.astype(BF16)
        edges = (0, QW, QW + KW, width)
        parts = []
        for group in range(3):
            where = slice(edges[group], edges[group + 1])
            grads = grad_ref[:, where]
            up_sum[:, where] += matmul(turned[RANK * group : RANK * (group + 1), :], grads)
            parts.append(contract_cols(grads, up_ref[:, where]))
        low_grad = jnp.concatenate(parts, axis=1)
        low_grad_ref[...] = low_grad.astype(BF16)
        inputs = hidden_ref[...].astype(F32)
        normed = (inputs * row_scale(inputs) * gain_ref[...]).astype(BF16)
        down_sum[...] += matmul(low_grad.T.astype(BF16), normed)

        @pl.when(pl.program_id(0) == rows // ROWS - 1)
        def _():
            for device in range(devices):
                for index, part, offset, size in places:
                    packed_ref[device, :, offset : offset + size] = (down_sum, up_sum)[index][
                        RANK * part : RANK * (part + 1), device * size : (device + 1) * size
                    ].astype(BF16)

    return pl.pallas_call(
        kernel,
        grid=(rows // ROWS,),
        in_specs=[
            pl.BlockSpec((KV_HEADS, ROWS, 2 * PAIR), lambda i: (0, i, 0)), row_block(QW + KW), fixed((2, PAIR)),
            row_block(PAIR), row_block(PAIR), row_block(D), fixed((1, D)), row_block(3 * RANK), fixed((RANK, width)),
        ],
        out_specs=[row_block(width), row_block(3 * RANK), fixed((devices, RANK, slab))],
        out_shape=[
            jax.ShapeDtypeStruct((rows, width), BF16),
            jax.ShapeDtypeStruct((rows, 3 * RANK), BF16),
            jax.ShapeDtypeStruct((devices, RANK, slab), BF16),
        ],
        scratch_shapes=[pltpu.VMEM((3 * RANK, D), F32), pltpu.VMEM((RANK, width), F32)],
        compiler_params=pltpu.CompilerParams(vmem_limit_bytes=40 << 20),
        name="project_back",
    )(back, in_hbm(kept), head_gain, *[in_hbm(table) for table in tables], hidden, gain[None, :], in_hbm(low), up)


def input_back(grad, low_grad, pieces, down, hidden, gain, middle_grad):
    rows = hidden.shape[0]
    count = len(pieces.blocks)

    def kernel(*refs):
        grad_ref, low_ref, down_ref, hidden_ref, gain_ref, middle_ref = refs[:6]
        blocks = refs[6 : 6 + count]
        out_ref, weight, sem = refs[6 + count :]

        @pl.when(pl.program_id(0) == 0)
        def _():
            start_loads(pieces, blocks, weight, sem)
            finish_loads(weight, sem)

        inputs = hidden_ref[...].astype(F32)
        scale = row_scale(inputs)
        slope = matmul(low_ref[...], down_ref[...]) + contract_cols(grad_ref[...], weight[...])
        slope = slope * gain_ref[...]
        unit = inputs * scale
        inner = jnp.mean(slope * unit, axis=1, keepdims=True)
        out_ref[...] = middle_ref[...] + scale * (slope - unit * inner)

    return pl.pallas_call(
        kernel,
        grid=(rows // ROWS,),
        in_specs=[
            row_block(QW + 2 * KW), row_block(3 * RANK), fixed((3 * RANK, D)), row_block(D), fixed((1, D)), row_block(D),
        ]
        + [ANY_SPEC] * count,
        out_specs=row_block(D),
        out_shape=jax.ShapeDtypeStruct((rows, D), F32),
        scratch_shapes=[pltpu.VMEM((D, QW + 2 * KW), BF16), pltpu.SemaphoreType.DMA],
        compiler_params=pltpu.CompilerParams(vmem_limit_bytes=40 << 20),
        cost_estimate=pl.CostEstimate(flops=2 * rows * D * 2048, bytes_accessed=10 << 20, transcendentals=0),
        name="input_back",
    )(in_hbm(grad), low_grad, down, hidden, gain[None, :], in_hbm(middle_grad), *[in_hbm(block) for block in pieces.blocks])


VMEM_SPEC = pl.BlockSpec(memory_space=pltpu.VMEM)
SMEM_SPEC = pl.BlockSpec(memory_space=pltpu.SMEM)


def lane_pad(width):
    return -(-width // 128) * 128


def layout_of(shapes):
    places = []
    offset = 0
    for index, (rows, width) in enumerate(shapes):
        for part in range(rows // RANK):
            places.append((index, part, offset, width))
            offset += width
    return places, lane_pad(offset)


def pack_adapters(adapter_ids, members, devices):
    places, width = layout_of([member.shape[1:] for member in members])
    per_seq = devices // NSEQ
    turned = [member.shape[1] % (2 * RANK) != 0 and member.shape[1] > RANK for member in members]
    members = [jnp.swapaxes(member, 1, 2) if turn else member for member, turn in zip(members, turned)]

    def kernel(ids, *refs):
        sources, out, slab = refs[: len(members)], refs[len(members)], refs[len(members) + 1]
        slab[...] = jnp.zeros_like(slab)
        for index, part, offset, size in places:
            picked = ids[pl.program_id(0)]
            rank_rows = slice(RANK * part, RANK * (part + 1))
            if turned[index]:
                piece = sources[index][picked, :, rank_rows].astype(F32).T.astype(BF16)
            else:
                piece = sources[index][picked, rank_rows, :]
            slab[:, offset : offset + size] = piece
        for step in range(per_seq):
            out[step] = slab[...]

    return pl.pallas_call(
        kernel,
        grid=(NSEQ,),
        in_specs=[SMEM_SPEC] + [pl.BlockSpec(member.shape, lambda s: (0, 0, 0)) for member in members],
        out_specs=pl.BlockSpec((per_seq, RANK, width), lambda s: (s, 0, 0)),
        out_shape=jax.ShapeDtypeStruct((devices, RANK, width), BF16),
        scratch_shapes=[pltpu.VMEM((RANK, width), BF16)],
        name="pack_adapters",
    )(adapter_ids, *members)


def unpack_adapters(slabs, shapes):
    devices = slabs.shape[0]
    places, _ = layout_of(shapes)

    def kernel(source, *outs):
        for index, part, offset, size in places:
            for device in range(devices):
                outs[index][RANK * part : RANK * (part + 1), device * size : (device + 1) * size] = source[
                    device, :, offset : offset + size
                ]

    return pl.pallas_call(
        kernel,
        in_specs=[VMEM_SPEC],
        out_specs=[VMEM_SPEC] * len(shapes),
        out_shape=[jax.ShapeDtypeStruct((rows, width * devices), BF16) for rows, width in shapes],
        name="unpack_adapters",
    )(slabs)


def pack_grads(grads, devices):
    places, width = layout_of([(grad.shape[0], grad.shape[1] // devices) for grad in grads])

    def kernel(*refs):
        sources, out = refs[: len(grads)], refs[len(grads)]
        for device in range(devices):
            for index, part, offset, size in places:
                out[device, :, offset : offset + size] = sources[index][
                    RANK * part : RANK * (part + 1), device * size : (device + 1) * size
                ].astype(BF16)

    return pl.pallas_call(
        kernel,
        in_specs=[VMEM_SPEC] * len(grads),
        out_specs=VMEM_SPEC,
        out_shape=jax.ShapeDtypeStruct((devices, RANK, width), BF16),
        name="pack_grads",
    )(*grads)


def reduce_grads(adapter_ids, slabs, shapes):
    devices, _, width = slabs.shape
    places, _ = layout_of(shapes)
    per_seq = devices // NSEQ
    turned = [rows % (2 * RANK) != 0 and rows > RANK for rows, _ in shapes]

    def kernel(ids, source, *refs):
        outs, total = refs[: len(shapes)], refs[len(shapes)]
        total[...] = jnp.zeros_like(total)
        for seq in range(NSEQ):
            part_sum = jnp.sum(source[seq * per_seq : (seq + 1) * per_seq].astype(F32), axis=0)
            total[ids[seq]] += part_sum
        for index, part, offset, size in places:
            rank_rows = slice(RANK * part, RANK * (part + 1))
            if turned[index]:
                for adapter in range(ADAPTERS):
                    outs[index][adapter, :, rank_rows] = total[adapter, :, offset : offset + size].T
            else:
                outs[index][:, rank_rows, :] = total[:, :, offset : offset + size]

    sums = pl.pallas_call(
        kernel,
        in_specs=[SMEM_SPEC, VMEM_SPEC],
        out_specs=[VMEM_SPEC] * len(shapes),
        out_shape=[
            jax.ShapeDtypeStruct((ADAPTERS, *((size, rows) if turn else (rows, size))), F32)
            for (rows, size), turn in zip(shapes, turned)
        ],
        scratch_shapes=[pltpu.VMEM((ADAPTERS, RANK, width), F32)],
        name="reduce_grads",
    )(adapter_ids, slabs)
    return [jnp.swapaxes(value, 1, 2) if turn else value for value, turn in zip(sums, turned)]


def split_three(value):
    first = value.astype(BF16)
    rest = value - first.astype(F32)
    second = rest.astype(BF16)
    third = (rest - second.astype(F32)).astype(BF16)
    return first, second, third


def with_columns(block, columns, lanes):
    out = jnp.where(lanes < HEAD_DIM, block, jnp.zeros_like(block))
    for step, column in enumerate(columns):
        out = jnp.where(lanes == HEAD_DIM + step, column, out)
    return out


def stacked_heads(pair, lanes):
    return jnp.concatenate([pair, pltpu.roll(pair, HEAD_DIM, 1)], axis=0)


def allowed(start_row, key_base, query_base, diagonal):
    keys = key_base + lax.broadcasted_iota(jnp.int32, (BLOCK, BLOCK), 0)
    inside = keys >= start_row
    if diagonal:
        queries = query_base + lax.broadcasted_iota(jnp.int32, (BLOCK, BLOCK), 1)
        inside = inside & (keys <= queries)
    return jnp.concatenate([inside, inside], axis=1)


def forward_attention(bounds, starts, queries, keyvals, column):
    rows = queries.shape[0]
    length = keyvals.shape[0]
    halo = length - rows
    steps = rows // BLOCK

    def kernel(bound_ref, start_ref, query_ref, keyval_ref, out_ref, log_ref, key_scr, value_scr):
        step = pl.program_id(0)

        @pl.when(step == 0)
        def _():
            lanes = lax.broadcasted_iota(jnp.int32, (length, 128), 1)
            both = keyval_ref[...].astype(F32)
            key_scr[...] = jnp.where(lanes < HEAD_DIM, both, 0.0).astype(BF16)
            values = jnp.where(lanes < HEAD_DIM, pltpu.roll(both, HEAD_DIM, 1), 1.0)
            value_scr[...] = values.T.astype(BF16)

        lanes = lax.broadcasted_iota(jnp.int32, (BLOCK, 128), 1)
        pair = query_ref[...].astype(F32)
        query = stacked_heads(pair, lanes).astype(BF16)
        start_row = start_ref[...]
        diagonal = halo // BLOCK + step
        first = bound_ref[0, step]
        clear = jnp.minimum(bound_ref[1, step], diagonal)

        def block(index, total, masked, is_diagonal):
            base = pl.multiple_of(index * BLOCK, BLOCK)
            scores = contract_cols(key_scr[pl.ds(base, BLOCK), :], query)
            weights = jnp.exp2(scores)
            if masked:
                keep = allowed(start_row, base, diagonal * BLOCK, is_diagonal)
                weights = jnp.where(keep, weights, 0.0)
            return total + matmul(value_scr[:, pl.ds(base, BLOCK)], weights.astype(BF16))

        total = jnp.zeros((128, 2 * BLOCK), F32)
        total = lax.fori_loop(first, clear, lambda i, t: block(i, t, True, False), total)
        total = lax.fori_loop(clear, diagonal, lambda i, t: block(i, t, False, False), total)
        total = block(diagonal, total, True, True)
        norm = total[HEAD_DIM : HEAD_DIM + 1, :]
        mixed = total[:HEAD_DIM, :] / norm
        out_ref[...] = jnp.concatenate([mixed[:, :BLOCK], mixed[:, BLOCK:]], axis=0).T.astype(BF16)
        log_ref[0] = jnp.broadcast_to(jnp.log2(norm), (8, 2 * BLOCK))

    return pl.pallas_call(
        kernel,
        grid_spec=pltpu.PrefetchScalarGridSpec(
            num_scalar_prefetch=1,
            grid=(steps,),
            in_specs=[
                pl.BlockSpec((1, BLOCK), lambda i, b: (0, i)),
                pl.BlockSpec((BLOCK, 128), lambda i, b: (i, 0)),
                pl.BlockSpec((length, 128), lambda i, b: (0, column)),
            ],
            out_specs=[
                pl.BlockSpec((BLOCK, 128), lambda i, b: (i, 0)),
                pl.BlockSpec((1, 8, 2 * BLOCK), lambda i, b: (i, 0, 0)),
            ],
            scratch_shapes=[pltpu.VMEM((length, 128), BF16), pltpu.VMEM((128, length), BF16)],
        ),
        out_shape=[
            jax.ShapeDtypeStruct((rows, 128), BF16),
            jax.ShapeDtypeStruct((steps, 8, 2 * BLOCK), F32),
        ],
        compiler_params=pltpu.CompilerParams(vmem_limit_bytes=40 << 20),
        cost_estimate=pl.CostEstimate(
            flops=4 * rows * 1024 * 256 * 2, bytes_accessed=4 * rows * 256, transcendentals=rows * 2048
        ),
        name="forward_attention",
    )(bounds, starts, queries, keyvals)


def backward_attention(bounds, starts, queries, keyvals, column, mixed, logs, grads):
    rows = queries.shape[0]
    length = keyvals.shape[0]
    halo = length - rows
    steps = rows // BLOCK

    def kernel(bound_ref, start_ref, query_ref, keyval_ref, mixed_ref, log_ref, grad_ref, *refs):
        outs, (key_scr, value_scr, turned_scr, key_sum, value_sum) = refs[:-5], refs[-5:]
        step = pl.program_id(0)

        @pl.when(step == 0)
        def _():
            lanes = lax.broadcasted_iota(jnp.int32, (length, 128), 1)
            both = keyval_ref[...].astype(F32)
            ones = jnp.where(lanes < HEAD_DIM + 3, 1.0, 0.0)
            keys = jnp.where(lanes < HEAD_DIM, both, ones)
            key_scr[...] = keys.astype(BF16)
            value_scr[...] = jnp.where(lanes < HEAD_DIM, pltpu.roll(both, HEAD_DIM, 1), ones).astype(BF16)
            turned_scr[...] = keys.T.astype(BF16)
            key_sum[...] = jnp.zeros_like(key_sum)
            value_sum[...] = jnp.zeros_like(value_sum)

        lanes = lax.broadcasted_iota(jnp.int32, (2 * BLOCK, 128), 1)
        query = stacked_heads(query_ref[...].astype(F32), lanes)
        grad = stacked_heads(grad_ref[...].astype(F32), lanes)
        weighed = stacked_heads(mixed_ref[...].astype(F32), lanes)
        inner = jnp.sum(jnp.where(lanes < HEAD_DIM, grad * weighed, 0.0), axis=1, keepdims=True)
        log_column = log_ref[0].T[:, :1]
        query_low = with_columns(query, [part.astype(F32) for part in split_three(-log_column)], lanes).astype(BF16)
        grad_low = with_columns(grad, [part.astype(F32) for part in split_three(-inner)], lanes).astype(BF16)
        start_row = start_ref[...]
        diagonal = halo // BLOCK + step
        first = bound_ref[0, step]
        clear = jnp.minimum(bound_ref[1, step], diagonal)

        def block(index, total, masked, is_diagonal):
            base = pl.multiple_of(index * BLOCK, BLOCK)
            where = pl.ds(base, BLOCK)
            weights = jnp.exp2(contract_cols(key_scr[where, :], query_low))
            if masked:
                keep = allowed(start_row, base, diagonal * BLOCK, is_diagonal)
                weights = jnp.where(keep, weights, 0.0)
            slopes = (weights * contract_cols(value_scr[where, :], grad_low)).astype(BF16)
            value_sum[where, :] += matmul(weights.astype(BF16), grad_low)
            key_sum[where, :] += matmul(slopes, query_low)
            return total + matmul(turned_scr[:, where], slopes)

        total = jnp.zeros((128, 2 * BLOCK), F32)
        total = lax.fori_loop(first, clear, lambda i, t: block(i, t, True, False), total)
        total = lax.fori_loop(clear, diagonal, lambda i, t: block(i, t, False, False), total)
        total = block(diagonal, total, True, True)
        total = total[:HEAD_DIM] * HEAD_DIM**-0.5
        query_grad = jnp.concatenate([total[:, :BLOCK], total[:, BLOCK:]], axis=0).T.astype(BF16)
        if halo:
            outs[0][...] = query_grad
        else:
            outs[0][pl.ds(pl.multiple_of(step * BLOCK, BLOCK), BLOCK), :PAIR] = query_grad

        @pl.when(step == steps - 1)
        def _():
            whole = lax.broadcasted_iota(jnp.int32, (length, 128), 1)
            keyval_grad = jnp.where(
                whole < HEAD_DIM, key_sum[...] * (1.0 / LOG2E), pltpu.roll(value_sum[...], HEAD_DIM, 1)
            )
            if halo:
                outs[1][...] = keyval_grad
            else:
                outs[0][:, PAIR:] = keyval_grad.astype(BF16)

    return pl.pallas_call(
        kernel,
        grid_spec=pltpu.PrefetchScalarGridSpec(
            num_scalar_prefetch=1,
            grid=(steps,),
            in_specs=[
                pl.BlockSpec((1, BLOCK), lambda i, b: (0, i)),
                pl.BlockSpec((BLOCK, 128), lambda i, b: (i, 0)),
                pl.BlockSpec((length, 128), lambda i, b: (0, column)),
                pl.BlockSpec((BLOCK, 128), lambda i, b: (i, 0)),
                pl.BlockSpec((1, 8, 2 * BLOCK), lambda i, b: (i, 0, 0)),
                pl.BlockSpec((BLOCK, 128), lambda i, b: (i, 0)),
            ],
            out_specs=[
                pl.BlockSpec((BLOCK, 128), lambda i, b: (i, 0)),
                pl.BlockSpec((length, 128), lambda i, b: (0, 0)),
            ]
            if halo
            else [pl.BlockSpec((rows, 2 * PAIR), lambda i, b: (0, 0))],
            scratch_shapes=[
                pltpu.VMEM((length, 128), BF16),
                pltpu.VMEM((length, 128), BF16),
                pltpu.VMEM((128, length), BF16),
                pltpu.VMEM((length, 128), F32),
                pltpu.VMEM((length, 128), F32),
            ],
        ),
        out_shape=[jax.ShapeDtypeStruct((rows, 128), BF16), jax.ShapeDtypeStruct((length, 128), F32)]
        if halo
        else [jax.ShapeDtypeStruct((rows, 2 * PAIR), BF16)],
        compiler_params=pltpu.CompilerParams(vmem_limit_bytes=48 << 20),
        cost_estimate=pl.CostEstimate(
            flops=10 * rows * 1024 * 256 * 2, bytes_accessed=8 * rows * 256, transcendentals=rows * 2048
        ),
        name="backward_attention",
    )(bounds, starts, queries, keyvals, mixed, logs, grads)


def document_bounds(segment_ids, origin, halo, span, seq_start):
    tokens = segment_ids.shape[0]
    names = jnp.arange(tokens // (SEGMAX // 2), dtype=jnp.int32)
    begin = jnp.sum((segment_ids[None, :] < names[:, None]).astype(jnp.int32), axis=1)
    own = lax.dynamic_slice_in_dim(segment_ids, origin, span, 0)
    start = jnp.sum(jnp.where(own[None, :] == names[:, None], begin[:, None], 0), axis=0)
    start = jnp.maximum(start, seq_start) - (origin - halo)
    first = start[::BLOCK] // BLOCK
    clear = -(-start[BLOCK - 1 :: BLOCK] // BLOCK)
    bounds = jnp.stack([first, jnp.maximum(clear, first)])
    return bounds, start[None, :]


TILE = 512


def silu_parts(gate):
    share = 1.0 / (1.0 + jnp.exp(-gate))
    return share, gate * share


def feed_forward(mixed, hidden, cotangent, gain, weights, chosen):
    members, rows, _ = mixed.shape
    tiles = FF // TILE
    packed = isinstance(weights, Pieces)
    arrays = weights.blocks if packed else weights
    count = len(arrays)
    slices = 2 * FF // D

    def kernel(*refs):
        (
            mixed_ref, hidden_ref, cot_ref, gain_ref,
            out_down_ref, out_up_ref, mlp_down_ref, mlp_up_ref, ffd_down_ref, ffd_up_ref,
        ) = refs[:10]
        weight_refs = refs[10 : 10 + count]
        (
            output_ref, middle_grad_ref, mixed_grad_ref,
            out_down_grad, out_up_grad, mlp_down_grad, mlp_up_grad, ffd_down_grad, ffd_up_grad,
            wide_scr, down_scr, mix_scr, middle_scr, normed_scr, branch_scr, slope_scr,
            low_scr, low_turned, back_scr, back_turned, out_low_scr, down_sum, gate_sum, up_sum, sems,
        ) = refs[10 + count :]
        out_columns = slice(2 * FF, 2 * FF + D)

        def column_piece(piece):
            return slice(piece * D, (piece + 1) * D)

        if packed:
            blocks = weights.copies(weight_refs)
            devices = len(blocks)
            part, down_part = D // devices, FF // devices

            def start_piece(piece):
                for ref, source, where, size in blocks:
                    row = pl.multiple_of(where // size * part, 8)
                    pltpu.make_async_copy(
                        ref.at[pl.ds(source + piece * part, part), :],
                        wide_scr.at[pl.ds(row, part), column_piece(piece)],
                        sems.at[piece],
                    ).start()

            def start_down():
                for ref, source, where, size in blocks:
                    row = pl.multiple_of(where // size * down_part, 8)
                    pltpu.make_async_copy(
                        ref.at[pl.ds(source + (slices + 1) * part, down_part), :],
                        down_scr.at[pl.ds(row, down_part), :],
                        sems.at[slices + 1],
                    ).start()
        else:

            def start_piece(piece):
                columns = column_piece(piece)
                pltpu.make_async_copy(
                    weight_refs[0].at[:, columns], wide_scr.at[:, columns], sems.at[piece]
                ).start()

            def start_down():
                pltpu.make_async_copy(weight_refs[1], down_scr, sems.at[slices + 1]).start()

        def finish_piece(piece):
            region = wide_scr.at[:, column_piece(piece)]
            pltpu.make_async_copy(region, region, sems.at[piece]).wait()

        per_piece = D // TILE
        first_use = {}
        for piece in range(slices):
            uses = [c // TILE % tiles for c in range(piece * D, (piece + 1) * D, TILE)]
            first_use.setdefault(min(uses), []).append(piece)
        start_piece(slices)
        for piece in first_use[0]:
            start_piece(piece)
        start_down()

        cot = cot_ref[...]
        for member in range(members):
            mix_scr[:, member * PAIR : (member + 1) * PAIR] = mixed_ref[member]
        out_low = contract_cols(mix_scr[...], out_down_ref[...]).astype(BF16)
        out_low_scr[...] = out_low
        back = contract_cols(cot, ffd_up_ref[...])
        back_scr[...] = back.astype(BF16)
        back_turned[...] = back.T.astype(BF16)
        branch_scr[...] = jnp.zeros_like(branch_scr)
        slope_scr[...] = jnp.zeros_like(slope_scr)
        down_sum[...] = jnp.zeros_like(down_sum)
        gate_sum[...] = jnp.zeros_like(gate_sum)
        up_sum[...] = jnp.zeros_like(up_sum)
        finish_piece(slices)
        middle = (
            hidden_ref[...].astype(F32)
            + matmul(mix_scr[...], wide_scr[:, out_columns])
            + matmul(out_low, out_up_ref[...])
        )
        middle_scr[...] = middle
        normed = (middle * row_scale(middle) * gain_ref[...]).astype(BF16)
        normed_scr[...] = normed
        low = contract_cols(normed, mlp_down_ref[...])
        low_scr[...] = low.astype(BF16)
        low_turned[...] = low.T.astype(BF16)
        pltpu.make_async_copy(down_scr, down_scr, sems.at[slices + 1]).wait()

        def tile(index, carry):
            base = pl.multiple_of(index * TILE, TILE)
            gate_at, up_at = pl.ds(base, TILE), pl.ds(base + FF, TILE)
            for use, group in sorted(first_use.items()):

                @pl.when(index == use)
                def _(group=group):
                    for piece in group:
                        finish_piece(piece)

                if use > 0:

                    @pl.when(index == max(use - per_piece, 0))
                    def _(group=group):
                        for piece in group:
                            start_piece(piece)

            normed = normed_scr[...]
            low = low_scr[...]
            gate = matmul(normed, wide_scr[:, gate_at]) + matmul(low[:, :RANK], mlp_up_ref[:, gate_at])
            up = matmul(normed, wide_scr[:, up_at]) + matmul(low[:, RANK:], mlp_up_ref[:, up_at])
            share, active = silu_parts(gate)
            units = (active * up).astype(BF16)
            down = down_scr[gate_at, :]
            branch_scr[...] += matmul(units, down)
            down_sum[...] += contract_cols(units, ffd_down_ref[:, gate_at])
            ffd_down_grad[:, gate_at] = matmul(back_turned[...], units)
            units_grad = contract_cols(cot_ref[...], down) + matmul(back_scr[...], ffd_down_ref[:, gate_at])
            gate_grad = (units_grad * up * (share * (1.0 + gate * (1.0 - share)))).astype(BF16)
            up_grad = (units_grad * active).astype(BF16)
            slope_scr[...] += contract_cols(gate_grad, wide_scr[:, gate_at]) + contract_cols(
                up_grad, wide_scr[:, up_at]
            )
            gate_sum[...] += contract_cols(gate_grad, mlp_up_ref[:, gate_at])
            up_sum[...] += contract_cols(up_grad, mlp_up_ref[:, up_at])
            mlp_up_grad[:, gate_at] = matmul(low_turned[:RANK, :], gate_grad)
            mlp_up_grad[:, up_at] = matmul(low_turned[RANK:, :], up_grad)
            return carry

        lax.fori_loop(0, tiles, tile, 0)

        middle = middle_scr[...]
        cot = cot_ref[...]
        down_low = down_sum[...].astype(BF16)
        output_ref[...] = (middle + branch_scr[...] + matmul(down_low, ffd_up_ref[...])).astype(BF16)
        ffd_up_grad[...] = contract_rows(down_low, cot)
        low_grad = jnp.concatenate([gate_sum[...], up_sum[...]], axis=1).astype(BF16)
        mlp_down_grad[...] = contract_rows(low_grad, normed_scr[...])
        slope = gain_ref[...] * (slope_scr[...] + matmul(low_grad, mlp_down_ref[...]))
        scale = row_scale(middle)
        inner = jnp.mean(slope * middle, axis=1, keepdims=True)
        middle_grad = cot.astype(F32) + scale * slope - middle * (scale * scale * scale * inner)
        middle_grad_ref[...] = middle_grad
        branch_grad = middle_grad.astype(BF16)
        out_up_grad[...] = contract_rows(out_low_scr[...], branch_grad)
        out_low_grad = contract_cols(branch_grad, out_up_ref[...]).astype(BF16)
        out_down_grad[...] = contract_rows(out_low_grad, mix_scr[...])
        mixed_grad = contract_cols(branch_grad, wide_scr[:, out_columns]) + matmul(out_low_grad, out_down_ref[...])
        for member in range(members):
            mixed_grad_ref[member] = mixed_grad[:, member * PAIR : (member + 1) * PAIR].astype(BF16)

    results = pl.pallas_call(
        kernel,
        in_specs=[VMEM_SPEC] * 10 + [ANY_SPEC] * count,
        out_specs=[VMEM_SPEC] * 9,
        out_shape=[
            jax.ShapeDtypeStruct((rows, D), BF16),
            jax.ShapeDtypeStruct((rows, D), F32),
            jax.ShapeDtypeStruct((members, rows, PAIR), BF16),
            jax.ShapeDtypeStruct((RANK, QW), F32),
            jax.ShapeDtypeStruct((RANK, D), F32),
            jax.ShapeDtypeStruct((2 * RANK, D), F32),
            jax.ShapeDtypeStruct((RANK, 2 * FF), F32),
            jax.ShapeDtypeStruct((RANK, FF), F32),
            jax.ShapeDtypeStruct((RANK, D), F32),
        ],
        scratch_shapes=[
            pltpu.VMEM((D, 2 * FF + D), BF16), pltpu.VMEM((FF, D), BF16),
            pltpu.VMEM((rows, QW), BF16), pltpu.VMEM((rows, D), F32), pltpu.VMEM((rows, D), BF16),
            pltpu.VMEM((rows, D), F32), pltpu.VMEM((rows, D), F32),
            pltpu.VMEM((rows, 2 * RANK), BF16), pltpu.VMEM((2 * RANK, rows), BF16),
            pltpu.VMEM((rows, RANK), BF16), pltpu.VMEM((RANK, rows), BF16), pltpu.VMEM((rows, RANK), BF16),
            pltpu.VMEM((rows, RANK), F32), pltpu.VMEM((rows, RANK), F32), pltpu.VMEM((rows, RANK), F32),
            pltpu.SemaphoreType.DMA((2 + slices,)),
        ],
        compiler_params=pltpu.CompilerParams(vmem_limit_bytes=60 << 20),
        cost_estimate=pl.CostEstimate(
            flops=rows * (12 * D * FF + 4 * D * QW), bytes_accessed=6 * D * FF + 16 * rows * D,
            transcendentals=rows * FF,
        ),
        name="feed_forward",
    )(mixed, hidden, cotangent, gain[None, :], *chosen, *arrays)
    return results[0], results[1], results[2], list(results[3:])


def local(
    hidden, cotangent, segment_ids, adapter_ids, attn_gain, query_gain, key_gain, ffn_gain,
    qkv_weight, out_weight, gate_up_weight, down_weight, *adapters,
):
    rows = hidden.shape[0]
    devices = lax.axis_size("ctx") * lax.axis_size("head")
    members = KV_HEADS
    groups = [[members * g + i for i in range(members)] for g in range(devices // members)]
    span = rows * members
    seq_length = rows * devices // NSEQ
    halo = 0 if span == seq_length else SEGMAX
    here = lax.axis_index("ctx") * lax.axis_size("head") + lax.axis_index("head")
    origin = here // members * span
    seq_start = origin // seq_length * seq_length
    positions = here * rows - seq_start + jnp.arange(rows, dtype=jnp.int32)
    bounds, starts = document_bounds(segment_ids, origin, halo, span, seq_start)

    def swap(value):
        return lax.all_to_all(value, AXES, 0, 0, axis_index_groups=groups, tiled=True)

    def shifted(value, by):
        pairs = [(i, i + by) for i in range(devices) if 0 <= i + by < devices]
        return lax.ppermute(value, AXES, pairs)

    def gather(value):
        return lax.all_gather(value, AXES, axis=0, tiled=True)

    shapes = [member.shape[1:] for member in adapters]
    def exchange(packed):
        return lax.all_to_all(packed, AXES, 0, 0, tiled=True)

    spread = by_axes()
    if spread:
        found = {(0, 0): stack_shard(gate_up_weight, out_weight, down_weight)}
        pending = []

        def move(*keys, extra=()):
            hops = [(found[key[0] ^ key[2], key[1] - key[3]], key[2], key[3]) for key in keys]
            hops += extra
            held = lax.optimization_barrier((*[value for value, _, _ in hops], *pending))
            results = [hop(value, flip, step) for value, (_, flip, step) in zip(held, hops)]
            found.update(zip([key[:2] for key in keys], results))
            pending[:] = results
            return results[len(keys) :]

        def cores(*keys):
            return [(flip, step, 1, 0) for flip, step in keys]

        def then(value):
            return lax.optimization_barrier((value, *pending))[0]

        line = move((2, 0, 2, 0), (4, 0, 4, 0), extra=[(qkv_weight, 0, step) for step in range(1, 4)])
        slabs = exchange(lax.optimization_barrier((pack_adapters(adapter_ids, adapters[:2], devices), *line))[0])
        line = jnp.concatenate([qkv_weight] + line, axis=0)
        plane = move((0, 1, 0, 1), extra=[(line, flip, 0) for flip in (2, 4, 6)])
        pending.append(slabs)
        plane = jnp.concatenate([line] + plane, axis=0)
        (across,) = move((0, 2, 0, 1), (2, 1, 2, 0), (6, 0, 4, 0), extra=[(plane, 1, 0)])
        qkv = Pieces([((0, (0, 1, 2, 3)), plane), ((1, (0, 1, 2, 3)), across)], D)
        hidden_then = hidden
    else:
        qkv = whole_gather(qkv_weight)
        weights = [gather(jnp.concatenate([gate_up_weight, out_weight], axis=1)), gather(down_weight)]
        hidden_then = hidden
        slabs = exchange(pack_adapters(adapter_ids, adapters[:2], devices))
    chosen = list(unpack_adapters(slabs, shapes[:2]))

    head_gain = jnp.stack([jnp.tile(query_gain, 2), jnp.tile(key_gain, 2)])
    tables = rope_tables(positions)
    sent, low_qkv, kept = project_heads(hidden_then, attn_gain, head_gain, tables, qkv, chosen[0], chosen[1])
    if spread:
        sent = then(sent)
    queries = swap(sent).reshape(span, 2 * PAIR)
    keyvals, column = queries, 1
    if halo:
        keyvals, column = queries[:, PAIR:], 0
        keyvals = jnp.concatenate([shifted(keyvals[span - halo :], members), keyvals], axis=0)
    if spread:
        move((2, 2, 2, 0), (4, 1, 4, 0), *cores((1, 0)))
        first = pending[:]
        move((0, 3, 0, 1))
        pending[:] = first
        late_adapters = then(adapters[2])
        move((6, 1, 2, 0), (4, 2, 4, 0), *cores((1, 1), (3, 0)))
        keyvals = queries = then(queries)
        move((2, 3, 2, 0), (4, 3, 4, 0), *cores((5, 0), (7, 0), (1, 2)))
    else:
        late_adapters = adapters[2]
    packed = pack_adapters(adapter_ids, (late_adapters, *adapters[3:]), devices)
    slabs = exchange(lax.optimization_barrier((packed, queries))[0])
    mixed, logs = forward_attention(bounds, starts, queries, keyvals, column)
    chosen += list(unpack_adapters(slabs, shapes[2:]))
    if spread:
        pending.append(logs)
        move((6, 3, 2, 0), (6, 2, 4, 0), *cores((3, 1), (5, 1), (3, 2)))
    mixed_then = lax.optimization_barrier((mixed, slabs))[0]
    mixture_tok = swap(mixed_then.reshape(members, rows, PAIR))
    if spread:
        move(*cores((5, 2), (7, 1), (1, 3), (3, 3), (5, 3)))
        pending.append(mixture_tok)
        move(*cores((7, 2), (7, 3)))
        weights = Pieces([((flip, (step,)), block) for (flip, step), block in found.items()], D)
    output, middle_grad, mixture_grad, early = feed_forward(
        mixture_tok, hidden, cotangent, ffn_gain, weights, chosen[2:]
    )
    grad_rows = swap(mixture_grad).reshape(span, PAIR)
    early_packed, grad_rows = lax.optimization_barrier((pack_grads(early, devices), grad_rows))
    early_slabs = exchange(early_packed)
    back = backward_attention(bounds, starts, queries, keyvals, column, mixed, logs, grad_rows)
    if halo:
        query_grads, keyval_grads = back
        returned = shifted(keyval_grads[:halo].astype(BF16), -members).astype(F32)
        keyval_grads = jnp.concatenate([keyval_grads[halo:span], keyval_grads[span:] + returned], axis=0)
        back = [jnp.concatenate([query_grads, keyval_grads.astype(BF16)], axis=1)]
    back, early_slabs = lax.optimization_barrier((back[0], early_slabs))
    early_owned = reduce_grads(adapter_ids, early_slabs, shapes[2:])
    back = back.reshape(members, rows, 2 * PAIR)
    arrived_back = swap(back)
    projected_grad, low_grad, packed = project_back(
        arrived_back, kept, head_gain, tables, hidden, attn_gain, low_qkv, chosen[1], devices
    )
    late_slabs = exchange(packed)
    late_owned = reduce_grads(adapter_ids, late_slabs, shapes[:2])
    input_grad = input_back(projected_grad, low_grad, qkv, chosen[0], hidden, attn_gain, middle_grad)
    return (output, input_grad, *late_owned, *early_owned)


def solution(mesh):
    by_rows = P(AXES, None)
    by_cols = P(None, None, AXES)
    placed = (by_rows, by_rows) + (P(),) * 6 + (by_rows,) * 4 + (by_cols,) * 8
    return jax.shard_map(
        local,
        mesh=mesh,
        in_specs=placed,
        out_specs=(by_rows, by_rows) + (by_cols,) * 8,
        check_vma=False,
    )
```

```python
import functools
import math

import jax
import jax.numpy as jnp
from jax import lax
from jax.experimental import pallas as pl
from jax.experimental.pallas import tpu as pltpu
from jax.sharding import PartitionSpec as P

D = 1024
HEADS = 16
KV_HEADS = 8
HEAD_DIM = 64
FF = 4608
RANK = 16
ADAPTERS = 8
NSEQ = 4
SEGMAX = 2048
QW = 1024
KW = 512
PAIR = 2 * HEAD_DIM
BLOCK = 256
AXES = ("ctx", "head")

epsilon = 1e-05
rope_base = 1000000.0
LOG2E = math.log2(math.e)
QSCALE = HEAD_DIM**-0.5 * LOG2E
F32 = jnp.float32
BF16 = jnp.bfloat16


def matmul(left_side, right_side):
    return jnp.dot(left_side, right_side, preferred_element_type=F32)


def contract_rows(left_side, right_side):
    return lax.dot_general(left_side, right_side, (((0,), (0,)), ((), ())), preferred_element_type=F32)


def contract_cols(left_side, right_side):
    return lax.dot_general(left_side, right_side, (((1,), (1,)), ((), ())), preferred_element_type=F32)


def rope_tables(positions):
    middle = HEAD_DIM // 2
    frequency = jnp.power(rope_base, -(2.0 / HEAD_DIM) * jnp.arange(middle, dtype=F32))
    angles = positions.astype(F32)[:, None] * frequency[None, :]
    cosine, sine = jnp.cos(angles), jnp.sin(angles)
    return jnp.concatenate([cosine] * 4, axis=1), jnp.concatenate([-sine, sine] * 2, axis=1)


ANY_SPEC = pl.BlockSpec(memory_space=pl.ANY)


class Pieces:
    def __init__(self, blocks, rows):
        self.keys = [key for key, _ in blocks]
        self.blocks = [block for _, block in blocks]
        self.rows = rows

    def offsets(self):
        if self.keys[0] is None:
            return [(0, 0, self.rows)]
        depth = lax.axis_size("head")
        ctx, head = lax.axis_index("ctx"), lax.axis_index("head")
        found = []
        for flip, steps in self.keys:
            flips = [flip] if len(steps) == 1 else [flip ^ other for other in (0, 2, 4, 6)]
            size = self.blocks[0].shape[0] // (len(steps) * len(flips))
            for place, (flip, step) in enumerate([(flip, step) for flip in flips for step in steps]):
                device = jnp.bitwise_xor(ctx, flip) * depth + lax.rem(head - step + depth, depth)
                found.append((place * size, pl.multiple_of(device * size, 8), size))
        return found

    def copies(self, refs):
        found, offsets = [], self.offsets()
        share = len(offsets) // len(refs)
        for place, (source, target, size) in enumerate(offsets):
            found.append((refs[place // share], source, target, size))
        return found


def by_axes():
    return lax.axis_size("ctx") == 8 and lax.axis_size("head") == 4


def hop(value, flip, step):
    depth = lax.axis_size("head")
    pairs = [
        (ctx * depth + head, (ctx ^ flip) * depth + (head + step) % depth)
        for ctx in range(lax.axis_size("ctx"))
        for head in range(depth)
    ]
    return lax.ppermute(value, AXES, pairs)


def stack_shard(gate_up_weight, out_weight, down_weight):
    part, down_part = out_weight.shape[0], down_weight.shape[0]
    slices = 2 * FF // D

    def kernel(wide_ref, out_ref, down_ref, stacked_ref):
        for piece in range(slices):
            stacked_ref[piece * part : (piece + 1) * part, :] = wide_ref[:, piece * D : (piece + 1) * D]
        stacked_ref[slices * part : (slices + 1) * part, :] = out_ref[...]
        stacked_ref[(slices + 1) * part :, :] = down_ref[...]

    return pl.pallas_call(
        kernel,
        in_specs=[VMEM_SPEC] * 3,
        out_specs=VMEM_SPEC,
        out_shape=jax.ShapeDtypeStruct(((slices + 1) * part + down_part, D), BF16),
        name="stack_shard",
    )(gate_up_weight, out_weight, down_weight)


def whole_gather(value):
    full = lax.all_gather(value, AXES, axis=0, tiled=True)
    return Pieces([(None, full)], full.shape[0])


def start_loads(pieces, refs, target, sem):
    for ref, source, where, size in pieces.copies(refs):
        pltpu.make_async_copy(ref.at[pl.ds(source, size), :], target.at[pl.ds(where, size), :], sem).start()


def finish_loads(target, sem, columns=None):
    region = target if columns is None else target.at[:, columns]
    pltpu.make_async_copy(region, region, sem).wait()


def head_means(values, ones):
    return matmul(values.astype(BF16), ones) * (1.0 / HEAD_DIM)


def head_ones():
    row = lax.broadcasted_iota(jnp.int32, (PAIR, PAIR), 0) // HEAD_DIM
    col = lax.broadcasted_iota(jnp.int32, (PAIR, PAIR), 1) // HEAD_DIM
    return jnp.where(row == col, 1.0, 0.0).astype(BF16)


def swapped_halves(values):
    lanes = lax.broadcasted_iota(jnp.int32, values.shape, 1)
    half = HEAD_DIM // 2
    return jnp.where(lanes % HEAD_DIM < half, pltpu.roll(values, PAIR - half, 1), pltpu.roll(values, half, 1))


def row_scale(values):
    return lax.rsqrt(jnp.mean(values * values, axis=1, keepdims=True) + epsilon)


ROWS = 256


def in_hbm(value):
    return pltpu.with_memory_space_constraint(value, pltpu.HBM)


def row_block(width):
    return pl.BlockSpec((ROWS, width), lambda i: (i, 0))


def fixed(shape):
    return pl.BlockSpec(shape, lambda i: (0,) * len(shape))


def project_heads(hidden, gain, head_gain, tables, pieces, down, up):
    rows = hidden.shape[0]
    count = len(pieces.blocks)
    width = QW + 2 * KW

    def kernel(*refs):
        hidden_ref, gain_ref, head_gain_ref, cos_ref, sin_ref, down_ref, up_ref = refs[:7]
        blocks = refs[7 : 7 + count]
        sent_ref, low_ref, kept_ref, weight, sem = refs[7 + count :]

        @pl.when(pl.program_id(0) == 0)
        def _():
            start_loads(pieces, blocks, weight, sem)

        inputs = hidden_ref[...].astype(F32)
        normed = (inputs * row_scale(inputs) * gain_ref[...]).astype(BF16)
        low = contract_cols(normed, down_ref[...]).astype(BF16)
        low_ref[...] = low
        ones = head_ones()
        cos, sin = cos_ref[...], sin_ref[...]
        lanes = lax.broadcasted_iota(jnp.int32, (ROWS, PAIR), 1)

        @pl.when(pl.program_id(0) == 0)
        def _():
            finish_loads(weight, sem)

        def columns(start, size, group):
            return matmul(normed, weight[:, start : start + size]) + matmul(
                low[:, RANK * group : RANK * (group + 1)], up_ref[:, start : start + size]
            )

        def turned(values, gains):
            unit = values * lax.rsqrt(head_means(values * values, ones) + epsilon) * gains
            return unit * cos + swapped_halves(unit) * sin

        step = 4 * PAIR
        for start in range(0, QW, step):
            some = columns(start, step, 0)
            kept_ref[:, start : start + step] = some.astype(BF16)
            for side in range(step // PAIR):
                query = turned(some[:, side * PAIR : (side + 1) * PAIR], head_gain_ref[0:1, :]) * QSCALE
                sent_ref[start // PAIR + side, :, :PAIR] = query.astype(BF16)
        for start in range(0, KW, step):
            some = columns(QW + start, step, 1)
            values = columns(QW + KW + start, step, 2)
            kept_ref[:, QW + start : QW + start + step] = some.astype(BF16)
            for side in range(step // PAIR):
                where = slice(side * PAIR, (side + 1) * PAIR)
                key = turned(some[:, where], head_gain_ref[1:2, :])
                value = values[:, where]
                group = (start + side * PAIR) // HEAD_DIM
                sent_ref[group, :, PAIR:] = jnp.where(
                    lanes < HEAD_DIM, key, pltpu.roll(value, HEAD_DIM, 1)
                ).astype(BF16)
                sent_ref[group + 1, :, PAIR:] = jnp.where(
                    lanes < HEAD_DIM, pltpu.roll(key, HEAD_DIM, 1), value
                ).astype(BF16)

    return pl.pallas_call(
        kernel,
        grid=(rows // ROWS,),
        in_specs=[
            row_block(D), fixed((1, D)), fixed((2, PAIR)), row_block(PAIR), row_block(PAIR),
            fixed((3 * RANK, D)), fixed((RANK, width)),
        ]
        + [ANY_SPEC] * count,
        out_specs=[
            pl.BlockSpec((KV_HEADS, ROWS, 2 * PAIR), lambda i: (0, i, 0)), row_block(3 * RANK), row_block(QW + KW),
        ],
        out_shape=[
            jax.ShapeDtypeStruct((KV_HEADS, rows, 2 * PAIR), BF16),
            jax.ShapeDtypeStruct((rows, 3 * RANK), BF16),
            jax.ShapeDtypeStruct((rows, QW + KW), BF16),
        ],
        scratch_shapes=[pltpu.VMEM((D, width), BF16), pltpu.SemaphoreType.DMA],
        compiler_params=pltpu.CompilerParams(vmem_limit_bytes=60 << 20),
        cost_estimate=pl.CostEstimate(flops=2 * rows * D * width, bytes_accessed=10 << 20, transcendentals=0),
        name="project_heads",
    )(hidden, gain[None, :], head_gain, *tables, down, up, *pieces.blocks)


def project_back(back, kept, head_gain, tables, hidden, gain, low, up, devices):
    rows = hidden.shape[0]
    width = QW + 2 * KW
    places, slab = layout_of([(3 * RANK, D // devices), (RANK, width // devices)])

    def kernel(
        back_ref, kept_ref, head_gain_ref, cos_ref, sin_ref, hidden_ref, gain_ref, low_ref, up_ref,
        grad_ref, low_grad_ref, packed_ref, down_sum, up_sum,
    ):
        ones = head_ones()
        cos, sin = cos_ref[...], sin_ref[...]
        lanes = lax.broadcasted_iota(jnp.int32, (ROWS, PAIR), 1)

        @pl.when(pl.program_id(0) == 0)
        def _():
            down_sum[...] = jnp.zeros_like(down_sum)
            up_sum[...] = jnp.zeros_like(up_sum)

        def through(grads, values, gains):
            slope = (grads * cos - swapped_halves(grads) * sin) * gains
            scale = lax.rsqrt(head_means(values * values, ones) + epsilon)
            unit = values * scale
            return scale * (slope - unit * head_means(slope * unit, ones))

        for group in range(KV_HEADS):
            where = slice(group * PAIR, (group + 1) * PAIR)
            grads = back_ref[group, :, :PAIR].astype(F32)
            grad_ref[:, where] = through(grads, kept_ref[:, where].astype(F32), head_gain_ref[0:1, :]).astype(BF16)
        for group in range(0, KV_HEADS, 2):
            even = back_ref[group, :, PAIR:].astype(F32)
            odd = back_ref[group + 1, :, PAIR:].astype(F32)
            keys = jnp.where(lanes < HEAD_DIM, even, pltpu.roll(odd, HEAD_DIM, 1))
            values = jnp.where(lanes < HEAD_DIM, pltpu.roll(even, HEAD_DIM, 1), odd)
            start = QW + group * HEAD_DIM
            where = slice(start, start + PAIR)
            grad_ref[:, where] = through(keys, kept_ref[:, where].astype(F32), head_gain_ref[1:2, :]).astype(BF16)
            grad_ref[:, start + KW : start + KW + PAIR] = values.astype(BF16)
        turned = low_ref[...].astype(F32).T.astype(BF16)
        edges = (0, QW, QW + KW, width)
        parts = []
        for group in range(3):
            where = slice(edges[group], edges[group + 1])
            grads = grad_ref[:, where]
            up_sum[:, where] += matmul(turned[RANK * group : RANK * (group + 1), :], grads)
            parts.append(contract_cols(grads, up_ref[:, where]))
        low_grad = jnp.concatenate(parts, axis=1)
        low_grad_ref[...] = low_grad.astype(BF16)
        inputs = hidden_ref[...].astype(F32)
        normed = (inputs * row_scale(inputs) * gain_ref[...]).astype(BF16)
        down_sum[...] += matmul(low_grad.T.astype(BF16), normed)

        @pl.when(pl.program_id(0) == rows // ROWS - 1)
        def _():
            for device in range(devices):
                for index, part, offset, size in places:
                    packed_ref[device, :, offset : offset + size] = (down_sum, up_sum)[index][
                        RANK * part : RANK * (part + 1), device * size : (device + 1) * size
                    ].astype(BF16)

    return pl.pallas_call(
        kernel,
        grid=(rows // ROWS,),
        in_specs=[
            pl.BlockSpec((KV_HEADS, ROWS, 2 * PAIR), lambda i: (0, i, 0)), row_block(QW + KW), fixed((2, PAIR)),
            row_block(PAIR), row_block(PAIR), row_block(D), fixed((1, D)), row_block(3 * RANK), fixed((RANK, width)),
        ],
        out_specs=[row_block(width), row_block(3 * RANK), fixed((devices, RANK, slab))],
        out_shape=[
            jax.ShapeDtypeStruct((rows, width), BF16),
            jax.ShapeDtypeStruct((rows, 3 * RANK), BF16),
            jax.ShapeDtypeStruct((devices, RANK, slab), BF16),
        ],
        scratch_shapes=[pltpu.VMEM((3 * RANK, D), F32), pltpu.VMEM((RANK, width), F32)],
        compiler_params=pltpu.CompilerParams(vmem_limit_bytes=60 << 20),
        name="project_back",
    )(back, in_hbm(kept), head_gain, *[in_hbm(table) for table in tables], hidden, gain[None, :], in_hbm(low), up)


def input_back(grad, low_grad, pieces, down, hidden, gain, middle_grad):
    rows = hidden.shape[0]
    count = len(pieces.blocks)

    def kernel(*refs):
        grad_ref, low_ref, down_ref, hidden_ref, gain_ref, middle_ref = refs[:6]
        blocks = refs[6 : 6 + count]
        out_ref, weight, sem = refs[6 + count :]

        @pl.when(pl.program_id(0) == 0)
        def _():
            start_loads(pieces, blocks, weight, sem)

        inputs = hidden_ref[...].astype(F32)
        scale = row_scale(inputs)

        @pl.when(pl.program_id(0) == 0)
        def _():
            finish_loads(weight, sem)

        slope = matmul(low_ref[...], down_ref[...]) + contract_cols(grad_ref[...], weight[...])
        slope = slope * gain_ref[...]
        unit = inputs * scale
        inner = jnp.mean(slope * unit, axis=1, keepdims=True)
        out_ref[...] = middle_ref[...] + scale * (slope - unit * inner)

    return pl.pallas_call(
        kernel,
        grid=(rows // ROWS,),
        in_specs=[
            row_block(QW + 2 * KW), row_block(3 * RANK), fixed((3 * RANK, D)), row_block(D), fixed((1, D)), row_block(D),
        ]
        + [ANY_SPEC] * count,
        out_specs=row_block(D),
        out_shape=jax.ShapeDtypeStruct((rows, D), F32),
        scratch_shapes=[pltpu.VMEM((D, QW + 2 * KW), BF16), pltpu.SemaphoreType.DMA],
        compiler_params=pltpu.CompilerParams(vmem_limit_bytes=60 << 20),
        cost_estimate=pl.CostEstimate(flops=2 * rows * D * 2048, bytes_accessed=10 << 20, transcendentals=0),
        name="input_back",
    )(in_hbm(grad), low_grad, down, hidden, gain[None, :], in_hbm(middle_grad), *[in_hbm(block) for block in pieces.blocks])


VMEM_SPEC = pl.BlockSpec(memory_space=pltpu.VMEM)
SMEM_SPEC = pl.BlockSpec(memory_space=pltpu.SMEM)


def lane_pad(width):
    return -(-width // 128) * 128


def layout_of(shapes):
    places = []
    offset = 0
    for index, (rows, width) in enumerate(shapes):
        for part in range(rows // RANK):
            places.append((index, part, offset, width))
            offset += width
    return places, lane_pad(offset)


def pack_adapters(adapter_ids, members, devices):
    places, width = layout_of([member.shape[1:] for member in members])
    per_seq = devices // NSEQ
    turned = [member.shape[1] % (2 * RANK) != 0 and member.shape[1] > RANK for member in members]
    members = [jnp.swapaxes(member, 1, 2) if turn else member for member, turn in zip(members, turned)]

    def kernel(ids, *refs):
        sources, out, slab = refs[: len(members)], refs[len(members)], refs[len(members) + 1]
        slab[...] = jnp.zeros_like(slab)
        for index, part, offset, size in places:
            picked = ids[pl.program_id(0)]
            rank_rows = slice(RANK * part, RANK * (part + 1))
            if turned[index]:
                piece = sources[index][picked, :, rank_rows].astype(F32).T.astype(BF16)
            else:
                piece = sources[index][picked, rank_rows, :]
            slab[:, offset : offset + size] = piece
        for step in range(per_seq):
            out[step] = slab[...]

    return pl.pallas_call(
        kernel,
        grid=(NSEQ,),
        in_specs=[SMEM_SPEC] + [pl.BlockSpec(member.shape, lambda s: (0, 0, 0)) for member in members],
        out_specs=pl.BlockSpec((per_seq, RANK, width), lambda s: (s, 0, 0)),
        out_shape=jax.ShapeDtypeStruct((devices, RANK, width), BF16),
        scratch_shapes=[pltpu.VMEM((RANK, width), BF16)],
        name="pack_adapters",
    )(adapter_ids, *members)


def unpack_adapters(slabs, shapes):
    devices = slabs.shape[0]
    places, _ = layout_of(shapes)

    def kernel(source, *outs):
        for index, part, offset, size in places:
            for device in range(devices):
                outs[index][RANK * part : RANK * (part + 1), device * size : (device + 1) * size] = source[
                    device, :, offset : offset + size
                ]

    return pl.pallas_call(
        kernel,
        in_specs=[VMEM_SPEC],
        out_specs=[VMEM_SPEC] * len(shapes),
        out_shape=[jax.ShapeDtypeStruct((rows, width * devices), BF16) for rows, width in shapes],
        name="unpack_adapters",
    )(slabs)


def pack_grads(grads, devices):
    places, width = layout_of([(grad.shape[0], grad.shape[1] // devices) for grad in grads])

    def kernel(*refs):
        sources, out = refs[: len(grads)], refs[len(grads)]
        for device in range(devices):
            for index, part, offset, size in places:
                out[device, :, offset : offset + size] = sources[index][
                    RANK * part : RANK * (part + 1), device * size : (device + 1) * size
                ].astype(BF16)

    return pl.pallas_call(
        kernel,
        in_specs=[VMEM_SPEC] * len(grads),
        out_specs=VMEM_SPEC,
        out_shape=jax.ShapeDtypeStruct((devices, RANK, width), BF16),
        name="pack_grads",
    )(*grads)


def reduce_grads(adapter_ids, slabs, shapes):
    devices, _, width = slabs.shape
    places, _ = layout_of(shapes)
    per_seq = devices // NSEQ
    turned = [rows % (2 * RANK) != 0 and rows > RANK for rows, _ in shapes]

    def kernel(ids, source, *refs):
        outs, total = refs[: len(shapes)], refs[len(shapes)]
        total[...] = jnp.zeros_like(total)
        for seq in range(NSEQ):
            part_sum = jnp.sum(source[seq * per_seq : (seq + 1) * per_seq].astype(F32), axis=0)
            total[ids[seq]] += part_sum
        for index, part, offset, size in places:
            rank_rows = slice(RANK * part, RANK * (part + 1))
            if turned[index]:
                for adapter in range(ADAPTERS):
                    outs[index][adapter, :, rank_rows] = total[adapter, :, offset : offset + size].T
            else:
                outs[index][:, rank_rows, :] = total[:, :, offset : offset + size]

    sums = pl.pallas_call(
        kernel,
        in_specs=[SMEM_SPEC, VMEM_SPEC],
        out_specs=[VMEM_SPEC] * len(shapes),
        out_shape=[
            jax.ShapeDtypeStruct((ADAPTERS, *((size, rows) if turn else (rows, size))), F32)
            for (rows, size), turn in zip(shapes, turned)
        ],
        scratch_shapes=[pltpu.VMEM((ADAPTERS, RANK, width), F32)],
        name="reduce_grads",
    )(adapter_ids, slabs)
    return [jnp.swapaxes(value, 1, 2) if turn else value for value, turn in zip(sums, turned)]


def split_three(value):
    first = value.astype(BF16)
    rest = value - first.astype(F32)
    second = rest.astype(BF16)
    third = (rest - second.astype(F32)).astype(BF16)
    return first, second, third


def with_columns(block, columns, lanes):
    out = jnp.where(lanes < HEAD_DIM, block, jnp.zeros_like(block))
    for step, column in enumerate(columns):
        out = jnp.where(lanes == HEAD_DIM + step, column, out)
    return out


def stacked_heads(pair):
    return jnp.concatenate([pair, pltpu.roll(pair, HEAD_DIM, 1)], axis=0)


def allowed(start_row, key_base, query_base):
    keys = lax.broadcasted_iota(jnp.int32, (BLOCK, BLOCK), 0)
    last = query_base - key_base + lax.broadcasted_iota(jnp.int32, (1, BLOCK), 1)
    inside = (keys >= start_row - key_base) & (keys <= last)
    return jnp.concatenate([inside, inside], axis=1)


def forward_attention(bounds, starts, queries, keyvals, column):
    rows = queries.shape[0]
    length = keyvals.shape[0]
    halo = length - rows
    steps = rows // BLOCK

    def kernel(bound_ref, start_ref, *refs):
        arrays, (out_ref, log_ref, key_scr, value_scr) = refs[:-4], refs[-4:]
        query_ref, keyval_ref = arrays[0], arrays[-1].at[:, column * PAIR : (column + 1) * PAIR]
        lanes = lax.broadcasted_iota(jnp.int32, (length, 128), 1)
        both = keyval_ref[...].astype(F32)
        key_scr[...] = jnp.where(lanes < HEAD_DIM, both, 0.0).astype(BF16)
        values = jnp.where(lanes < HEAD_DIM, pltpu.roll(both, HEAD_DIM, 1), 1.0)
        value_scr[...] = values.T.astype(BF16)

        def one_step(step, carry):
            own = pl.ds(pl.multiple_of(step * BLOCK, BLOCK), BLOCK)
            query = stacked_heads(query_ref[own, :PAIR].astype(F32)).astype(BF16)
            start_row = start_ref[:, own]
            diagonal = halo // BLOCK + step
            count = diagonal - bound_ref[0, step] + 1

            def block(index):
                base = pl.multiple_of(jnp.maximum(index, 0) * BLOCK, BLOCK)
                scores = contract_cols(key_scr[pl.ds(base, BLOCK), :], query)
                keep = allowed(start_row, index * BLOCK, diagonal * BLOCK)
                weights = jnp.where(keep, jnp.exp2(scores), 0.0).astype(BF16)
                return matmul(value_scr[:, pl.ds(base, BLOCK)], weights)

            def pair_of_blocks(turn, total):
                index = diagonal - 2 * turn
                return total + (block(index) + block(index - 1))

            total = lax.fori_loop(0, (count + 1) // 2, pair_of_blocks, jnp.zeros((128, 2 * BLOCK), F32))
            norm = total[HEAD_DIM : HEAD_DIM + 1, :]
            mixed = total[:HEAD_DIM, :] / norm
            out_ref[own, :] = jnp.concatenate([mixed[:, :BLOCK], mixed[:, BLOCK:]], axis=0).T.astype(BF16)
            log_ref[step] = jnp.broadcast_to(jnp.log2(norm), (8, 2 * BLOCK))
            return carry

        lax.fori_loop(0, steps, one_step, 0)

    arrays = [queries, keyvals] if halo else [queries]
    return pl.pallas_call(
        kernel,
        in_specs=[SMEM_SPEC] + [VMEM_SPEC] * (1 + len(arrays)),
        out_specs=[VMEM_SPEC] * 2,
        out_shape=[
            jax.ShapeDtypeStruct((rows, 128), BF16),
            jax.ShapeDtypeStruct((steps, 8, 2 * BLOCK), F32),
        ],
        scratch_shapes=[pltpu.VMEM((length, 128), BF16), pltpu.VMEM((128, length), BF16)],
        compiler_params=pltpu.CompilerParams(vmem_limit_bytes=40 << 20),
        cost_estimate=pl.CostEstimate(
            flops=4 * rows * 1024 * 256 * 2, bytes_accessed=4 * rows * 256, transcendentals=rows * 2048
        ),
        name="forward_attention",
    )(bounds, starts, *arrays)


TURNS = (SEGMAX // BLOCK + 2) // 2


def probabilities(bounds, starts, queries, keyvals, column, logs):
    rows = queries.shape[0]
    length = keyvals.shape[0]
    halo = length - rows
    steps = rows // BLOCK

    def kernel(bound_ref, start_ref, log_ref, *refs):
        arrays, (out_ref, key_scr, buffer, sems) = refs[:-4], refs[-4:]
        query_ref, keyval_ref = arrays[0], arrays[-1].at[:, column * PAIR : (column + 1) * PAIR]
        whole = lax.broadcasted_iota(jnp.int32, (length, 128), 1)
        ones = jnp.where(whole < HEAD_DIM + 3, 1.0, 0.0)
        key_scr[...] = jnp.where(whole < HEAD_DIM, keyval_ref[...].astype(F32), ones).astype(BF16)

        def turns(step):
            return (halo // BLOCK + step - bound_ref[0, step] + 2) // 2

        def stored(slot, step, turn):
            blocks = pl.ds(2 * turn, 2)
            return pltpu.make_async_copy(buffer.at[slot, blocks], out_ref.at[step, blocks], sems.at[slot])

        def finish(step):
            def wait(turn, carry):
                stored(lax.rem(step, 2), step, turn).wait()
                return carry

            lax.fori_loop(0, turns(step), wait, 0)

        def one_step(step, carry):
            @pl.when(step >= 2)
            def _():
                finish(step - 2)

            slot = lax.rem(step, 2)
            own = pl.ds(pl.multiple_of(step * BLOCK, BLOCK), BLOCK)
            lanes = lax.broadcasted_iota(jnp.int32, (2 * BLOCK, 128), 1)
            query = stacked_heads(query_ref[own, :PAIR].astype(F32))
            log_column = log_ref[step].T[:, :1]
            query_low = with_columns(query, [part.astype(F32) for part in split_three(-log_column)], lanes).astype(BF16)
            start_row = start_ref[:, own]
            diagonal = halo // BLOCK + step

            def block(index):
                where = pl.ds(pl.multiple_of(jnp.maximum(index, 0) * BLOCK, BLOCK), BLOCK)
                weights = jnp.exp2(contract_cols(key_scr[where, :], query_low))
                keep = allowed(start_row, index * BLOCK, diagonal * BLOCK)
                return jnp.where(keep, weights, 0.0).astype(BF16)

            def pair_of_blocks(turn, carry):
                index = diagonal - 2 * turn
                found = [block(index), block(index - 1)]
                buffer[slot, 2 * turn] = found[0]
                buffer[slot, 2 * turn + 1] = found[1]
                stored(slot, step, turn).start()
                return carry

            lax.fori_loop(0, turns(step), pair_of_blocks, 0)
            return carry

        lax.fori_loop(0, steps, one_step, 0)
        finish(steps - 2)
        finish(steps - 1)

    arrays = [queries, keyvals] if halo else [queries]
    return pl.pallas_call(
        kernel,
        in_specs=[SMEM_SPEC] + [VMEM_SPEC] * (2 + len(arrays)),
        out_specs=ANY_SPEC,
        out_shape=jax.ShapeDtypeStruct((steps, 2 * TURNS, BLOCK, 2 * BLOCK), BF16),
        scratch_shapes=[
            pltpu.VMEM((length, 128), BF16),
            pltpu.VMEM((2, 2 * TURNS, BLOCK, 2 * BLOCK), BF16),
            pltpu.SemaphoreType.DMA((2,)),
        ],
        compiler_params=pltpu.CompilerParams(vmem_limit_bytes=40 << 20),
        cost_estimate=pl.CostEstimate(
            flops=4 * rows * 1024 * 256, bytes_accessed=20 << 20, transcendentals=rows * 2048
        ),
        name="probabilities",
    )(bounds, starts, logs, *arrays)


def backward_attention(bounds, queries, keyvals, column, mixed, probs, grads):
    rows = queries.shape[0]
    length = keyvals.shape[0]
    halo = length - rows
    steps = rows // BLOCK

    def kernel(bound_ref, *refs):
        arrays, refs = refs[: 2 if halo else 1], refs[2 if halo else 1 :]
        mixed_ref, grad_ref, probs_ref = refs[:3]
        outs, (value_scr, turned_scr, key_sum, value_sum, buffer, sems) = refs[3:-6], refs[-6:]
        query_ref, keyval_ref = arrays[0], arrays[-1].at[:, column * PAIR : (column + 1) * PAIR]

        def turns(step):
            return (halo // BLOCK + step - bound_ref[0, step] + 2) // 2

        def loaded(step, turn):
            slot, blocks = lax.rem(step, 2), pl.ds(2 * turn, 2)
            return pltpu.make_async_copy(probs_ref.at[step, blocks], buffer.at[slot, blocks], sems.at[slot])

        def begin(step):
            def start(turn, carry):
                loaded(step, turn).start()
                return carry

            lax.fori_loop(0, turns(step), start, 0)

        begin(0)
        whole = lax.broadcasted_iota(jnp.int32, (length, 128), 1)
        both = keyval_ref[...].astype(F32)
        ones = jnp.where(whole < HEAD_DIM + 3, 1.0, 0.0)
        value_scr[...] = jnp.where(whole < HEAD_DIM, pltpu.roll(both, HEAD_DIM, 1), ones).astype(BF16)
        turned_scr[...] = both.T.astype(BF16)
        key_sum[...] = jnp.zeros_like(key_sum)
        value_sum[...] = jnp.zeros_like(value_sum)

        def one_step(step, carry):
            @pl.when(step + 1 < steps)
            def _():
                begin(step + 1)

            slot = lax.rem(step, 2)
            own = pl.ds(pl.multiple_of(step * BLOCK, BLOCK), BLOCK)
            lanes = lax.broadcasted_iota(jnp.int32, (2 * BLOCK, 128), 1)
            query_low = stacked_heads(query_ref[own, :PAIR].astype(F32)).astype(BF16)
            grad = stacked_heads(grad_ref[own, :].astype(F32))
            weighed = stacked_heads(mixed_ref[own, :].astype(F32))
            inner = jnp.sum(jnp.where(lanes < HEAD_DIM, grad * weighed, 0.0), axis=1, keepdims=True)
            grad_low = with_columns(grad, [part.astype(F32) for part in split_three(-inner)], lanes).astype(BF16)
            diagonal = halo // BLOCK + step

            def wait(turn, carry):
                loaded(step, turn).wait()
                return carry

            lax.fori_loop(0, turns(step), wait, 0)

            def block(index, weights):
                where = pl.ds(pl.multiple_of(jnp.maximum(index, 0) * BLOCK, BLOCK), BLOCK)
                slopes = (weights.astype(F32) * contract_cols(value_scr[where, :], grad_low)).astype(BF16)
                value_part = matmul(weights, grad_low)
                return where, value_part, matmul(slopes, query_low), matmul(turned_scr[:, where], slopes)

            def pair_of_blocks(turn, total):
                index = diagonal - 2 * turn
                parts = [block(index, buffer[slot, 2 * turn]), block(index - 1, buffer[slot, 2 * turn + 1])]
                for where, value_part, key_part, _ in parts:
                    value_sum[where, :] += value_part
                    key_sum[where, :] += key_part
                return total + (parts[0][3] + parts[1][3])

            total = lax.fori_loop(0, turns(step), pair_of_blocks, jnp.zeros((128, 2 * BLOCK), F32))
            total = total[:HEAD_DIM] * HEAD_DIM**-0.5
            outs[0][own, :PAIR] = jnp.concatenate([total[:, :BLOCK], total[:, BLOCK:]], axis=0).T.astype(BF16)
            return carry

        lax.fori_loop(0, steps, one_step, 0)
        keyval_grad = jnp.where(whole < HEAD_DIM, key_sum[...] * (1.0 / LOG2E), pltpu.roll(value_sum[...], HEAD_DIM, 1))
        if halo:
            outs[1][...] = keyval_grad
        else:
            outs[0][:, PAIR:] = keyval_grad.astype(BF16)

    arrays = [queries, keyvals] if halo else [queries]
    return pl.pallas_call(
        kernel,
        in_specs=[SMEM_SPEC] + [VMEM_SPEC] * (2 + len(arrays)) + [ANY_SPEC],
        out_specs=[VMEM_SPEC] * (2 if halo else 1),
        out_shape=[jax.ShapeDtypeStruct((rows, 128), BF16), jax.ShapeDtypeStruct((length, 128), F32)]
        if halo
        else [jax.ShapeDtypeStruct((rows, 2 * PAIR), BF16)],
        scratch_shapes=[
            pltpu.VMEM((length, 128), BF16),
            pltpu.VMEM((128, length), BF16),
            pltpu.VMEM((length, 128), F32),
            pltpu.VMEM((length, 128), F32),
            pltpu.VMEM((2, 2 * TURNS, BLOCK, 2 * BLOCK), BF16),
            pltpu.SemaphoreType.DMA((2,)),
        ],
        compiler_params=pltpu.CompilerParams(vmem_limit_bytes=40 << 20),
        cost_estimate=pl.CostEstimate(
            flops=8 * rows * 1024 * 256 * 2, bytes_accessed=20 << 20, transcendentals=0
        ),
        name="backward_attention",
    )(bounds, *arrays, mixed, grads, probs)


def document_bounds(segment_ids, origin, halo, span, seq_start):
    tokens = segment_ids.shape[0]
    names = jnp.arange(tokens // (SEGMAX // 2), dtype=jnp.int32)
    begin = jnp.sum((segment_ids[None, :] < names[:, None]).astype(jnp.int32), axis=1)
    own = lax.dynamic_slice_in_dim(segment_ids, origin, span, 0)
    start = jnp.sum(jnp.where(own[None, :] == names[:, None], begin[:, None], 0), axis=0)
    start = jnp.maximum(start, seq_start) - (origin - halo)
    first = start[::BLOCK] // BLOCK
    clear = -(-start[BLOCK - 1 :: BLOCK] // BLOCK)
    bounds = jnp.stack([first, jnp.maximum(clear, first)])
    return bounds, start[None, :]


TILE = 512


def silu_parts(gate):
    share = 1.0 / (1.0 + jnp.exp(-gate))
    return share, gate * share


def feed_forward(mixed, hidden, cotangent, gain, weights, chosen):
    members, rows, _ = mixed.shape
    tiles = FF // TILE
    packed = isinstance(weights, Pieces)
    arrays = weights.blocks if packed else weights
    count = len(arrays)
    slices = 2 * FF // D

    def kernel(*refs):
        (
            mixed_ref, hidden_ref, cot_ref, gain_ref,
            out_down_ref, out_up_ref, mlp_down_ref, mlp_up_ref, ffd_down_ref, ffd_up_ref,
        ) = refs[:10]
        weight_refs = refs[10 : 10 + count]
        (
            output_ref, middle_grad_ref, mixed_grad_ref,
            out_down_grad, out_up_grad, mlp_down_grad, mlp_up_grad, ffd_down_grad, ffd_up_grad,
            wide_scr, down_scr, mix_scr, middle_scr, normed_scr, branch_scr, slope_scr,
            low_scr, low_turned, back_scr, back_turned, out_low_scr, down_sum, gate_sum, up_sum, sems,
        ) = refs[10 + count :]
        out_columns = slice(2 * FF, 2 * FF + D)

        def column_piece(piece):
            return slice(piece * D, (piece + 1) * D)

        if packed:
            blocks = weights.copies(weight_refs)
            devices = len(blocks)
            part, down_part = D // devices, FF // devices

            def start_piece(piece):
                for ref, source, where, size in blocks:
                    row = pl.multiple_of(where // size * part, 8)
                    pltpu.make_async_copy(
                        ref.at[pl.ds(source + piece * part, part), :],
                        wide_scr.at[pl.ds(row, part), column_piece(piece)],
                        sems.at[piece],
                    ).start()

            def start_down():
                for ref, source, where, size in blocks:
                    row = pl.multiple_of(where // size * down_part, 8)
                    pltpu.make_async_copy(
                        ref.at[pl.ds(source + (slices + 1) * part, down_part), :],
                        down_scr.at[pl.ds(row, down_part), :],
                        sems.at[slices + 1],
                    ).start()
        else:

            def start_piece(piece):
                columns = column_piece(piece)
                pltpu.make_async_copy(
                    weight_refs[0].at[:, columns], wide_scr.at[:, columns], sems.at[piece]
                ).start()

            def start_down():
                pltpu.make_async_copy(weight_refs[1], down_scr, sems.at[slices + 1]).start()

        def finish_piece(piece):
            region = wide_scr.at[:, column_piece(piece)]
            pltpu.make_async_copy(region, region, sems.at[piece]).wait()

        per_piece = D // TILE
        first_use = {}
        for piece in range(slices):
            uses = [c // TILE % tiles for c in range(piece * D, (piece + 1) * D, TILE)]
            first_use.setdefault(min(uses), []).append(piece)
        start_piece(slices)
        for piece in first_use[0]:
            start_piece(piece)
        start_down()

        cot = cot_ref[...]
        for member in range(members):
            mix_scr[:, member * PAIR : (member + 1) * PAIR] = mixed_ref[member]
        out_low = contract_cols(mix_scr[...], out_down_ref[...]).astype(BF16)
        out_low_scr[...] = out_low
        back = contract_cols(cot, ffd_up_ref[...])
        back_scr[...] = back.astype(BF16)
        back_turned[...] = back.T.astype(BF16)
        branch_scr[...] = jnp.zeros_like(branch_scr)
        slope_scr[...] = jnp.zeros_like(slope_scr)
        down_sum[...] = jnp.zeros_like(down_sum)
        gate_sum[...] = jnp.zeros_like(gate_sum)
        up_sum[...] = jnp.zeros_like(up_sum)
        finish_piece(slices)
        middle = (
            hidden_ref[...].astype(F32)
            + matmul(mix_scr[...], wide_scr[:, out_columns])
            + matmul(out_low, out_up_ref[...])
        )
        middle_scr[...] = middle
        normed = (middle * row_scale(middle) * gain_ref[...]).astype(BF16)
        normed_scr[...] = normed
        low = contract_cols(normed, mlp_down_ref[...])
        low_scr[...] = low.astype(BF16)
        low_turned[...] = low.T.astype(BF16)
        pltpu.make_async_copy(down_scr, down_scr, sems.at[slices + 1]).wait()

        def tile(index, carry):
            base = pl.multiple_of(index * TILE, TILE)
            gate_at, up_at = pl.ds(base, TILE), pl.ds(base + FF, TILE)
            for use, group in sorted(first_use.items()):

                @pl.when(index == use)
                def _(group=group):
                    for piece in group:
                        finish_piece(piece)

                if use > 0:

                    @pl.when(index == max(use - per_piece, 0))
                    def _(group=group):
                        for piece in group:
                            start_piece(piece)

            normed = normed_scr[...]
            low = low_scr[...]
            gate = matmul(normed, wide_scr[:, gate_at]) + matmul(low[:, :RANK], mlp_up_ref[:, gate_at])
            up = matmul(normed, wide_scr[:, up_at]) + matmul(low[:, RANK:], mlp_up_ref[:, up_at])
            share, active = silu_parts(gate)
            units = (active * up).astype(BF16)
            down = down_scr[gate_at, :]
            branch_scr[...] += matmul(units, down)
            down_sum[...] += contract_cols(units, ffd_down_ref[:, gate_at])
            ffd_down_grad[:, gate_at] = matmul(back_turned[...], units)
            units_grad = contract_cols(cot_ref[...], down) + matmul(back_scr[...], ffd_down_ref[:, gate_at])
            gate_grad = (units_grad * up * (share * (1.0 + gate * (1.0 - share)))).astype(BF16)
            up_grad = (units_grad * active).astype(BF16)
            slope_scr[...] += contract_cols(gate_grad, wide_scr[:, gate_at]) + contract_cols(
                up_grad, wide_scr[:, up_at]
            )
            gate_sum[...] += contract_cols(gate_grad, mlp_up_ref[:, gate_at])
            up_sum[...] += contract_cols(up_grad, mlp_up_ref[:, up_at])
            mlp_up_grad[:, gate_at] = matmul(low_turned[:RANK, :], gate_grad)
            mlp_up_grad[:, up_at] = matmul(low_turned[RANK:, :], up_grad)
            return carry

        lax.fori_loop(0, tiles, tile, 0)

        middle = middle_scr[...]
        cot = cot_ref[...]
        down_low = down_sum[...].astype(BF16)
        output_ref[...] = (middle + branch_scr[...] + matmul(down_low, ffd_up_ref[...])).astype(BF16)
        ffd_up_grad[...] = contract_rows(down_low, cot)
        low_grad = jnp.concatenate([gate_sum[...], up_sum[...]], axis=1).astype(BF16)
        mlp_down_grad[...] = contract_rows(low_grad, normed_scr[...])
        slope = gain_ref[...] * (slope_scr[...] + matmul(low_grad, mlp_down_ref[...]))
        scale = row_scale(middle)
        inner = jnp.mean(slope * middle, axis=1, keepdims=True)
        middle_grad = cot.astype(F32) + scale * slope - middle * (scale * scale * scale * inner)
        middle_grad_ref[...] = middle_grad
        branch_grad = middle_grad.astype(BF16)
        out_up_grad[...] = contract_rows(out_low_scr[...], branch_grad)
        out_low_grad = contract_cols(branch_grad, out_up_ref[...]).astype(BF16)
        out_down_grad[...] = contract_rows(out_low_grad, mix_scr[...])
        mixed_grad = contract_cols(branch_grad, wide_scr[:, out_columns]) + matmul(out_low_grad, out_down_ref[...])
        for member in range(members):
            mixed_grad_ref[member] = mixed_grad[:, member * PAIR : (member + 1) * PAIR].astype(BF16)

    results = pl.pallas_call(
        kernel,
        in_specs=[VMEM_SPEC] * 10 + [ANY_SPEC] * count,
        out_specs=[VMEM_SPEC] * 9,
        out_shape=[
            jax.ShapeDtypeStruct((rows, D), BF16),
            jax.ShapeDtypeStruct((rows, D), F32),
            jax.ShapeDtypeStruct((members, rows, PAIR), BF16),
            jax.ShapeDtypeStruct((RANK, QW), F32),
            jax.ShapeDtypeStruct((RANK, D), F32),
            jax.ShapeDtypeStruct((2 * RANK, D), F32),
            jax.ShapeDtypeStruct((RANK, 2 * FF), F32),
            jax.ShapeDtypeStruct((RANK, FF), F32),
            jax.ShapeDtypeStruct((RANK, D), F32),
        ],
        scratch_shapes=[
            pltpu.VMEM((D, 2 * FF + D), BF16), pltpu.VMEM((FF, D), BF16),
            pltpu.VMEM((rows, QW), BF16), pltpu.VMEM((rows, D), F32), pltpu.VMEM((rows, D), BF16),
            pltpu.VMEM((rows, D), F32), pltpu.VMEM((rows, D), F32),
            pltpu.VMEM((rows, 2 * RANK), BF16), pltpu.VMEM((2 * RANK, rows), BF16),
            pltpu.VMEM((rows, RANK), BF16), pltpu.VMEM((RANK, rows), BF16), pltpu.VMEM((rows, RANK), BF16),
            pltpu.VMEM((rows, RANK), F32), pltpu.VMEM((rows, RANK), F32), pltpu.VMEM((rows, RANK), F32),
            pltpu.SemaphoreType.DMA((2 + slices,)),
        ],
        compiler_params=pltpu.CompilerParams(vmem_limit_bytes=60 << 20),
        cost_estimate=pl.CostEstimate(
            flops=rows * (12 * D * FF + 4 * D * QW), bytes_accessed=6 * D * FF + 16 * rows * D,
            transcendentals=rows * FF,
        ),
        name="feed_forward",
    )(mixed, hidden, cotangent, gain[None, :], *chosen, *arrays)
    return results[0], results[1], results[2], list(results[3:])


def local(
    hidden, cotangent, segment_ids, adapter_ids, attn_gain, query_gain, key_gain, ffn_gain,
    qkv_weight, out_weight, gate_up_weight, down_weight, *adapters,
):
    rows = hidden.shape[0]
    devices = lax.axis_size("ctx") * lax.axis_size("head")
    members = KV_HEADS
    groups = [[members * g + i for i in range(members)] for g in range(devices // members)]
    span = rows * members
    seq_length = rows * devices // NSEQ
    halo = 0 if span == seq_length else SEGMAX
    here = lax.axis_index("ctx") * lax.axis_size("head") + lax.axis_index("head")
    origin = here // members * span
    seq_start = origin // seq_length * seq_length
    positions = here * rows - seq_start + jnp.arange(rows, dtype=jnp.int32)
    bounds, starts = document_bounds(segment_ids, origin, halo, span, seq_start)

    def swap(value):
        return lax.all_to_all(value, AXES, 0, 0, axis_index_groups=groups, tiled=True)

    def shifted(value, by):
        pairs = [(i, i + by) for i in range(devices) if 0 <= i + by < devices]
        return lax.ppermute(value, AXES, pairs)

    def gather(value):
        return lax.all_gather(value, AXES, axis=0, tiled=True)

    shapes = [member.shape[1:] for member in adapters]
    def exchange(packed):
        return lax.all_to_all(packed, AXES, 0, 0, tiled=True)

    spread = by_axes()
    if spread:
        found = {(0, 0): stack_shard(gate_up_weight, out_weight, down_weight)}
        pending = []

        def move(*keys, extra=()):
            hops = [(found[key[0] ^ key[2], key[1] - key[3]], key[2], key[3]) for key in keys]
            hops += extra
            held = lax.optimization_barrier((*[value for value, _, _ in hops], *pending))
            results = [hop(value, flip, step) for value, (_, flip, step) in zip(held, hops)]
            found.update(zip([key[:2] for key in keys], results))
            pending[:] = results
            return results[len(keys) :]

        def cores(*keys):
            return [(flip, step, 1, 0) for flip, step in keys]

        def then(value):
            return lax.optimization_barrier((value, *pending))[0]

        line = move((2, 0, 2, 0), (4, 0, 4, 0), extra=[(qkv_weight, 0, step) for step in range(1, 4)])
        slabs = exchange(lax.optimization_barrier((pack_adapters(adapter_ids, adapters[:2], devices), *line))[0])
        line = jnp.concatenate([qkv_weight] + line, axis=0)
        plane = move((0, 1, 0, 1), extra=[(line, flip, 0) for flip in (2, 4, 6)])
        pending.append(slabs)
        plane = jnp.concatenate([line] + plane, axis=0)
        (across,) = move((0, 2, 0, 1), (2, 1, 2, 0), (6, 0, 4, 0), extra=[(plane, 1, 0)])
        qkv = Pieces([((0, (0, 1, 2, 3)), plane), ((1, (0, 1, 2, 3)), across)], D)
        hidden_then = hidden
    else:
        qkv = whole_gather(qkv_weight)
        weights = [gather(jnp.concatenate([gate_up_weight, out_weight], axis=1)), gather(down_weight)]
        hidden_then = hidden
        slabs = exchange(pack_adapters(adapter_ids, adapters[:2], devices))
    chosen = list(unpack_adapters(slabs, shapes[:2]))

    head_gain = jnp.stack([jnp.tile(query_gain, 2), jnp.tile(key_gain, 2)])
    tables = rope_tables(positions)
    sent, low_qkv, kept = project_heads(hidden_then, attn_gain, head_gain, tables, qkv, chosen[0], chosen[1])
    if spread:
        sent = then(sent)
    queries = swap(sent).reshape(span, 2 * PAIR)
    keyvals, column = queries, 1
    if halo:
        keyvals, column = queries[:, PAIR:], 0
        keyvals = jnp.concatenate([shifted(keyvals[span - halo :], members), keyvals], axis=0)
    if spread:
        move((2, 2, 2, 0), (4, 1, 4, 0), *cores((1, 0)))
        first = pending[:]
        move((0, 3, 0, 1))
        pending[:] = first
        late_adapters = then(adapters[2])
        move((6, 1, 2, 0), (4, 2, 4, 0), *cores((1, 1), (3, 0)))
        keyvals = queries = then(queries)
        move((2, 3, 2, 0), (4, 3, 4, 0), *cores((5, 0), (7, 0), (1, 2)))
    else:
        late_adapters = adapters[2]
    packed = pack_adapters(adapter_ids, (late_adapters, *adapters[3:]), devices)
    slabs = exchange(lax.optimization_barrier((packed, queries))[0])
    mixed, logs = forward_attention(bounds, starts, queries, keyvals, column)
    chosen += list(unpack_adapters(slabs, shapes[2:]))
    if spread:
        pending.append(logs)
        move((6, 3, 2, 0), (6, 2, 4, 0), *cores((3, 1), (5, 1), (3, 2)))
    mixed_then = lax.optimization_barrier((mixed, slabs))[0]
    mixture_tok = swap(mixed_then.reshape(members, rows, PAIR))
    if spread:
        pending.append(chosen[-1])
        move(*cores((5, 2), (7, 1), (1, 3), (3, 3), (5, 3)))
        pending.append(mixture_tok)
        move(*cores((7, 2), (7, 3)))
        weights = Pieces([((flip, (step,)), block) for (flip, step), block in found.items()], D)
    output, middle_grad, mixture_grad, early = feed_forward(
        mixture_tok, hidden, cotangent, ffn_gain, weights, chosen[2:]
    )
    grad_rows = swap(mixture_grad).reshape(span, PAIR)
    logs_then = lax.optimization_barrier((logs, mixture_grad))[0]
    probs = probabilities(bounds, starts, queries, keyvals, column, logs_then)
    early_packed, grad_rows = lax.optimization_barrier((pack_grads(early, devices), grad_rows))
    early_slabs = exchange(early_packed)
    back = backward_attention(bounds, queries, keyvals, column, mixed, probs, grad_rows)
    if halo:
        query_grads, keyval_grads = back
        returned = shifted(keyval_grads[:halo].astype(BF16), -members).astype(F32)
        keyval_grads = jnp.concatenate([keyval_grads[halo:span], keyval_grads[span:] + returned], axis=0)
        back = [jnp.concatenate([query_grads, keyval_grads.astype(BF16)], axis=1)]
    back, early_slabs = lax.optimization_barrier((back[0], early_slabs))
    early_owned = reduce_grads(adapter_ids, early_slabs, shapes[2:])
    back = back.reshape(members, rows, 2 * PAIR)
    arrived_back = swap(back)
    projected_grad, low_grad, packed = project_back(
        arrived_back, kept, head_gain, tables, hidden, attn_gain, low_qkv, chosen[1], devices
    )
    late_slabs = exchange(packed)
    late_owned = reduce_grads(adapter_ids, late_slabs, shapes[:2])
    input_grad = input_back(projected_grad, low_grad, qkv, chosen[0], hidden, attn_gain, middle_grad)
    return (output, input_grad, *late_owned, *early_owned)


def solution(mesh):
    by_rows = P(AXES, None)
    by_cols = P(None, None, AXES)
    placed = (by_rows, by_rows) + (P(),) * 6 + (by_rows,) * 4 + (by_cols,) * 8
    return jax.shard_map(
        local,
        mesh=mesh,
        in_specs=placed,
        out_specs=(by_rows, by_rows) + (by_cols,) * 8,
        check_vma=False,
    )
```

```python
import functools
import math

import jax
import jax.numpy as jnp
from jax import lax
from jax.experimental import pallas as pl
from jax.experimental.pallas import tpu as pltpu
from jax.sharding import PartitionSpec as P

D = 1024
HEADS = 16
KV_HEADS = 8
HEAD_DIM = 64
FF = 4608
RANK = 16
ADAPTERS = 8
NSEQ = 4
SEGMAX = 2048
QW = 1024
KW = 512
PAIR = 2 * HEAD_DIM
BLOCK = 256
AXES = ("ctx", "head")

epsilon = 1e-05
rope_base = 1000000.0
LOG2E = math.log2(math.e)
QSCALE = HEAD_DIM**-0.5 * LOG2E
F32 = jnp.float32
BF16 = jnp.bfloat16


def matmul(left_side, right_side):
    return jnp.dot(left_side, right_side, preferred_element_type=F32)


def contract_rows(left_side, right_side):
    return lax.dot_general(left_side, right_side, (((0,), (0,)), ((), ())), preferred_element_type=F32)


def contract_cols(left_side, right_side):
    return lax.dot_general(left_side, right_side, (((1,), (1,)), ((), ())), preferred_element_type=F32)


def rope_tables(positions):
    middle = HEAD_DIM // 2
    frequency = jnp.power(rope_base, -(2.0 / HEAD_DIM) * jnp.arange(middle, dtype=F32))
    angles = positions.astype(F32)[:, None] * frequency[None, :]
    cosine, sine = jnp.cos(angles), jnp.sin(angles)
    return jnp.concatenate([cosine] * 4, axis=1), jnp.concatenate([-sine, sine] * 2, axis=1)


ANY_SPEC = pl.BlockSpec(memory_space=pl.ANY)


class Pieces:
    def __init__(self, blocks, rows):
        self.keys = [key for key, _ in blocks]
        self.blocks = [block for _, block in blocks]
        self.rows = rows

    def offsets(self):
        if self.keys[0] is None:
            return [(0, 0, self.rows)]
        depth = lax.axis_size("head")
        ctx, head = lax.axis_index("ctx"), lax.axis_index("head")
        found = []
        for flip, steps in self.keys:
            flips = [flip] if len(steps) == 1 else [flip ^ other for other in (0, 2, 4, 6)]
            size = self.blocks[0].shape[0] // (len(steps) * len(flips))
            for place, (flip, step) in enumerate([(flip, step) for flip in flips for step in steps]):
                device = jnp.bitwise_xor(ctx, flip) * depth + lax.rem(head - step + depth, depth)
                found.append((place * size, pl.multiple_of(device * size, 8), size))
        return found

    def copies(self, refs):
        found, offsets = [], self.offsets()
        share = len(offsets) // len(refs)
        for place, (source, target, size) in enumerate(offsets):
            found.append((refs[place // share], source, target, size))
        return found


def by_axes():
    return lax.axis_size("ctx") == 8 and lax.axis_size("head") == 4


def hop(value, flip, step):
    depth = lax.axis_size("head")
    pairs = [
        (ctx * depth + head, (ctx ^ flip) * depth + (head + step) % depth)
        for ctx in range(lax.axis_size("ctx"))
        for head in range(depth)
    ]
    return lax.ppermute(value, AXES, pairs)


def stack_shard(gate_up_weight, out_weight, down_weight):
    part, down_part = out_weight.shape[0], down_weight.shape[0]
    slices = 2 * FF // D

    def kernel(wide_ref, out_ref, down_ref, stacked_ref):
        for piece in range(slices):
            stacked_ref[piece * part : (piece + 1) * part, :] = wide_ref[:, piece * D : (piece + 1) * D]
        stacked_ref[slices * part : (slices + 1) * part, :] = out_ref[...]
        stacked_ref[(slices + 1) * part :, :] = down_ref[...]

    return pl.pallas_call(
        kernel,
        in_specs=[VMEM_SPEC] * 3,
        out_specs=VMEM_SPEC,
        out_shape=jax.ShapeDtypeStruct(((slices + 1) * part + down_part, D), BF16),
        name="stack_shard",
    )(gate_up_weight, out_weight, down_weight)


def whole_gather(value):
    full = lax.all_gather(value, AXES, axis=0, tiled=True)
    return Pieces([(None, full)], full.shape[0])


def start_loads(pieces, refs, target, sem):
    for ref, source, where, size in pieces.copies(refs):
        pltpu.make_async_copy(ref.at[pl.ds(source, size), :], target.at[pl.ds(where, size), :], sem).start()


def finish_loads(target, sem, columns=None):
    region = target if columns is None else target.at[:, columns]
    pltpu.make_async_copy(region, region, sem).wait()


def head_means(values, ones):
    return matmul(values.astype(BF16), ones) * (1.0 / HEAD_DIM)


def head_ones():
    row = lax.broadcasted_iota(jnp.int32, (PAIR, PAIR), 0) // HEAD_DIM
    col = lax.broadcasted_iota(jnp.int32, (PAIR, PAIR), 1) // HEAD_DIM
    return jnp.where(row == col, 1.0, 0.0).astype(BF16)


def swapped_halves(values):
    lanes = lax.broadcasted_iota(jnp.int32, values.shape, 1)
    half = HEAD_DIM // 2
    return jnp.where(lanes % HEAD_DIM < half, pltpu.roll(values, PAIR - half, 1), pltpu.roll(values, half, 1))


def row_scale(values):
    return lax.rsqrt(jnp.mean(values * values, axis=1, keepdims=True) + epsilon)


ROWS = 256


def in_hbm(value):
    return pltpu.with_memory_space_constraint(value, pltpu.HBM)


def row_block(width):
    return pl.BlockSpec((ROWS, width), lambda i: (i, 0))


def fixed(shape):
    return pl.BlockSpec(shape, lambda i: (0,) * len(shape))


def project_heads(hidden, gain, head_gain, tables, pieces, down, up):
    rows = hidden.shape[0]
    count = len(pieces.blocks)
    width = QW + 2 * KW

    def kernel(*refs):
        hidden_ref, gain_ref, head_gain_ref, cos_ref, sin_ref, down_ref, up_ref = refs[:7]
        blocks = refs[7 : 7 + count]
        sent_ref, low_ref, kept_ref, weight, sem = refs[7 + count :]

        @pl.when(pl.program_id(0) == 0)
        def _():
            start_loads(pieces, blocks, weight, sem)

        inputs = hidden_ref[...].astype(F32)
        normed = (inputs * row_scale(inputs) * gain_ref[...]).astype(BF16)
        low = contract_cols(normed, down_ref[...]).astype(BF16)
        low_ref[...] = low
        ones = head_ones()
        cos, sin = cos_ref[...], sin_ref[...]
        lanes = lax.broadcasted_iota(jnp.int32, (ROWS, PAIR), 1)

        @pl.when(pl.program_id(0) == 0)
        def _():
            finish_loads(weight, sem)

        def columns(start, size, group):
            return matmul(normed, weight[:, start : start + size]) + matmul(
                low[:, RANK * group : RANK * (group + 1)], up_ref[:, start : start + size]
            )

        def turned(values, gains):
            unit = values * lax.rsqrt(head_means(values * values, ones) + epsilon) * gains
            return unit * cos + swapped_halves(unit) * sin

        step = 4 * PAIR
        for start in range(0, QW, step):
            some = columns(start, step, 0)
            kept_ref[:, start : start + step] = some.astype(BF16)
            for side in range(step // PAIR):
                query = turned(some[:, side * PAIR : (side + 1) * PAIR], head_gain_ref[0:1, :]) * QSCALE
                sent_ref[start // PAIR + side, :, :PAIR] = query.astype(BF16)
        for start in range(0, KW, step):
            some = columns(QW + start, step, 1)
            values = columns(QW + KW + start, step, 2)
            kept_ref[:, QW + start : QW + start + step] = some.astype(BF16)
            for side in range(step // PAIR):
                where = slice(side * PAIR, (side + 1) * PAIR)
                key = turned(some[:, where], head_gain_ref[1:2, :])
                value = values[:, where]
                group = (start + side * PAIR) // HEAD_DIM
                sent_ref[group, :, PAIR:] = jnp.where(
                    lanes < HEAD_DIM, key, pltpu.roll(value, HEAD_DIM, 1)
                ).astype(BF16)
                sent_ref[group + 1, :, PAIR:] = jnp.where(
                    lanes < HEAD_DIM, pltpu.roll(key, HEAD_DIM, 1), value
                ).astype(BF16)

    return pl.pallas_call(
        kernel,
        grid=(rows // ROWS,),
        in_specs=[
            row_block(D), fixed((1, D)), fixed((2, PAIR)), row_block(PAIR), row_block(PAIR),
            fixed((3 * RANK, D)), fixed((RANK, width)),
        ]
        + [ANY_SPEC] * count,
        out_specs=[
            pl.BlockSpec((KV_HEADS, ROWS, 2 * PAIR), lambda i: (0, i, 0)), row_block(3 * RANK), row_block(QW + KW),
        ],
        out_shape=[
            jax.ShapeDtypeStruct((KV_HEADS, rows, 2 * PAIR), BF16),
            jax.ShapeDtypeStruct((rows, 3 * RANK), BF16),
            jax.ShapeDtypeStruct((rows, QW + KW), BF16),
        ],
        scratch_shapes=[pltpu.VMEM((D, width), BF16), pltpu.SemaphoreType.DMA],
        compiler_params=pltpu.CompilerParams(vmem_limit_bytes=60 << 20),
        cost_estimate=pl.CostEstimate(flops=2 * rows * D * width, bytes_accessed=10 << 20, transcendentals=0),
        name="project_heads",
    )(hidden, gain[None, :], head_gain, *tables, down, up, *pieces.blocks)


def project_back(back, kept, head_gain, tables, hidden, gain, low, up, devices):
    rows = hidden.shape[0]
    width = QW + 2 * KW
    places, slab = layout_of([(3 * RANK, D // devices), (RANK, width // devices)])

    def kernel(
        back_ref, kept_ref, head_gain_ref, cos_ref, sin_ref, hidden_ref, gain_ref, low_ref, up_ref,
        grad_ref, low_grad_ref, packed_ref, down_sum, up_sum,
    ):
        ones = head_ones()
        cos, sin = cos_ref[...], sin_ref[...]
        lanes = lax.broadcasted_iota(jnp.int32, (ROWS, PAIR), 1)

        @pl.when(pl.program_id(0) == 0)
        def _():
            down_sum[...] = jnp.zeros_like(down_sum)
            up_sum[...] = jnp.zeros_like(up_sum)

        def through(grads, values, gains):
            slope = (grads * cos - swapped_halves(grads) * sin) * gains
            scale = lax.rsqrt(head_means(values * values, ones) + epsilon)
            unit = values * scale
            return scale * (slope - unit * head_means(slope * unit, ones))

        for group in range(KV_HEADS):
            where = slice(group * PAIR, (group + 1) * PAIR)
            grads = back_ref[group, :, :PAIR].astype(F32)
            grad_ref[:, where] = through(grads, kept_ref[:, where].astype(F32), head_gain_ref[0:1, :]).astype(BF16)
        for group in range(0, KV_HEADS, 2):
            even = back_ref[group, :, PAIR:].astype(F32)
            odd = back_ref[group + 1, :, PAIR:].astype(F32)
            keys = jnp.where(lanes < HEAD_DIM, even, pltpu.roll(odd, HEAD_DIM, 1))
            values = jnp.where(lanes < HEAD_DIM, pltpu.roll(even, HEAD_DIM, 1), odd)
            start = QW + group * HEAD_DIM
            where = slice(start, start + PAIR)
            grad_ref[:, where] = through(keys, kept_ref[:, where].astype(F32), head_gain_ref[1:2, :]).astype(BF16)
            grad_ref[:, start + KW : start + KW + PAIR] = values.astype(BF16)
        turned = low_ref[...].astype(F32).T.astype(BF16)
        edges = (0, QW, QW + KW, width)
        parts = []
        for group in range(3):
            where = slice(edges[group], edges[group + 1])
            grads = grad_ref[:, where]
            up_sum[:, where] += matmul(turned[RANK * group : RANK * (group + 1), :], grads)
            parts.append(contract_cols(grads, up_ref[:, where]))
        low_grad = jnp.concatenate(parts, axis=1)
        low_grad_ref[...] = low_grad.astype(BF16)
        inputs = hidden_ref[...].astype(F32)
        normed = (inputs * row_scale(inputs) * gain_ref[...]).astype(BF16)
        down_sum[...] += matmul(low_grad.T.astype(BF16), normed)

        @pl.when(pl.program_id(0) == rows // ROWS - 1)
        def _():
            for device in range(devices):
                for index, part, offset, size in places:
                    packed_ref[device, :, offset : offset + size] = (down_sum, up_sum)[index][
                        RANK * part : RANK * (part + 1), device * size : (device + 1) * size
                    ].astype(BF16)

    return pl.pallas_call(
        kernel,
        grid=(rows // ROWS,),
        in_specs=[
            pl.BlockSpec((KV_HEADS, ROWS, 2 * PAIR), lambda i: (0, i, 0)), row_block(QW + KW), fixed((2, PAIR)),
            row_block(PAIR), row_block(PAIR), row_block(D), fixed((1, D)), row_block(3 * RANK), fixed((RANK, width)),
        ],
        out_specs=[row_block(width), row_block(3 * RANK), fixed((devices, RANK, slab))],
        out_shape=[
            jax.ShapeDtypeStruct((rows, width), BF16),
            jax.ShapeDtypeStruct((rows, 3 * RANK), BF16),
            jax.ShapeDtypeStruct((devices, RANK, slab), BF16),
        ],
        scratch_shapes=[pltpu.VMEM((3 * RANK, D), F32), pltpu.VMEM((RANK, width), F32)],
        compiler_params=pltpu.CompilerParams(vmem_limit_bytes=60 << 20),
        name="project_back",
    )(back, in_hbm(kept), head_gain, *[in_hbm(table) for table in tables], hidden, gain[None, :], in_hbm(low), up)


def input_back(grad, low_grad, pieces, down, hidden, gain, middle_grad):
    rows = hidden.shape[0]
    count = len(pieces.blocks)

    def kernel(*refs):
        grad_ref, low_ref, down_ref, hidden_ref, gain_ref, middle_ref = refs[:6]
        blocks = refs[6 : 6 + count]
        out_ref, weight, sem = refs[6 + count :]

        @pl.when(pl.program_id(0) == 0)
        def _():
            start_loads(pieces, blocks, weight, sem)

        inputs = hidden_ref[...].astype(F32)
        scale = row_scale(inputs)

        @pl.when(pl.program_id(0) == 0)
        def _():
            finish_loads(weight, sem)

        slope = matmul(low_ref[...], down_ref[...]) + contract_cols(grad_ref[...], weight[...])
        slope = slope * gain_ref[...]
        unit = inputs * scale
        inner = jnp.mean(slope * unit, axis=1, keepdims=True)
        out_ref[...] = middle_ref[...] + scale * (slope - unit * inner)

    return pl.pallas_call(
        kernel,
        grid=(rows // ROWS,),
        in_specs=[
            row_block(QW + 2 * KW), row_block(3 * RANK), fixed((3 * RANK, D)), row_block(D), fixed((1, D)), row_block(D),
        ]
        + [ANY_SPEC] * count,
        out_specs=row_block(D),
        out_shape=jax.ShapeDtypeStruct((rows, D), F32),
        scratch_shapes=[pltpu.VMEM((D, QW + 2 * KW), BF16), pltpu.SemaphoreType.DMA],
        compiler_params=pltpu.CompilerParams(vmem_limit_bytes=60 << 20),
        cost_estimate=pl.CostEstimate(flops=2 * rows * D * 2048, bytes_accessed=10 << 20, transcendentals=0),
        name="input_back",
    )(in_hbm(grad), low_grad, down, hidden, gain[None, :], in_hbm(middle_grad), *[in_hbm(block) for block in pieces.blocks])


VMEM_SPEC = pl.BlockSpec(memory_space=pltpu.VMEM)
SMEM_SPEC = pl.BlockSpec(memory_space=pltpu.SMEM)


def lane_pad(width):
    return -(-width // 128) * 128


def layout_of(shapes):
    places = []
    offset = 0
    for index, (rows, width) in enumerate(shapes):
        for part in range(rows // RANK):
            places.append((index, part, offset, width))
            offset += width
    return places, lane_pad(offset)


def pack_adapters(adapter_ids, members, devices):
    places, width = layout_of([member.shape[1:] for member in members])
    per_seq = devices // NSEQ
    turned = [member.shape[1] % (2 * RANK) != 0 and member.shape[1] > RANK for member in members]
    members = [jnp.swapaxes(member, 1, 2) if turn else member for member, turn in zip(members, turned)]

    def kernel(ids, *refs):
        sources, out, slab = refs[: len(members)], refs[len(members)], refs[len(members) + 1]
        slab[...] = jnp.zeros_like(slab)
        for index, part, offset, size in places:
            picked = ids[pl.program_id(0)]
            rank_rows = slice(RANK * part, RANK * (part + 1))
            if turned[index]:
                piece = sources[index][picked, :, rank_rows].astype(F32).T.astype(BF16)
            else:
                piece = sources[index][picked, rank_rows, :]
            slab[:, offset : offset + size] = piece
        for step in range(per_seq):
            out[step] = slab[...]

    return pl.pallas_call(
        kernel,
        grid=(NSEQ,),
        in_specs=[SMEM_SPEC] + [pl.BlockSpec(member.shape, lambda s: (0, 0, 0)) for member in members],
        out_specs=pl.BlockSpec((per_seq, RANK, width), lambda s: (s, 0, 0)),
        out_shape=jax.ShapeDtypeStruct((devices, RANK, width), BF16),
        scratch_shapes=[pltpu.VMEM((RANK, width), BF16)],
        name="pack_adapters",
    )(adapter_ids, *members)


def unpack_adapters(slabs, shapes):
    devices = slabs.shape[0]
    places, _ = layout_of(shapes)

    def kernel(source, *outs):
        for index, part, offset, size in places:
            for device in range(devices):
                outs[index][RANK * part : RANK * (part + 1), device * size : (device + 1) * size] = source[
                    device, :, offset : offset + size
                ]

    return pl.pallas_call(
        kernel,
        in_specs=[VMEM_SPEC],
        out_specs=[VMEM_SPEC] * len(shapes),
        out_shape=[jax.ShapeDtypeStruct((rows, width * devices), BF16) for rows, width in shapes],
        name="unpack_adapters",
    )(slabs)


def pack_grads(grads, devices):
    places, width = layout_of([(grad.shape[0], grad.shape[1] // devices) for grad in grads])

    def kernel(*refs):
        sources, out = refs[: len(grads)], refs[len(grads)]
        for device in range(devices):
            for index, part, offset, size in places:
                out[device, :, offset : offset + size] = sources[index][
                    RANK * part : RANK * (part + 1), device * size : (device + 1) * size
                ].astype(BF16)

    return pl.pallas_call(
        kernel,
        in_specs=[VMEM_SPEC] * len(grads),
        out_specs=VMEM_SPEC,
        out_shape=jax.ShapeDtypeStruct((devices, RANK, width), BF16),
        name="pack_grads",
    )(*grads)


def reduce_grads(adapter_ids, slabs, shapes):
    devices, _, width = slabs.shape
    places, _ = layout_of(shapes)
    per_seq = devices // NSEQ
    turned = [rows % (2 * RANK) != 0 and rows > RANK for rows, _ in shapes]

    def kernel(ids, source, *refs):
        outs, total = refs[: len(shapes)], refs[len(shapes)]
        total[...] = jnp.zeros_like(total)
        for seq in range(NSEQ):
            part_sum = jnp.sum(source[seq * per_seq : (seq + 1) * per_seq].astype(F32), axis=0)
            total[ids[seq]] += part_sum
        for index, part, offset, size in places:
            rank_rows = slice(RANK * part, RANK * (part + 1))
            if turned[index]:
                for adapter in range(ADAPTERS):
                    outs[index][adapter, :, rank_rows] = total[adapter, :, offset : offset + size].T
            else:
                outs[index][:, rank_rows, :] = total[:, :, offset : offset + size]

    sums = pl.pallas_call(
        kernel,
        in_specs=[SMEM_SPEC, VMEM_SPEC],
        out_specs=[VMEM_SPEC] * len(shapes),
        out_shape=[
            jax.ShapeDtypeStruct((ADAPTERS, *((size, rows) if turn else (rows, size))), F32)
            for (rows, size), turn in zip(shapes, turned)
        ],
        scratch_shapes=[pltpu.VMEM((ADAPTERS, RANK, width), F32)],
        name="reduce_grads",
    )(adapter_ids, slabs)
    return [jnp.swapaxes(value, 1, 2) if turn else value for value, turn in zip(sums, turned)]


def split_three(value):
    first = value.astype(BF16)
    rest = value - first.astype(F32)
    second = rest.astype(BF16)
    third = (rest - second.astype(F32)).astype(BF16)
    return first, second, third


def with_columns(block, columns, lanes):
    out = jnp.where(lanes < HEAD_DIM, block, jnp.zeros_like(block))
    for step, column in enumerate(columns):
        out = jnp.where(lanes == HEAD_DIM + step, column, out)
    return out


def stacked_heads(pair):
    return jnp.concatenate([pair, pltpu.roll(pair, HEAD_DIM, 1)], axis=0)


def allowed(start_row, key_base, query_base):
    keys = lax.broadcasted_iota(jnp.int32, (BLOCK, BLOCK), 0)
    last = query_base - key_base + lax.broadcasted_iota(jnp.int32, (1, BLOCK), 1)
    inside = (keys >= start_row - key_base) & (keys <= last)
    return jnp.concatenate([inside, inside], axis=1)


def forward_attention(bounds, starts, queries, keyvals, column):
    rows = queries.shape[0]
    length = keyvals.shape[0]
    halo = length - rows
    steps = rows // BLOCK

    def kernel(bound_ref, start_ref, *refs):
        arrays, (out_ref, log_ref, key_scr, value_scr) = refs[:-4], refs[-4:]
        query_ref, keyval_ref = arrays[0], arrays[-1].at[:, column * PAIR : (column + 1) * PAIR]
        lanes = lax.broadcasted_iota(jnp.int32, (length, 128), 1)
        both = keyval_ref[...].astype(F32)
        key_scr[...] = jnp.where(lanes < HEAD_DIM, both, 0.0).astype(BF16)
        values = jnp.where(lanes < HEAD_DIM, pltpu.roll(both, HEAD_DIM, 1), 1.0)
        value_scr[...] = values.T.astype(BF16)

        def one_step(step, carry):
            own = pl.ds(pl.multiple_of(step * BLOCK, BLOCK), BLOCK)
            query = stacked_heads(query_ref[own, :PAIR].astype(F32)).astype(BF16)
            start_row = start_ref[:, own]
            diagonal = halo // BLOCK + step
            count = diagonal - bound_ref[0, step] + 1

            def block(index):
                base = pl.multiple_of(jnp.maximum(index, 0) * BLOCK, BLOCK)
                scores = contract_cols(key_scr[pl.ds(base, BLOCK), :], query)
                keep = allowed(start_row, index * BLOCK, diagonal * BLOCK)
                weights = jnp.where(keep, jnp.exp2(scores), 0.0).astype(BF16)
                return matmul(value_scr[:, pl.ds(base, BLOCK)], weights)

            def pair_of_blocks(turn, total):
                index = diagonal - 2 * turn
                return total + (block(index) + block(index - 1))

            total = lax.fori_loop(0, (count + 1) // 2, pair_of_blocks, jnp.zeros((128, 2 * BLOCK), F32))
            norm = total[HEAD_DIM : HEAD_DIM + 1, :]
            mixed = total[:HEAD_DIM, :] / norm
            out_ref[own, :] = jnp.concatenate([mixed[:, :BLOCK], mixed[:, BLOCK:]], axis=0).T.astype(BF16)
            log_ref[step] = jnp.broadcast_to(jnp.log2(norm), (8, 2 * BLOCK))
            return carry

        lax.fori_loop(0, steps, one_step, 0)

    arrays = [queries, keyvals] if halo else [queries]
    return pl.pallas_call(
        kernel,
        in_specs=[SMEM_SPEC] + [VMEM_SPEC] * (1 + len(arrays)),
        out_specs=[VMEM_SPEC] * 2,
        out_shape=[
            jax.ShapeDtypeStruct((rows, 128), BF16),
            jax.ShapeDtypeStruct((steps, 8, 2 * BLOCK), F32),
        ],
        scratch_shapes=[pltpu.VMEM((length, 128), BF16), pltpu.VMEM((128, length), BF16)],
        compiler_params=pltpu.CompilerParams(vmem_limit_bytes=40 << 20),
        cost_estimate=pl.CostEstimate(
            flops=4 * rows * 1024 * 256 * 2, bytes_accessed=4 * rows * 256, transcendentals=rows * 2048
        ),
        name="forward_attention",
    )(bounds, starts, *arrays)


TURNS = (SEGMAX // BLOCK + 2) // 2


def probabilities(bounds, starts, queries, keyvals, column, logs):
    rows = queries.shape[0]
    length = keyvals.shape[0]
    halo = length - rows
    steps = rows // BLOCK

    def kernel(bound_ref, start_ref, log_ref, *refs):
        arrays, (out_ref, key_scr, buffer, sems) = refs[:-4], refs[-4:]
        query_ref, keyval_ref = arrays[0], arrays[-1].at[:, column * PAIR : (column + 1) * PAIR]
        whole = lax.broadcasted_iota(jnp.int32, (length, 128), 1)
        ones = jnp.where(whole < HEAD_DIM + 3, 1.0, 0.0)
        key_scr[...] = jnp.where(whole < HEAD_DIM, keyval_ref[...].astype(F32), ones).astype(BF16)

        def turns(step):
            return (halo // BLOCK + step - bound_ref[0, step] + 2) // 2

        def stored(slot, step, turn):
            blocks = pl.ds(2 * turn, 2)
            return pltpu.make_async_copy(buffer.at[slot, blocks], out_ref.at[step, blocks], sems.at[slot])

        def finish(step):
            def wait(turn, carry):
                stored(lax.rem(step, 2), step, turn).wait()
                return carry

            lax.fori_loop(0, turns(step), wait, 0)

        def one_step(step, carry):
            @pl.when(step >= 2)
            def _():
                finish(step - 2)

            slot = lax.rem(step, 2)
            own = pl.ds(pl.multiple_of(step * BLOCK, BLOCK), BLOCK)
            lanes = lax.broadcasted_iota(jnp.int32, (2 * BLOCK, 128), 1)
            query = stacked_heads(query_ref[own, :PAIR].astype(F32))
            log_column = log_ref[step].T[:, :1]
            query_low = with_columns(query, [part.astype(F32) for part in split_three(-log_column)], lanes).astype(BF16)
            start_row = start_ref[:, own]
            diagonal = halo // BLOCK + step

            def block(index):
                where = pl.ds(pl.multiple_of(jnp.maximum(index, 0) * BLOCK, BLOCK), BLOCK)
                weights = jnp.exp2(contract_cols(key_scr[where, :], query_low))
                keep = allowed(start_row, index * BLOCK, diagonal * BLOCK)
                return jnp.where(keep, weights, 0.0).astype(BF16)

            def pair_of_blocks(turn, carry):
                index = diagonal - 2 * turn
                found = [block(index), block(index - 1)]
                buffer[slot, 2 * turn] = found[0]
                buffer[slot, 2 * turn + 1] = found[1]
                stored(slot, step, turn).start()
                return carry

            lax.fori_loop(0, turns(step), pair_of_blocks, 0)
            return carry

        lax.fori_loop(0, steps, one_step, 0)
        finish(steps - 2)
        finish(steps - 1)

    arrays = [queries, keyvals] if halo else [queries]
    return pl.pallas_call(
        kernel,
        in_specs=[SMEM_SPEC] + [VMEM_SPEC] * (2 + len(arrays)),
        out_specs=ANY_SPEC,
        out_shape=jax.ShapeDtypeStruct((steps, 2 * TURNS, BLOCK, 2 * BLOCK), BF16),
        scratch_shapes=[
            pltpu.VMEM((length, 128), BF16),
            pltpu.VMEM((2, 2 * TURNS, BLOCK, 2 * BLOCK), BF16),
            pltpu.SemaphoreType.DMA((2,)),
        ],
        compiler_params=pltpu.CompilerParams(vmem_limit_bytes=40 << 20),
        cost_estimate=pl.CostEstimate(
            flops=4 * rows * 1024 * 256, bytes_accessed=20 << 20, transcendentals=rows * 2048
        ),
        name="probabilities",
    )(bounds, starts, logs, *arrays)


def backward_attention(bounds, queries, keyvals, column, mixed, probs, grads):
    rows = queries.shape[0]
    length = keyvals.shape[0]
    halo = length - rows
    steps = rows // BLOCK

    def kernel(bound_ref, *refs):
        arrays, refs = refs[: 2 if halo else 1], refs[2 if halo else 1 :]
        mixed_ref, grad_ref, probs_ref = refs[:3]
        outs, (value_scr, turned_scr, key_sum, value_sum, buffer, sems) = refs[3:-6], refs[-6:]
        query_ref, keyval_ref = arrays[0], arrays[-1].at[:, column * PAIR : (column + 1) * PAIR]

        def turns(step):
            return (halo // BLOCK + step - bound_ref[0, step] + 2) // 2

        def loaded(step, turn):
            slot, blocks = lax.rem(step, 2), pl.ds(2 * turn, 2)
            return pltpu.make_async_copy(probs_ref.at[step, blocks], buffer.at[slot, blocks], sems.at[slot])

        def begin(step):
            def start(turn, carry):
                loaded(step, turn).start()
                return carry

            lax.fori_loop(0, turns(step), start, 0)

        begin(0)
        whole = lax.broadcasted_iota(jnp.int32, (length, 128), 1)
        both = keyval_ref[...].astype(F32)
        ones = jnp.where(whole < HEAD_DIM + 3, 1.0, 0.0)
        value_scr[...] = jnp.where(whole < HEAD_DIM, pltpu.roll(both, HEAD_DIM, 1), ones).astype(BF16)
        turned_scr[...] = both.T.astype(BF16)
        key_sum[...] = jnp.zeros_like(key_sum)
        value_sum[...] = jnp.zeros_like(value_sum)

        def one_step(step, carry):
            @pl.when(step + 1 < steps)
            def _():
                begin(step + 1)

            slot = lax.rem(step, 2)
            own = pl.ds(pl.multiple_of(step * BLOCK, BLOCK), BLOCK)
            lanes = lax.broadcasted_iota(jnp.int32, (2 * BLOCK, 128), 1)
            query_low = stacked_heads(query_ref[own, :PAIR].astype(F32)).astype(BF16)
            pair = grad_ref[own, :].astype(F32)
            grad = stacked_heads(pair)
            weighed = stacked_heads(pair * mixed_ref[own, :].astype(F32))
            inner = jnp.sum(jnp.where(lanes < HEAD_DIM, weighed, 0.0), axis=1, keepdims=True)
            grad_low = with_columns(grad, [part.astype(F32) for part in split_three(-inner)], lanes).astype(BF16)
            diagonal = halo // BLOCK + step

            def wait(turn, carry):
                loaded(step, turn).wait()
                return carry

            lax.fori_loop(0, turns(step), wait, 0)

            def block(index, weights):
                where = pl.ds(pl.multiple_of(jnp.maximum(index, 0) * BLOCK, BLOCK), BLOCK)
                slopes = (weights.astype(F32) * contract_cols(value_scr[where, :], grad_low)).astype(BF16)
                value_part = matmul(weights, grad_low)
                return where, value_part, matmul(slopes, query_low), matmul(turned_scr[:, where], slopes)

            def pair_of_blocks(turn, total):
                index = diagonal - 2 * turn
                parts = [block(index, buffer[slot, 2 * turn]), block(index - 1, buffer[slot, 2 * turn + 1])]
                for where, value_part, key_part, _ in parts:
                    value_sum[where, :] += value_part
                    key_sum[where, :] += key_part
                return total + (parts[0][3] + parts[1][3])

            total = lax.fori_loop(0, turns(step), pair_of_blocks, jnp.zeros((128, 2 * BLOCK), F32))
            total = total[:HEAD_DIM] * HEAD_DIM**-0.5
            outs[0][own, :PAIR] = jnp.concatenate([total[:, :BLOCK], total[:, BLOCK:]], axis=0).T.astype(BF16)
            return carry

        lax.fori_loop(0, steps, one_step, 0)
        keyval_grad = jnp.where(whole < HEAD_DIM, key_sum[...] * (1.0 / LOG2E), pltpu.roll(value_sum[...], HEAD_DIM, 1))
        if halo:
            outs[1][...] = keyval_grad
        else:
            outs[0][:, PAIR:] = keyval_grad.astype(BF16)

    arrays = [queries, keyvals] if halo else [queries]
    return pl.pallas_call(
        kernel,
        in_specs=[SMEM_SPEC] + [VMEM_SPEC] * (2 + len(arrays)) + [ANY_SPEC],
        out_specs=[VMEM_SPEC] * (2 if halo else 1),
        out_shape=[jax.ShapeDtypeStruct((rows, 128), BF16), jax.ShapeDtypeStruct((length, 128), F32)]
        if halo
        else [jax.ShapeDtypeStruct((rows, 2 * PAIR), BF16)],
        scratch_shapes=[
            pltpu.VMEM((length, 128), BF16),
            pltpu.VMEM((128, length), BF16),
            pltpu.VMEM((length, 128), F32),
            pltpu.VMEM((length, 128), F32),
            pltpu.VMEM((2, 2 * TURNS, BLOCK, 2 * BLOCK), BF16),
            pltpu.SemaphoreType.DMA((2,)),
        ],
        compiler_params=pltpu.CompilerParams(vmem_limit_bytes=40 << 20),
        cost_estimate=pl.CostEstimate(
            flops=8 * rows * 1024 * 256 * 2, bytes_accessed=20 << 20, transcendentals=0
        ),
        name="backward_attention",
    )(bounds, *arrays, mixed, grads, probs)


def document_bounds(segment_ids, origin, halo, span, seq_start):
    tokens = segment_ids.shape[0]
    names = jnp.arange(tokens // (SEGMAX // 2), dtype=jnp.int32)
    begin = jnp.sum((segment_ids[None, :] < names[:, None]).astype(jnp.int32), axis=1)
    own = lax.dynamic_slice_in_dim(segment_ids, origin, span, 0)
    start = jnp.sum(jnp.where(own[None, :] == names[:, None], begin[:, None], 0), axis=0)
    start = jnp.maximum(start, seq_start) - (origin - halo)
    first = start[::BLOCK] // BLOCK
    clear = -(-start[BLOCK - 1 :: BLOCK] // BLOCK)
    bounds = jnp.stack([first, jnp.maximum(clear, first)])
    return bounds, start[None, :]


TILE = 512


def silu_parts(gate):
    share = 1.0 / (1.0 + jnp.exp(-gate))
    return share, gate * share


def feed_forward(mixed, hidden, cotangent, gain, weights, chosen):
    members, rows, _ = mixed.shape
    tiles = FF // TILE
    packed = isinstance(weights, Pieces)
    arrays = weights.blocks if packed else weights
    count = len(arrays)
    slices = 2 * FF // D

    def kernel(*refs):
        (
            mixed_ref, hidden_ref, cot_ref, gain_ref,
            out_down_ref, out_up_ref, mlp_down_ref, mlp_up_ref, ffd_down_ref, ffd_up_ref,
        ) = refs[:10]
        weight_refs = refs[10 : 10 + count]
        (
            output_ref, middle_grad_ref, mixed_grad_ref,
            out_down_grad, out_up_grad, mlp_down_grad, mlp_up_grad, ffd_down_grad, ffd_up_grad,
            wide_scr, down_scr, mix_scr, middle_scr, normed_scr, branch_scr, slope_scr,
            low_scr, low_turned, back_scr, back_turned, out_low_scr, down_sum, gate_sum, up_sum, sems,
        ) = refs[10 + count :]
        out_columns = slice(2 * FF, 2 * FF + D)

        def column_piece(piece):
            return slice(piece * D, (piece + 1) * D)

        if packed:
            blocks = weights.copies(weight_refs)
            devices = len(blocks)
            part, down_part = D // devices, FF // devices

            def start_piece(piece):
                for ref, source, where, size in blocks:
                    row = pl.multiple_of(where // size * part, 8)
                    pltpu.make_async_copy(
                        ref.at[pl.ds(source + piece * part, part), :],
                        wide_scr.at[pl.ds(row, part), column_piece(piece)],
                        sems.at[piece],
                    ).start()

            def start_down():
                for ref, source, where, size in blocks:
                    row = pl.multiple_of(where // size * down_part, 8)
                    pltpu.make_async_copy(
                        ref.at[pl.ds(source + (slices + 1) * part, down_part), :],
                        down_scr.at[pl.ds(row, down_part), :],
                        sems.at[slices + 1],
                    ).start()
        else:

            def start_piece(piece):
                columns = column_piece(piece)
                pltpu.make_async_copy(
                    weight_refs[0].at[:, columns], wide_scr.at[:, columns], sems.at[piece]
                ).start()

            def start_down():
                pltpu.make_async_copy(weight_refs[1], down_scr, sems.at[slices + 1]).start()

        def finish_piece(piece):
            region = wide_scr.at[:, column_piece(piece)]
            pltpu.make_async_copy(region, region, sems.at[piece]).wait()

        per_piece = D // TILE
        first_use = {}
        for piece in range(slices):
            uses = [c // TILE % tiles for c in range(piece * D, (piece + 1) * D, TILE)]
            first_use.setdefault(min(uses), []).append(piece)
        start_piece(slices)
        for piece in first_use[0]:
            start_piece(piece)
        start_down()

        cot = cot_ref[...]
        for member in range(members):
            mix_scr[:, member * PAIR : (member + 1) * PAIR] = mixed_ref[member]
        out_low = contract_cols(mix_scr[...], out_down_ref[...]).astype(BF16)
        out_low_scr[...] = out_low
        back = contract_cols(cot, ffd_up_ref[...])
        back_scr[...] = back.astype(BF16)
        back_turned[...] = back.T.astype(BF16)
        branch_scr[...] = jnp.zeros_like(branch_scr)
        slope_scr[...] = jnp.zeros_like(slope_scr)
        down_sum[...] = jnp.zeros_like(down_sum)
        gate_sum[...] = jnp.zeros_like(gate_sum)
        up_sum[...] = jnp.zeros_like(up_sum)
        finish_piece(slices)
        middle = (
            hidden_ref[...].astype(F32)
            + matmul(mix_scr[...], wide_scr[:, out_columns])
            + matmul(out_low, out_up_ref[...])
        )
        middle_scr[...] = middle
        normed = (middle * row_scale(middle) * gain_ref[...]).astype(BF16)
        normed_scr[...] = normed
        low = contract_cols(normed, mlp_down_ref[...])
        low_scr[...] = low.astype(BF16)
        low_turned[...] = low.T.astype(BF16)
        pltpu.make_async_copy(down_scr, down_scr, sems.at[slices + 1]).wait()

        def tile(index, carry):
            base = pl.multiple_of(index * TILE, TILE)
            gate_at, up_at = pl.ds(base, TILE), pl.ds(base + FF, TILE)
            for use, group in sorted(first_use.items()):

                @pl.when(index == use)
                def _(group=group):
                    for piece in group:
                        finish_piece(piece)

                if use > 0:

                    @pl.when(index == max(use - per_piece, 0))
                    def _(group=group):
                        for piece in group:
                            start_piece(piece)

            normed = normed_scr[...]
            low = low_scr[...]
            gate = matmul(normed, wide_scr[:, gate_at]) + matmul(low[:, :RANK], mlp_up_ref[:, gate_at])
            up = matmul(normed, wide_scr[:, up_at]) + matmul(low[:, RANK:], mlp_up_ref[:, up_at])
            share, active = silu_parts(gate)
            units = (active * up).astype(BF16)
            down = down_scr[gate_at, :]
            branch_scr[...] += matmul(units, down)
            down_sum[...] += contract_cols(units, ffd_down_ref[:, gate_at])
            ffd_down_grad[:, gate_at] = matmul(back_turned[...], units)
            units_grad = contract_cols(cot_ref[...], down) + matmul(back_scr[...], ffd_down_ref[:, gate_at])
            gate_grad = (units_grad * up * (share * (1.0 + gate * (1.0 - share)))).astype(BF16)
            up_grad = (units_grad * active).astype(BF16)
            slope_scr[...] += contract_cols(gate_grad, wide_scr[:, gate_at]) + contract_cols(
                up_grad, wide_scr[:, up_at]
            )
            gate_sum[...] += contract_cols(gate_grad, mlp_up_ref[:, gate_at])
            up_sum[...] += contract_cols(up_grad, mlp_up_ref[:, up_at])
            mlp_up_grad[:, gate_at] = matmul(low_turned[:RANK, :], gate_grad)
            mlp_up_grad[:, up_at] = matmul(low_turned[RANK:, :], up_grad)
            return carry

        lax.fori_loop(0, tiles, tile, 0)

        middle = middle_scr[...]
        cot = cot_ref[...]
        down_low = down_sum[...].astype(BF16)
        output_ref[...] = (middle + branch_scr[...] + matmul(down_low, ffd_up_ref[...])).astype(BF16)
        ffd_up_grad[...] = contract_rows(down_low, cot)
        low_grad = jnp.concatenate([gate_sum[...], up_sum[...]], axis=1).astype(BF16)
        mlp_down_grad[...] = contract_rows(low_grad, normed_scr[...])
        slope = gain_ref[...] * (slope_scr[...] + matmul(low_grad, mlp_down_ref[...]))
        scale = row_scale(middle)
        inner = jnp.mean(slope * middle, axis=1, keepdims=True)
        middle_grad = cot.astype(F32) + scale * slope - middle * (scale * scale * scale * inner)
        middle_grad_ref[...] = middle_grad
        branch_grad = middle_grad.astype(BF16)
        out_up_grad[...] = contract_rows(out_low_scr[...], branch_grad)
        out_low_grad = contract_cols(branch_grad, out_up_ref[...]).astype(BF16)
        out_down_grad[...] = contract_rows(out_low_grad, mix_scr[...])
        mixed_grad = contract_cols(branch_grad, wide_scr[:, out_columns]) + matmul(out_low_grad, out_down_ref[...])
        for member in range(members):
            mixed_grad_ref[member] = mixed_grad[:, member * PAIR : (member + 1) * PAIR].astype(BF16)

    results = pl.pallas_call(
        kernel,
        in_specs=[VMEM_SPEC] * 10 + [ANY_SPEC] * count,
        out_specs=[VMEM_SPEC] * 9,
        out_shape=[
            jax.ShapeDtypeStruct((rows, D), BF16),
            jax.ShapeDtypeStruct((rows, D), F32),
            jax.ShapeDtypeStruct((members, rows, PAIR), BF16),
            jax.ShapeDtypeStruct((RANK, QW), F32),
            jax.ShapeDtypeStruct((RANK, D), F32),
            jax.ShapeDtypeStruct((2 * RANK, D), F32),
            jax.ShapeDtypeStruct((RANK, 2 * FF), F32),
            jax.ShapeDtypeStruct((RANK, FF), F32),
            jax.ShapeDtypeStruct((RANK, D), F32),
        ],
        scratch_shapes=[
            pltpu.VMEM((D, 2 * FF + D), BF16), pltpu.VMEM((FF, D), BF16),
            pltpu.VMEM((rows, QW), BF16), pltpu.VMEM((rows, D), F32), pltpu.VMEM((rows, D), BF16),
            pltpu.VMEM((rows, D), F32), pltpu.VMEM((rows, D), F32),
            pltpu.VMEM((rows, 2 * RANK), BF16), pltpu.VMEM((2 * RANK, rows), BF16),
            pltpu.VMEM((rows, RANK), BF16), pltpu.VMEM((RANK, rows), BF16), pltpu.VMEM((rows, RANK), BF16),
            pltpu.VMEM((rows, RANK), F32), pltpu.VMEM((rows, RANK), F32), pltpu.VMEM((rows, RANK), F32),
            pltpu.SemaphoreType.DMA((2 + slices,)),
        ],
        compiler_params=pltpu.CompilerParams(vmem_limit_bytes=60 << 20),
        cost_estimate=pl.CostEstimate(
            flops=rows * (12 * D * FF + 4 * D * QW), bytes_accessed=6 * D * FF + 16 * rows * D,
            transcendentals=rows * FF,
        ),
        name="feed_forward",
    )(mixed, hidden, cotangent, gain[None, :], *chosen, *arrays)
    return results[0], results[1], results[2], list(results[3:])


def local(
    hidden, cotangent, segment_ids, adapter_ids, attn_gain, query_gain, key_gain, ffn_gain,
    qkv_weight, out_weight, gate_up_weight, down_weight, *adapters,
):
    rows = hidden.shape[0]
    devices = lax.axis_size("ctx") * lax.axis_size("head")
    members = KV_HEADS
    groups = [[members * g + i for i in range(members)] for g in range(devices // members)]
    span = rows * members
    seq_length = rows * devices // NSEQ
    halo = 0 if span == seq_length else SEGMAX
    here = lax.axis_index("ctx") * lax.axis_size("head") + lax.axis_index("head")
    origin = here // members * span
    seq_start = origin // seq_length * seq_length
    positions = here * rows - seq_start + jnp.arange(rows, dtype=jnp.int32)
    bounds, starts = document_bounds(segment_ids, origin, halo, span, seq_start)

    def swap(value):
        return lax.all_to_all(value, AXES, 0, 0, axis_index_groups=groups, tiled=True)

    def shifted(value, by):
        pairs = [(i, i + by) for i in range(devices) if 0 <= i + by < devices]
        return lax.ppermute(value, AXES, pairs)

    def gather(value):
        return lax.all_gather(value, AXES, axis=0, tiled=True)

    shapes = [member.shape[1:] for member in adapters]
    def exchange(packed):
        return lax.all_to_all(packed, AXES, 0, 0, tiled=True)

    spread = by_axes()
    if spread:
        found = {(0, 0): stack_shard(gate_up_weight, out_weight, down_weight)}
        pending = []

        def move(*keys, extra=()):
            hops = [(found[key[0] ^ key[2], key[1] - key[3]], key[2], key[3]) for key in keys]
            hops += extra
            held = lax.optimization_barrier((*[value for value, _, _ in hops], *pending))
            results = [hop(value, flip, step) for value, (_, flip, step) in zip(held, hops)]
            found.update(zip([key[:2] for key in keys], results))
            pending[:] = results
            return results[len(keys) :]

        def cores(*keys):
            return [(flip, step, 1, 0) for flip, step in keys]

        def then(value):
            return lax.optimization_barrier((value, *pending))[0]

        line = move((2, 0, 2, 0), (4, 0, 4, 0), extra=[(qkv_weight, 0, step) for step in range(1, 4)])
        slabs = exchange(lax.optimization_barrier((pack_adapters(adapter_ids, adapters[:2], devices), *line))[0])
        line = jnp.concatenate([qkv_weight] + line, axis=0)
        plane = move((0, 1, 0, 1), extra=[(line, flip, 0) for flip in (2, 4, 6)])
        pending.append(slabs)
        plane = jnp.concatenate([line] + plane, axis=0)
        (across,) = move((0, 2, 0, 1), (2, 1, 2, 0), (6, 0, 4, 0), extra=[(plane, 1, 0)])
        qkv = Pieces([((0, (0, 1, 2, 3)), plane), ((1, (0, 1, 2, 3)), across)], D)
        hidden_then = hidden
    else:
        qkv = whole_gather(qkv_weight)
        weights = [gather(jnp.concatenate([gate_up_weight, out_weight], axis=1)), gather(down_weight)]
        hidden_then = hidden
        slabs = exchange(pack_adapters(adapter_ids, adapters[:2], devices))
    chosen = list(unpack_adapters(slabs, shapes[:2]))

    head_gain = jnp.stack([jnp.tile(query_gain, 2), jnp.tile(key_gain, 2)])
    tables = rope_tables(positions)
    sent, low_qkv, kept = project_heads(hidden_then, attn_gain, head_gain, tables, qkv, chosen[0], chosen[1])
    if spread:
        sent = then(sent)
    queries = swap(sent).reshape(span, 2 * PAIR)
    keyvals, column = queries, 1
    if halo:
        keyvals, column = queries[:, PAIR:], 0
        keyvals = jnp.concatenate([shifted(keyvals[span - halo :], members), keyvals], axis=0)
    if spread:
        move((2, 2, 2, 0), (4, 1, 4, 0), *cores((1, 0)))
        first = pending[:]
        move((0, 3, 0, 1))
        pending[:] = first
        late_adapters = then(adapters[2])
        move((6, 1, 2, 0), (4, 2, 4, 0), *cores((1, 1), (3, 0)))
        keyvals = queries = then(queries)
        move((2, 3, 2, 0), (4, 3, 4, 0), *cores((5, 0), (7, 0), (1, 2)))
    else:
        late_adapters = adapters[2]
    packed = pack_adapters(adapter_ids, (late_adapters, *adapters[3:]), devices)
    slabs = exchange(lax.optimization_barrier((packed, queries))[0])
    mixed, logs = forward_attention(bounds, starts, queries, keyvals, column)
    chosen += list(unpack_adapters(slabs, shapes[2:]))
    if spread:
        pending += [logs, chosen[-1]]
        move((6, 3, 2, 0), (6, 2, 4, 0), *cores((3, 3), (5, 3), (3, 1)))
    mixed_then = lax.optimization_barrier((mixed, slabs))[0]
    mixture_tok = swap(mixed_then.reshape(members, rows, PAIR))
    if spread:
        ended, pending[:] = pending[:2], pending[2:]
        move(*cores((5, 1), (3, 2), (5, 2), (7, 1), (1, 3)))
        pending += [mixture_tok, *ended]
        move(*cores((7, 2), (7, 3)))
        weights = Pieces([((flip, (step,)), block) for (flip, step), block in found.items()], D)
    output, middle_grad, mixture_grad, early = feed_forward(
        mixture_tok, hidden, cotangent, ffn_gain, weights, chosen[2:]
    )
    grad_rows = swap(mixture_grad).reshape(span, PAIR)
    logs_then = lax.optimization_barrier((logs, mixture_grad))[0]
    probs = probabilities(bounds, starts, queries, keyvals, column, logs_then)
    early_packed, grad_rows = lax.optimization_barrier((pack_grads(early, devices), grad_rows))
    early_slabs = exchange(early_packed)
    back = backward_attention(bounds, queries, keyvals, column, mixed, probs, grad_rows)
    if halo:
        query_grads, keyval_grads = back
        returned = shifted(keyval_grads[:halo].astype(BF16), -members).astype(F32)
        keyval_grads = jnp.concatenate([keyval_grads[halo:span], keyval_grads[span:] + returned], axis=0)
        back = [jnp.concatenate([query_grads, keyval_grads.astype(BF16)], axis=1)]
    back, early_slabs = lax.optimization_barrier((back[0], early_slabs))
    early_owned = reduce_grads(adapter_ids, early_slabs, shapes[2:])
    back = back.reshape(members, rows, 2 * PAIR)
    arrived_back = swap(back)
    projected_grad, low_grad, packed = project_back(
        arrived_back, kept, head_gain, tables, hidden, attn_gain, low_qkv, chosen[1], devices
    )
    late_slabs = exchange(packed)
    late_owned = reduce_grads(adapter_ids, late_slabs, shapes[:2])
    input_grad = input_back(projected_grad, low_grad, qkv, chosen[0], hidden, attn_gain, middle_grad)
    return (output, input_grad, *late_owned, *early_owned)


def solution(mesh):
    by_rows = P(AXES, None)
    by_cols = P(None, None, AXES)
    placed = (by_rows, by_rows) + (P(),) * 6 + (by_rows,) * 4 + (by_cols,) * 8
    return jax.shard_map(
        local,
        mesh=mesh,
        in_specs=placed,
        out_specs=(by_rows, by_rows) + (by_cols,) * 8,
        check_vma=False,
    )
```
